32 devices in a mesh: grp: 8 (over y, x, core), shard: 4 (over z).
Axes of the slice: x: 2, y: 2, z: 4, core: 2. Of those that a mesh axis runs over, the one named last changes fastest.
Arguments:
- tokens: bfloat16 [16, 1024, 768], P('grp', 'shard'), may hold values from -6 to 6
- cotangent: bfloat16 [16, 1024, 768], P('grp', 'shard'), may hold values from -6 to 6
- lengths: int32 [16], P('grp'), may hold values from 256 to 1024, as said below
- w_qkv: bfloat16 [768, 2304], P('shard'), may hold values from -0.21875 to 0.21875
- bias_q: bfloat16 [768], P('shard'), may hold values from -3 to 3
- bias_v: bfloat16 [768], P('shard'), may hold values from -3 to 3
- w_out: bfloat16 [768, 768], P('shard'), may hold values from -1.75 to 1.75
- bias_out: bfloat16 [768], P('shard'), may hold values from -3 to 3
- gain_attn: bfloat16 [768], P('shard'), may hold values from 0.25 to 1.75
- shift_attn: bfloat16 [768], P('shard'), may hold values from -3 to 3
- w_up: bfloat16 [768, 3072], P('shard'), may hold values from -0.21875 to 0.21875
- bias_up: bfloat16 [3072], P('shard'), may hold values from -3 to 3
- w_down: bfloat16 [3072, 768], P('shard'), may hold values from -0.109375 to 0.109375
- bias_down: bfloat16 [768], P('shard'), may hold values from -3 to 3
- gain_ffn: bfloat16 [768], P('shard'), may hold values from 0.25 to 1.75
- shift_ffn: bfloat16 [768], P('shard'), may hold values from -3 to 3
Outputs:
- layer_out: bfloat16 [16, 1024, 768], P('grp', 'shard')
- grad_tokens: bfloat16 [16, 1024, 768], P('grp', 'shard')
- grad_w_qkv: float32 [768, 2304], P('shard')
- grad_bias_q: float32 [768], P('shard')
- grad_bias_v: float32 [768], P('shard')
- grad_w_out: float32 [768, 768], P('shard')
- grad_bias_out: float32 [768], P('shard')
- grad_gain_attn: float32 [768], P('shard')
- grad_shift_attn: float32 [768], P('shard')
- grad_w_up: float32 [768, 3072], P('shard')
- grad_bias_up: float32 [3072], P('shard')
- grad_w_down: float32 [3072, 768], P('shard')
- grad_bias_down: float32 [768], P('shard')
- grad_gain_ffn: float32 [768], P('shard')
- grad_shift_ffn: float32 [768], P('shard')
The draws below stay inside these ranges and needn't reach their ends.
Inputs may be any that keep to these rules, and one draw needn't show every extreme that they name: `lengths`: valid slots of a sequence come first; some sequence fills all 1024 slots.
All inputs are finite; a program needn't handle non-finite values.
Results may differ from the reference program's by a relative error of at most 0.03.
Values may be sent and summed in bfloat16 or wider, within the bound.
No kernel may reach another device: no remote copies, remote signals or barrier semaphores. Data moves between devices by JAX's collectives and lax.ppermute only.
A program may use at most 256 MiB of HBM per device.

```python
import jax
import jax.numpy as jnp
from jax import lax

D = 768
H = 12
HD = 64
FF = 3072
SLOTS = 1024
SEQS = 16


def draw_lengths(key, part):
    drawn_len = jax.random.randint(jax.random.fold_in(key, 11), (SEQS,), SLOTS // 4, SLOTS + 1, dtype=jnp.int32)
    chosen = jax.random.randint(jax.random.fold_in(key, 12), (), 0, SEQS, dtype=jnp.int32)
    return jnp.where(jnp.arange(SEQS, dtype=jnp.int32) == chosen, SLOTS, drawn_len).astype(jnp.int32)


def level_of(stream_key, extent, shards, low, top_value):
    def one(axis_at, parts):
        steps = jax.random.uniform(jax.random.fold_in(jax.random.fold_in(stream_key, 6), axis_at), (parts,), jnp.float32, low / len(shards), top_value / len(shards))
        return jnp.repeat(jnp.exp(steps), extent[axis_at] // parts).reshape((-1,) + (1,) * (len(extent) - axis_at - 1))

    factor_of = one(*shards[0])
    for cut in shards[1:]:
        factor_of = factor_of * one(*cut)
    return factor_of


def gaussian(stream_key, shape, scale, bound, shards=(), kind=jnp.bfloat16):
    drawn = scale * jax.random.normal(stream_key, shape, jnp.float32)
    if shards:
        drawn = drawn * level_of(stream_key, shape, shards, -0.22, 0.18)
    return jnp.clip(drawn, -bound, bound).astype(kind)


def setup_inputs(seed: int = 0) -> dict:
    streams_of = jax.random.split(jax.random.key(seed), 17)
    return {
        "tokens": gaussian(streams_of[0], (SEQS, SLOTS, D), 1.0, 6.0, ((0, 8), (1, 4))),
        "cotangent": gaussian(streams_of[1], (SEQS, SLOTS, D), 1.0, 6.0, ((0, 8), (1, 4))),
        "lengths": draw_lengths(jax.random.fold_in(streams_of[16], 71), 0),
        "w_qkv": gaussian(streams_of[3], (D, 3 * D), D ** -0.5, 0.21875, ((0, 4),)),
        "bias_q": gaussian(streams_of[4], (D,), 0.5, 3.0, ((0, 4),)),
        "bias_v": gaussian(streams_of[5], (D,), 0.5, 3.0, ((0, 4),)),
        "w_out": gaussian(streams_of[6], (D, D), (max(1, D * 16 // SLOTS)) ** -0.5, 1.75, ((0, 4),)),
        "bias_out": gaussian(streams_of[7], (D,), 0.5, 3.0, ((0, 4),)),
        "gain_attn": jnp.clip(1.0 + 0.15 * jax.random.normal(streams_of[8], (D,), jnp.float32), 0.25, 1.75).astype(jnp.bfloat16),
        "shift_attn": gaussian(streams_of[9], (D,), 0.5, 3.0, ((0, 4),)),
        "w_up": gaussian(streams_of[10], (D, FF), D ** -0.5, 0.21875, ((0, 4),)),
        "bias_up": gaussian(streams_of[11], (FF,), 0.5, 3.0, ((0, 4),)),
        "w_down": gaussian(streams_of[12], (FF, D), FF ** -0.5, 0.109375, ((0, 4),)),
        "bias_down": gaussian(streams_of[13], (D,), 0.5, 3.0, ((0, 4),)),
        "gain_ffn": jnp.clip(1.0 + 0.15 * jax.random.normal(streams_of[14], (D,), jnp.float32), 0.25, 1.75).astype(jnp.bfloat16),
        "shift_ffn": gaussian(streams_of[15], (D,), 0.5, 3.0, ((0, 4),)),
    }


@jax.custom_vjp
def low(v):
    return lax.optimization_barrier(v.astype(jnp.bfloat16)).astype(jnp.float32)

@jax.custom_vjp
def low_back(v):
    return v

def low_keep(v):
    return (low(v), None)

def low_pass(kept, grad):
    return (grad,)

def back_keep(v):
    return (v, None)

def back_low(kept, grad):
    return (low(grad),)
low.defvjp(low_keep, low_pass)
low_back.defvjp(back_keep, back_low)
eps = 1e-12
masked_score = -1000000000.0

def matmul(left_mat, right_mat):
    return jnp.dot(left_mat, right_mat, precision=lax.Precision.HIGHEST)

def layer_norm(values_in, gain_vec, shift_vec):
    row_mean = lax.optimization_barrier(jnp.mean(values_in, axis=-1, keepdims=True))
    centered = values_in - row_mean
    variance = lax.optimization_barrier(jnp.mean(centered * centered, axis=-1, keepdims=True))
    return centered * lax.rsqrt(variance + eps) * gain_vec + shift_vec

def attend(queries, keys, values, key_mask):
    slot_count = queries.shape[0]

    def split_heads(tensor):
        return jnp.transpose(tensor.reshape(slot_count, H, HD), (1, 0, 2))

    def one_head(operands):
        q_head, k_head, v_head = operands
        scores = matmul(q_head, k_head.T) * HD ** (-0.5)
        scores = low_back(jnp.where(key_mask[None, :], scores, masked_score))
        probs = jax.nn.softmax(scores, axis=-1)
        return matmul(low(probs), v_head)
    result = lax.map(jax.checkpoint(one_head), (split_heads(queries), split_heads(keys), split_heads(values)))
    return jnp.transpose(result, (1, 0, 2)).reshape(slot_count, H * HD)

def forward(seq_in, params, row_mask, key_mask):
    w_qkv, bias_q, bias_v, w_out, bias_out, gain_attn, shift_attn, w_up, bias_up, w_down, bias_down, gain_ffn, shift_ffn = params
    width = seq_in.shape[1]
    qkv_bias = jnp.concatenate([bias_q, jnp.zeros_like(bias_q), bias_v])
    qkv_all = low(low_back(matmul(seq_in, w_qkv) + qkv_bias))
    context = attend(qkv_all[:, :width], qkv_all[:, width:2 * width], qkv_all[:, 2 * width:], key_mask)
    context = low(low_back(context))
    attn_out = low_back(matmul(context, w_out) + bias_out)
    hidden = layer_norm(seq_in + attn_out, gain_attn, shift_attn)
    up_proj = low_back(matmul(low(hidden), w_up) + bias_up)
    activation = low(jax.nn.gelu(up_proj, approximate=False))
    ffn_out = low_back(matmul(activation, w_down) + bias_down)
    result = layer_norm(hidden + ffn_out, gain_ffn, shift_ffn)
    return result * row_mask[:, None]

def reference(tokens, cotangent, lengths, w_qkv, bias_q, bias_v, w_out, bias_out, gain_attn, shift_attn, w_up, bias_up, w_down, bias_down, gain_ffn, shift_ffn):
    params = tuple((p.astype(jnp.float32) for p in (w_qkv, bias_q, bias_v, w_out, bias_out, gain_attn, shift_attn, w_up, bias_up, w_down, bias_down, gain_ffn, shift_ffn)))
    positions = jnp.arange(SLOTS, dtype=jnp.int32)

    def one_sequence(totals, inputs):
        seq_in, cot_seq, length = inputs
        key_mask = positions < length.astype(jnp.int32)
        row_mask = key_mask.astype(jnp.float32)
        result, pullback = jax.vjp(lambda xin, pin: forward(xin, pin, row_mask, key_mask), seq_in.astype(jnp.float32), params)
        grad_x, grad_params = pullback(cot_seq.astype(jnp.float32))
        totals = jax.tree.map(lambda left_sum, right_sum: left_sum + right_sum, totals, grad_params)
        return (totals, (result.astype(jnp.bfloat16), grad_x.astype(jnp.bfloat16)))
    zero_grads = tuple((jnp.zeros_like(p) for p in params))
    totals, (outputs, grad_xs) = lax.scan(one_sequence, zero_grads, (tokens, cotangent, lengths))
    return (outputs, grad_xs, totals[0], totals[1], totals[2], totals[3], totals[4], totals[5], totals[6], totals[7], totals[8], totals[9], totals[10], totals[11], totals[12])
```

```python
import functools
import math

import jax
import jax.numpy as jnp
from jax import lax
from jax.experimental import pallas as pl
from jax.experimental.pallas import tpu as pltpu
from jax.sharding import PartitionSpec as P


H = 12
HD = 64


eps = 1e-12
masked_score = -1000000000.0


def layer_norm(values_in, gain_vec, shift_vec):
    row_mean = jnp.mean(values_in, axis=-1, keepdims=True)
    centered = values_in - row_mean
    variance = jnp.mean(centered * centered, axis=-1, keepdims=True)
    return centered * lax.rsqrt(variance + eps) * gain_vec + shift_vec


def gelu_exact(values_in):
    return jax.nn.gelu(values_in, approximate=False)


def contract_cols(left_mat, right_mat):
    return lax.dot_general(
        left_mat, right_mat, (((1,), (1,)), ((), ())), preferred_element_type=jnp.float32
    )


def contract_rows(left_mat, right_mat):
    return lax.dot_general(
        left_mat, right_mat, (((0,), (0,)), ((), ())), preferred_element_type=jnp.float32
    )


def column_sums(matrix):
    return jnp.sum(matrix.astype(jnp.float32), axis=0)


def unpack(weights_full):
    (
        qkv_weight,
        query_bias,
        value_bias,
        out_weight,
        out_bias,
        gain_one,
        shift_one,
        up_weight,
        up_bias,
        down_weight,
        down_bias,
        gain_two,
        shift_two,
    ) = weights_full
    as_float = lambda vector: vector.astype(jnp.float32)
    return (
        qkv_weight,
        as_float(query_bias),
        as_float(value_bias),
        out_weight,
        as_float(out_bias),
        as_float(gain_one),
        as_float(shift_one),
        up_weight,
        as_float(up_bias),
        down_weight,
        as_float(down_bias),
        as_float(gain_two),
        as_float(shift_two),
    )


def head_scores(queries, keys, key_mask, head_idx):
    col_start = head_idx * HD
    q_head = lax.dynamic_slice_in_dim(queries, col_start, HD, 1)
    k_head = lax.dynamic_slice_in_dim(keys, col_start, HD, 1)
    scores = contract_cols(q_head, k_head) * HD ** (-0.5)
    return (q_head, k_head, jnp.where(key_mask[None, :], scores, masked_score))


def attend_forward(queries, keys, values, key_mask):
    row_count, width = queries.shape

    def one_head(head_idx, carry):
        context, lse_rows = carry
        q_head, k_head, scores = head_scores(queries, keys, key_mask, head_idx)
        v_head = lax.dynamic_slice_in_dim(values, head_idx * HD, HD, 1)
        row_max = jnp.max(scores, axis=1, keepdims=True)
        exp_scores = jnp.exp(scores - row_max)
        row_total = jnp.sum(exp_scores, axis=1, keepdims=True)
        prob_low = (exp_scores / row_total).astype(jnp.bfloat16)
        head_out = jnp.dot(prob_low, v_head, preferred_element_type=jnp.float32)
        context = lax.dynamic_update_slice_in_dim(context, head_out, head_idx * HD, 1)
        lse_rows = lax.dynamic_update_slice_in_dim(
            lse_rows, row_max + jnp.log(row_total), head_idx, 1
        )
        return (context, lse_rows)

    start_state = (
        jnp.zeros((row_count, width), jnp.float32),
        jnp.zeros((row_count, H), jnp.float32),
    )
    return lax.fori_loop(0, H, one_head, start_state)


def attend_backward(queries, keys, values, key_mask, lse_rows, grad_context):
    row_count, width = queries.shape
    slot_count = keys.shape[0]

    def one_head(head_idx, carry):
        grad_q, grad_k, grad_v = carry
        col_start = head_idx * HD
        q_head, k_head, scores = head_scores(queries, keys, key_mask, head_idx)
        v_head = lax.dynamic_slice_in_dim(values, col_start, HD, 1)
        grad_head = lax.dynamic_slice_in_dim(grad_context, col_start, HD, 1)
        probs = jnp.exp(scores - lax.dynamic_slice_in_dim(lse_rows, head_idx, 1, 1))
        grad_probs = contract_cols(grad_head, v_head)
        delta = jnp.sum(probs * grad_probs, axis=1, keepdims=True)
        grad_scores = (probs * (grad_probs - delta)).astype(jnp.bfloat16)
        head_gq = jnp.dot(grad_scores, k_head, preferred_element_type=jnp.float32) * HD ** (-0.5)
        head_gk = contract_rows(grad_scores, q_head) * HD ** (-0.5)
        head_gv = contract_rows(probs.astype(jnp.bfloat16), grad_head)
        grad_q = lax.dynamic_update_slice_in_dim(grad_q, head_gq, col_start, 1)
        grad_k = lax.dynamic_update_slice_in_dim(grad_k, head_gk, col_start, 1)
        grad_v = lax.dynamic_update_slice_in_dim(grad_v, head_gv, col_start, 1)
        return (grad_q, grad_k, grad_v)

    start_state = (
        jnp.zeros((row_count, width), jnp.float32),
        jnp.zeros((slot_count, width), jnp.float32),
        jnp.zeros((slot_count, width), jnp.float32),
    )
    return lax.fori_loop(0, H, one_head, start_state)


def per_device(
    tokens,
    cotangent,
    lengths,
    w_qkv,
    bias_q,
    bias_v,
    w_out,
    bias_out,
    gain_attn,
    shift_attn,
    w_up,
    bias_up,
    w_down,
    bias_down,
    gain_ffn,
    shift_ffn,
):
    batch_count, row_count, width = tokens.shape
    dev_count = lax.axis_size("shard")
    slot_count = row_count * dev_count
    first_row = lax.axis_index("shard") * row_count
    key_place = jnp.arange(slot_count, dtype=jnp.int32)
    row_place = first_row + jnp.arange(row_count, dtype=jnp.int32)
    sharded = (
        w_qkv,
        bias_q,
        bias_v,
        w_out,
        bias_out,
        gain_attn,
        shift_attn,
        w_up,
        bias_up,
        w_down,
        bias_down,
        gain_ffn,
        shift_ffn,
    )
    totals = [
        jnp.zeros((piece.shape[0] * dev_count,) + piece.shape[1:], jnp.float32) for piece in sharded
    ]
    layer_rows = []
    grad_rows = []
    for batch_idx in range(batch_count):
        weights_full = unpack(
            (
                lax.all_gather(w_qkv, "shard", axis=0, tiled=True),
                lax.all_gather(bias_q, "shard", axis=0, tiled=True),
                lax.all_gather(bias_v, "shard", axis=0, tiled=True),
                lax.all_gather(w_out, "shard", axis=0, tiled=True),
                lax.all_gather(bias_out, "shard", axis=0, tiled=True),
                lax.all_gather(gain_attn, "shard", axis=0, tiled=True),
                lax.all_gather(shift_attn, "shard", axis=0, tiled=True),
                lax.all_gather(w_up, "shard", axis=0, tiled=True),
                lax.all_gather(bias_up, "shard", axis=0, tiled=True),
                lax.all_gather(w_down, "shard", axis=0, tiled=True),
                lax.all_gather(bias_down, "shard", axis=0, tiled=True),
                lax.all_gather(gain_ffn, "shard", axis=0, tiled=True),
                lax.all_gather(shift_ffn, "shard", axis=0, tiled=True),
            )
        )
        (
            qkv_weight,
            query_bias,
            value_bias,
            out_weight,
            out_bias,
            gain_one,
            shift_one,
            up_weight,
            up_bias,
            down_weight,
            down_bias,
            gain_two,
            shift_two,
        ) = weights_full
        seq_in = tokens[batch_idx]
        seq_len = lengths[batch_idx]
        key_mask = key_place < seq_len
        own_valid = row_place < seq_len
        row_mask = own_valid.astype(jnp.float32)[:, None]
        qkv_bias = jnp.concatenate([query_bias, jnp.zeros_like(query_bias), value_bias])
        qkv_low = (
            jnp.dot(seq_in, qkv_weight, preferred_element_type=jnp.float32) + qkv_bias
        ).astype(jnp.bfloat16)
        queries = qkv_low[:, :width]
        key_part = qkv_low[:, width : 2 * width]
        value_part = qkv_low[:, 2 * width :]
        keys_all, values_all = (
            lax.all_gather(key_part, "shard", axis=0, tiled=True),
            lax.all_gather(value_part, "shard", axis=0, tiled=True),
        )
        context, lse_rows = attend_forward(queries, keys_all, values_all, key_mask)
        context_low = context.astype(jnp.bfloat16)
        attn_out = jnp.dot(context_low, out_weight, preferred_element_type=jnp.float32) + out_bias
        hidden, norm_one_back = jax.vjp(
            layer_norm, seq_in.astype(jnp.float32) + attn_out, gain_one, shift_one
        )
        hidden_low = hidden.astype(jnp.bfloat16)
        up_proj = jnp.dot(hidden_low, up_weight, preferred_element_type=jnp.float32) + up_bias
        activation, gelu_back = jax.vjp(gelu_exact, up_proj)
        act_low = activation.astype(jnp.bfloat16)
        ffn_out = jnp.dot(act_low, down_weight, preferred_element_type=jnp.float32) + down_bias
        normed, norm_two_back = jax.vjp(layer_norm, hidden + ffn_out, gain_two, shift_two)
        layer_rows.append((normed * row_mask).astype(jnp.bfloat16))
        weights_full = unpack(
            (
                lax.all_gather(w_qkv, "shard", axis=0, tiled=True),
                lax.all_gather(bias_q, "shard", axis=0, tiled=True),
                lax.all_gather(bias_v, "shard", axis=0, tiled=True),
                lax.all_gather(w_out, "shard", axis=0, tiled=True),
                lax.all_gather(bias_out, "shard", axis=0, tiled=True),
                lax.all_gather(gain_attn, "shard", axis=0, tiled=True),
                lax.all_gather(shift_attn, "shard", axis=0, tiled=True),
                lax.all_gather(w_up, "shard", axis=0, tiled=True),
                lax.all_gather(bias_up, "shard", axis=0, tiled=True),
                lax.all_gather(w_down, "shard", axis=0, tiled=True),
                lax.all_gather(bias_down, "shard", axis=0, tiled=True),
                lax.all_gather(gain_ffn, "shard", axis=0, tiled=True),
                lax.all_gather(shift_ffn, "shard", axis=0, tiled=True),
            )
        )
        (
            qkv_weight,
            query_bias,
            value_bias,
            out_weight,
            out_bias,
            gain_one,
            shift_one,
            up_weight,
            up_bias,
            down_weight,
            down_bias,
            gain_two,
            shift_two,
        ) = weights_full
        grad_out = cotangent[batch_idx].astype(jnp.float32) * row_mask
        grad_res_two, grad_gain_two, grad_shift_two = norm_two_back(grad_out)
        grad_ffn_low = grad_res_two.astype(jnp.bfloat16)
        grad_act = contract_cols(grad_ffn_low, down_weight)
        (grad_up,) = gelu_back(grad_act)
        grad_up_low = grad_up.astype(jnp.bfloat16)
        grad_hidden = grad_res_two + contract_cols(grad_up_low, up_weight)
        grad_res_one, grad_gain_one, grad_shift_one = norm_one_back(grad_hidden)
        grad_attn_low = grad_res_one.astype(jnp.bfloat16)
        grad_ctx_low = contract_cols(grad_attn_low, out_weight).astype(jnp.bfloat16)
        keys_all, values_all = (
            lax.all_gather(key_part, "shard", axis=0, tiled=True),
            lax.all_gather(value_part, "shard", axis=0, tiled=True),
        )
        grad_q, grad_keys_all, grad_values_all = attend_backward(
            queries, keys_all, values_all, key_mask, lse_rows, grad_ctx_low
        )
        grad_keys, grad_values = (
            lax.psum_scatter(
                grad_keys_all.astype(jnp.bfloat16), "shard", scatter_dimension=0, tiled=True
            ).astype(jnp.float32),
            lax.psum_scatter(
                grad_values_all.astype(jnp.bfloat16), "shard", scatter_dimension=0, tiled=True
            ).astype(jnp.float32),
        )
        grad_qkv_low = jnp.concatenate([grad_q, grad_keys, grad_values], axis=1).astype(
            jnp.bfloat16
        )
        grad_input = grad_res_one + contract_cols(grad_qkv_low, qkv_weight)
        grad_rows.append(grad_input.astype(jnp.bfloat16))
        terms = (
            contract_rows(seq_in, grad_qkv_low),
            column_sums(grad_qkv_low[:, :width]),
            column_sums(grad_qkv_low[:, 2 * width :]),
            contract_rows(context_low, grad_attn_low),
            column_sums(grad_attn_low),
            grad_gain_one,
            grad_shift_one,
            contract_rows(hidden_low, grad_up_low),
            column_sums(grad_up_low),
            contract_rows(act_low, grad_ffn_low),
            column_sums(grad_ffn_low),
            grad_gain_two,
            grad_shift_two,
        )
        totals = [running + fresh for running, fresh in zip(totals, terms)]
    grad_local = (
        lax.psum_scatter(
            totals[0].astype(jnp.bfloat16), "shard", scatter_dimension=0, tiled=True
        ).astype(jnp.float32),
        lax.psum_scatter(
            totals[1].astype(jnp.bfloat16), "shard", scatter_dimension=0, tiled=True
        ).astype(jnp.float32),
        lax.psum_scatter(
            totals[2].astype(jnp.bfloat16), "shard", scatter_dimension=0, tiled=True
        ).astype(jnp.float32),
        lax.psum_scatter(
            totals[3].astype(jnp.bfloat16), "shard", scatter_dimension=0, tiled=True
        ).astype(jnp.float32),
        lax.psum_scatter(
            totals[4].astype(jnp.bfloat16), "shard", scatter_dimension=0, tiled=True
        ).astype(jnp.float32),
        lax.psum_scatter(
            totals[5].astype(jnp.bfloat16), "shard", scatter_dimension=0, tiled=True
        ).astype(jnp.float32),
        lax.psum_scatter(
            totals[6].astype(jnp.bfloat16), "shard", scatter_dimension=0, tiled=True
        ).astype(jnp.float32),
        lax.psum_scatter(
            totals[7].astype(jnp.bfloat16), "shard", scatter_dimension=0, tiled=True
        ).astype(jnp.float32),
        lax.psum_scatter(
            totals[8].astype(jnp.bfloat16), "shard", scatter_dimension=0, tiled=True
        ).astype(jnp.float32),
        lax.psum_scatter(
            totals[9].astype(jnp.bfloat16), "shard", scatter_dimension=0, tiled=True
        ).astype(jnp.float32),
        lax.psum_scatter(
            totals[10].astype(jnp.bfloat16), "shard", scatter_dimension=0, tiled=True
        ).astype(jnp.float32),
        lax.psum_scatter(
            totals[11].astype(jnp.bfloat16), "shard", scatter_dimension=0, tiled=True
        ).astype(jnp.float32),
        lax.psum_scatter(
            totals[12].astype(jnp.bfloat16), "shard", scatter_dimension=0, tiled=True
        ).astype(jnp.float32),
    )
    grad_total = (
        lax.psum(grad_local[0].astype(jnp.bfloat16), "grp").astype(jnp.float32),
        lax.psum(grad_local[1].astype(jnp.bfloat16), "grp").astype(jnp.float32),
        lax.psum(grad_local[2].astype(jnp.bfloat16), "grp").astype(jnp.float32),
        lax.psum(grad_local[3].astype(jnp.bfloat16), "grp").astype(jnp.float32),
        lax.psum(grad_local[4].astype(jnp.bfloat16), "grp").astype(jnp.float32),
        lax.psum(grad_local[5].astype(jnp.bfloat16), "grp").astype(jnp.float32),
        lax.psum(grad_local[6].astype(jnp.bfloat16), "grp").astype(jnp.float32),
        lax.psum(grad_local[7].astype(jnp.bfloat16), "grp").astype(jnp.float32),
        lax.psum(grad_local[8].astype(jnp.bfloat16), "grp").astype(jnp.float32),
        lax.psum(grad_local[9].astype(jnp.bfloat16), "grp").astype(jnp.float32),
        lax.psum(grad_local[10].astype(jnp.bfloat16), "grp").astype(jnp.float32),
        lax.psum(grad_local[11].astype(jnp.bfloat16), "grp").astype(jnp.float32),
        lax.psum(grad_local[12].astype(jnp.bfloat16), "grp").astype(jnp.float32),
    )
    return (
        jnp.stack(layer_rows),
        jnp.stack(grad_rows),
        grad_total[0],
        grad_total[1],
        grad_total[2],
        grad_total[3],
        grad_total[4],
        grad_total[5],
        grad_total[6],
        grad_total[7],
        grad_total[8],
        grad_total[9],
        grad_total[10],
        grad_total[11],
        grad_total[12],
    )


BF = jnp.bfloat16
GRANT = 60 << 20
COST = pl.CostEstimate(flops=1024, bytes_accessed=1024, transcendentals=0)
F32 = jnp.float32


def swap_core(value):
    return lax.ppermute(value, "grp", [(i, i ^ 1) for i in range(8)])


def swap_x(value):
    return lax.ppermute(value, "grp", [(i, i ^ 2) for i in range(8)])


def swap_y(value):
    return lax.ppermute(value, "grp", [(i, i ^ 4) for i in range(8)])


def swap_z(value, flip):
    return lax.ppermute(value, "shard", [(i, i ^ flip) for i in range(4)])


def swap_xy(value):
    return lax.ppermute(value, "grp", [(i, i ^ 6) for i in range(8)])


def dot32(left_mat, right_mat):
    return jnp.dot(left_mat, right_mat, preferred_element_type=F32)


def after(values, *others):
    return lax.optimization_barrier((values, others))[0]


def sequence_perm(flip):
    pairs = []
    for grp in range(8):
        for line in range(4):
            dst_grp = (grp & 6) | (line // 2)
            dst_line = 2 * (grp & 1) + ((line % 2) ^ flip)
            pairs.append((grp * 4 + line, dst_grp * 4 + dst_line))
    return pairs


def send_rows(first, second):
    first = lax.ppermute(first, ("grp", "shard"), sequence_perm(0))
    second = lax.ppermute(second, ("grp", "shard"), sequence_perm(1))
    return first, second


def return_rows(first, second):
    back = lambda flip: [(dst, src) for src, dst in sequence_perm(flip)]
    first = lax.ppermute(first, ("grp", "shard"), back(0))
    second = lax.ppermute(second, ("grp", "shard"), back(1))
    return first, second


def join_rows(first, second, parity):
    return jnp.where(parity == 0, jnp.stack([first, second]), jnp.stack([second, first]))


CORE, PLANE, LINE, PARITY = range(4)


def start_moves(moves, where_ref, sources, targets, sems):
    where = [where_ref[idx] for idx in range(4)]
    place = lambda at, unit: at if isinstance(at, int) else pl.multiple_of(at(*where), unit)
    copies = []
    for idx, (src, src_row, src_col, rows, cols, dst, dst_row, dst_col) in enumerate(moves):
        copies.append(
            pltpu.make_async_copy(
                sources[src].at[pl.ds(place(src_row, 8), rows), pl.ds(place(src_col, 128), cols)],
                targets[dst].at[pl.ds(place(dst_row, 8), rows), pl.ds(place(dst_col, 128), cols)],
                sems.at[idx],
            )
        )
    for copy in copies:
        copy.start()
    return copies


def move_kernel(count, moves, where_ref, *refs):
    for copy in start_moves(moves, where_ref, refs[:count], refs[count:-1], refs[-1]):
        copy.wait()


def move_blocks(where, sources, moves, shapes):
    moved = sum(move[3] * move[4] for move in moves) * 2
    return pl.pallas_call(
        functools.partial(move_kernel, len(sources), moves),
        out_shape=[jax.ShapeDtypeStruct(shape, sources[0].dtype) for shape in shapes],
        in_specs=[pl.BlockSpec(memory_space=pltpu.SMEM)]
        + [pl.BlockSpec(memory_space=pl.ANY)] * len(sources),
        out_specs=[pl.BlockSpec(memory_space=pltpu.VMEM)] * len(shapes),
        scratch_shapes=[pltpu.SemaphoreType.DMA((len(moves),))],
        cost_estimate=COST,
        compiler_params=pltpu.CompilerParams(vmem_limit_bytes=16 << 20),
    )(where, *sources)


def along_line(piece, hops):
    if hops == 1:
        return jnp.concatenate([swap_z(piece, flip) for flip in (1, 2, 3)], axis=0)
    far = swap_z(piece, 2)
    near = swap_z(jnp.concatenate([piece, far], axis=0), 1)
    height = piece.shape[0]
    return jnp.concatenate([near[:height], far, near[height:]], axis=0)


def across_plane(came):
    return [swap_x(came), swap_y(came), swap_xy(came)]


def placed_moves(first_src, height, piece_rows, col, cols, dst):
    moves = []
    for flip in range(4):
        for step in range(1, 4):
            at = lambda core, plane, line, parity, flip=flip, step=step: (
                (line ^ step) * (4 * piece_rows) + (plane ^ flip) * piece_rows
            )
            moves.append((first_src + flip, (step - 1) * height, col, piece_rows, cols, dst, at, 0))
    return moves


def pick(arr, idx, axis):
    return lax.dynamic_index_in_dim(arr, idx, axis, keepdims=False)


def add_low(left, right):
    return (left.astype(F32) + right.astype(F32)).astype(BF)


def reduce_first(grads, cut, col, row, small=None):
    join = lambda arrs: arrs[0] if len(arrs) == 1 else jnp.concatenate(arrs, axis=-1)
    below = lambda arr, idx, axis: arr if small is None else jnp.concatenate([arr, pick(small, idx, axis)], axis=-2)
    low_part = lambda idx: join([pick(grad[:, :, :, :cut], idx, 2) for grad in grads])
    high_part = lambda idx: below(join([pick(grad[:, :, :, cut:], idx, 1) for grad in grads]), idx, 1)
    sent = (low_part(1 - col), high_part(1 - row))
    return (low_part(col), high_part(row), swap_x(sent[0]), swap_y(sent[1])), sent


def reduce_second(state, col, row):
    low, high, low_got, high_got = state
    low, high = add_low(low, low_got), add_low(high, high_got)
    sent = (pick(low, 1 - row, 1), pick(high, 1 - col, 1))
    return (pick(low, row, 1), pick(high, col, 1), swap_y(sent[0]), swap_x(sent[1])), sent


def reduce_near(state, line):
    low, high, low_got, high_got = state
    mine = jnp.concatenate([add_low(low, low_got), add_low(high, high_got)], axis=1)
    pairs = mine.reshape((2, 2) + mine.shape[1:])
    sent = pick(pairs, 1 - line % 2, 1)
    return (pick(pairs, line % 2, 1), swap_z(sent, 1)), sent


def reduce_far(state, line):
    mine = add_low(*state)
    sent = pick(mine, 1 - line // 2, 0)
    return (pick(mine, line // 2, 0), swap_z(sent, 2)), sent


def direct_plane(grad, small, plane):
    block = lambda flip: jnp.concatenate([pick(grad, plane ^ flip, 1), pick(small, plane ^ flip, 1)], axis=1)
    blocks = [block(flip) for flip in range(4)]
    got = [swap_x(blocks[1]), swap_y(blocks[2]), swap_xy(blocks[3])]
    return [blocks[0]] + got, blocks[1:]


def direct_line(state, line):
    mine = sum(part.astype(F32) for part in state).astype(BF)
    sent = [pick(mine, line ^ flip, 0) for flip in range(4)]
    return [sent[0]] + [swap_z(sent[flip], flip) for flip in (1, 2, 3)], sent


def direct_spread(state):
    piece = sum(part.astype(F32) for part in state).astype(BF)
    return [piece] + across_plane(piece), piece


def final_kernel(layout, rows, extra, flips, where_ref, *refs):
    sources, outs, buf, sems = refs[:2], refs[2:-2], refs[-2], refs[-1]
    core, plane = where_ref[CORE], where_ref[PLANE]
    height = buf.shape[1]
    copies = []
    for idx in range(8):
        side, at = idx // 4, idx % 4
        owner = core if side == 0 else 1 - core
        copies.append(
            pltpu.make_async_copy(
                sources[side].at[pl.ds(at * height, height)],
                buf.at[owner * 4 + (plane ^ flips[at])],
                sems.at[idx],
            )
        )
    for copy in copies:
        copy.start()
    for copy in copies:
        copy.wait()
    for half in range(2):
        for part in range(4):
            for src_col, cols, dst, dst_row, dst_col in layout(half, part):
                outs[dst][pl.ds(dst_row, rows), pl.ds(dst_col, cols)] = buf[
                    half * 4 + part, pl.ds(0, rows), pl.ds(src_col, cols)
                ].astype(F32)
    if extra:
        outs[-1][...] = buf[0, pl.ds(rows, extra), :].astype(F32) + buf[4, pl.ds(rows, extra), :].astype(F32)


def spread_first(state, through_x):
    piece = add_low(*state)
    return piece, (swap_x if through_x else swap_y)(piece)


def spread_second(state, through_x):
    both = jnp.concatenate(state, axis=0)
    return both, (swap_y if through_x else swap_x)(both)


def spread_core(state):
    mine = jnp.concatenate(state, axis=0)
    return mine, swap_core(mine)


def finish_grad(where, state, through_x, layout, rows, shapes, extra=0):
    mine, other = state
    mine_flips = (0, 1, 2, 3) if through_x else (0, 2, 1, 3)
    height, cols = mine.shape[0] // 4, mine.shape[1]
    shapes = list(shapes) + ([(extra, cols)] if extra else [])
    return pl.pallas_call(
        functools.partial(final_kernel, layout, rows, extra, mine_flips),
        out_shape=[jax.ShapeDtypeStruct(shape, F32) for shape in shapes],
        in_specs=[pl.BlockSpec(memory_space=pltpu.SMEM)] + [pl.BlockSpec(memory_space=pl.ANY)] * 2,
        out_specs=[pl.BlockSpec(memory_space=pltpu.VMEM)] * len(shapes),
        scratch_shapes=[pltpu.VMEM((8, height, cols), BF), pltpu.SemaphoreType.DMA((8,))],
        cost_estimate=COST,
        compiler_params=pltpu.CompilerParams(vmem_limit_bytes=24 << 20),
    )(where, mine, other)


ROWS = 256


def row_spec(width, shift=0, steps=1):
    if shift:
        return pl.BlockSpec((ROWS, width), lambda blk: ((blk + shift) % steps, 0))
    return pl.BlockSpec((ROWS, width), lambda blk: (blk, 0))


def whole_spec(rows, width):
    return pl.BlockSpec((rows, width), lambda blk: (0, 0))


def mean_last(values):
    return jnp.mean(values, axis=-1, keepdims=True)


def norm_parts(values):
    centered = values - mean_last(values)
    scale = lax.rsqrt(mean_last(centered * centered) + eps)
    return centered * scale, scale


def norm_back(grad_normed, normed, scale):
    return scale * (grad_normed - mean_last(grad_normed) - normed * mean_last(grad_normed * normed))


def up_kernel(part_ref, got_ref, tok_ref, vec_ref, bias_ref, w_ref, low_ref, n_ref, r_ref, act_ref, slope_ref):
    vec = vec_ref[...]
    attn_out = part_ref[...].astype(F32) + got_ref[...].astype(F32) + vec[0:1]
    normed, scale = norm_parts(tok_ref[...].astype(F32) + attn_out)
    hidden = (normed * vec[1:2] + vec[2:3]).astype(BF)
    n_ref[...] = normed
    r_ref[...] = jnp.broadcast_to(scale, r_ref.shape)
    low_ref[...] = hidden
    for at in range(0, w_ref.shape[1], 384):
        cols = pl.ds(at, 384)
        up = dot32(hidden, w_ref[:, cols]) + bias_ref[:, cols]
        cdf = 0.5 + 0.5 * lax.erf(up * 0.5**0.5)
        act_ref[:, cols] = (up * cdf).astype(BF)
        slope = cdf + up * (jnp.exp(up * up * -0.5) * (2 * math.pi) ** -0.5)
        slope_ref[:, cols] = slope.astype(BF)


def ffn_up(part, got, tokens, vectors, up_bias, weight):
    rows, width = part.shape
    units = weight.shape[1]
    steps = rows // ROWS
    return pl.pallas_call(
        up_kernel,
        grid=(steps,),
        out_shape=[
            jax.ShapeDtypeStruct((rows, width), BF),
            jax.ShapeDtypeStruct((rows, width), F32),
            jax.ShapeDtypeStruct((rows, 128), F32),
            jax.ShapeDtypeStruct((rows, units), BF),
            jax.ShapeDtypeStruct((rows, units), BF),
        ],
        in_specs=[
            row_spec(width),
            row_spec(width, steps // 2, steps),
            row_spec(width),
            whole_spec(8, width),
            whole_spec(1, units),
            whole_spec(width, units),
        ],
        out_specs=[row_spec(width), row_spec(width), row_spec(128), row_spec(units), row_spec(units)],
        cost_estimate=COST,
        compiler_params=pltpu.CompilerParams(vmem_limit_bytes=20 << 20),
    )(part, got, tokens, vectors, up_bias, weight)


def turn_kernel(
    half_steps, part_ref, got_ref, n_ref, cot_ref, bias_ref, vec_ref, first_ref, second_ref, dr_ref, low_ref, sum_ref
):
    blk = pl.program_id(0)
    vec = vec_ref[...]
    hidden = n_ref[...] * vec[1:2] + vec[2:3]
    ffn_out = part_ref[...].astype(F32) + got_ref[...].astype(F32) + vec[3:4]
    normed, scale = norm_parts(hidden + ffn_out)
    mask = jnp.where(bias_ref[:, 0:1] < 0.0, 0.0, 1.0)
    result = ((normed * vec[4:5] + vec[5:6]) * mask).astype(BF)
    dy = cot_ref[...].astype(F32) * mask
    dr = norm_back(dy * vec[4:5], normed, scale)
    dr_low = dr.astype(BF)
    dr_ref[...] = dr
    low_ref[...] = dr_low

    @pl.when(blk == 0)
    def _():
        sum_ref[...] = jnp.zeros_like(sum_ref)
        first_ref[...] = result

    @pl.when(blk == 1)
    def _():
        second_ref[...] = result

    @pl.when(blk < half_steps)
    def _():
        sum_ref[0:1] += jnp.sum(dy * normed, axis=0, keepdims=True)
        sum_ref[1:2] += jnp.sum(dy, axis=0, keepdims=True)
        sum_ref[2:3] += jnp.sum(dr_low.astype(F32), axis=0, keepdims=True)


def norm_turn(part, got, n_one, cot, bias, vectors):
    rows, width = part.shape
    steps = rows // ROWS
    return pl.pallas_call(
        functools.partial(turn_kernel, steps // 2),
        grid=(steps,),
        out_shape=[jax.ShapeDtypeStruct((ROWS, width), BF)] * 2
        + [
            jax.ShapeDtypeStruct((rows, width), F32),
            jax.ShapeDtypeStruct((rows, width), BF),
            jax.ShapeDtypeStruct((8, width), F32),
        ],
        in_specs=[
            row_spec(width),
            row_spec(width, steps // 2, steps),
            row_spec(width),
            row_spec(width),
            row_spec(128),
            whole_spec(8, width),
        ],
        out_specs=[whole_spec(ROWS, width)] * 2 + [row_spec(width), row_spec(width), whole_spec(8, width)],
        cost_estimate=COST,
        compiler_params=pltpu.CompilerParams(vmem_limit_bytes=28 << 20),
    )(part, got, n_one, cot, bias, vectors)


def back_kernel(
    half_steps, where_ref, dr_ref, part_ref, got_ref, n_ref, r_ref, vec_ref, own_ref, low_ref, part_low_ref, sum_ref
):
    blk = pl.program_id(0)
    vec = vec_ref[...]
    normed = n_ref[...]
    dhidden = dr_ref[...] + (part_ref[...].astype(F32) + got_ref[...].astype(F32))
    dr = norm_back(dhidden * vec[1:2], normed, r_ref[:, 0:1])
    dr_low = dr.astype(BF)
    low_ref[...] = dr_low
    half = dr.shape[1] // 2
    part_low_ref[...] = jnp.where(where_ref[CORE] == 0, dr_low[:, :half], dr_low[:, half:])

    @pl.when(blk == 0)
    def _():
        sum_ref[...] = jnp.zeros_like(sum_ref)

    @pl.when(blk < half_steps)
    def _():
        own_ref[...] = dr
        sum_ref[0:1] += jnp.sum(dhidden * normed, axis=0, keepdims=True)
        sum_ref[1:2] += jnp.sum(dhidden, axis=0, keepdims=True)
        sum_ref[2:3] += jnp.sum(dr_low.astype(F32), axis=0, keepdims=True)


def norm_one_back(where, dr_two, part, got, n_one, r_one, vectors):
    rows, width = part.shape
    steps = rows // ROWS
    return pl.pallas_call(
        functools.partial(back_kernel, steps // 2),
        grid=(steps,),
        out_shape=[
            jax.ShapeDtypeStruct((rows // 2, width), F32),
            jax.ShapeDtypeStruct((rows, width), BF),
            jax.ShapeDtypeStruct((rows, width // 2), BF),
            jax.ShapeDtypeStruct((8, width), F32),
        ],
        in_specs=[
            pl.BlockSpec(memory_space=pltpu.SMEM),
            row_spec(width),
            row_spec(width),
            row_spec(width, steps // 2, steps),
            row_spec(width),
            row_spec(128),
            whole_spec(8, width),
        ],
        out_specs=[
            pl.BlockSpec((ROWS, width), lambda blk: (jnp.minimum(blk, steps // 2 - 1), 0)),
            row_spec(width),
            row_spec(width // 2),
            whole_spec(8, width),
        ],
        cost_estimate=COST,
        compiler_params=pltpu.CompilerParams(vmem_limit_bytes=28 << 20),
    )(where, dr_two, part, got, n_one, r_one, vectors)


Q_BLOCK = 256
PAIR = 128


def contract_last(left_mat, right_mat):
    return lax.dot_general(
        left_mat, right_mat, (((1,), (1,)), ((), ())), preferred_element_type=F32
    )


def head_lanes(block, head):
    lane = lax.broadcasted_iota(jnp.int32, block.shape, 1)
    return jnp.where((lane // HD) == head, block, jnp.zeros_like(block))


def attend_fwd_kernel(q_ref, k_ref, v_ref, bias_ref, ctx_ref, lse_ref, vt_ref):
    vt_ref[...] = v_ref[...].T

    @pl.loop(0, q_ref.shape[0] // Q_BLOCK)
    def _(blk):
        at = pl.multiple_of(blk * Q_BLOCK, Q_BLOCK)
        q_blk = q_ref[pl.ds(at, Q_BLOCK), :] * jnp.asarray(HD ** (-0.5), BF)
        outs = []
        for head in range(2):
            scores = contract_last(k_ref[...], head_lanes(q_blk, head))
            scores = scores + jnp.concatenate([bias_ref[...]] * (Q_BLOCK // 128), axis=1)
            top = jnp.max(scores, axis=0, keepdims=True)
            exps = jnp.exp(scores - top)
            total = jnp.sum(exps, axis=0, keepdims=True)
            out = dot32(vt_ref[pl.ds(head * HD, HD), :], exps.astype(BF))
            outs.append(out * (1.0 / total))
            lse_ref[0, pl.ds(head, 1), pl.ds(at, Q_BLOCK)] = top + jnp.log(total)
        ctx_ref[pl.ds(at, Q_BLOCK), :] = jnp.concatenate(outs, axis=0).T.astype(BF)


def attend_bwd_kernel(
    q_ref, k_ref, v_ref, bias_ref, lse_ref, grad_ref, dq_ref, dk_ref, dv_ref, kt_ref, dk_acc, dv_acc
):
    kt_ref[...] = k_ref[...].T
    dk_acc[...] = jnp.zeros_like(dk_acc)
    dv_acc[...] = jnp.zeros_like(dv_acc)

    @pl.loop(0, q_ref.shape[0] // Q_BLOCK)
    def _(blk):
        at = pl.multiple_of(blk * Q_BLOCK, Q_BLOCK)
        q_blk = q_ref[pl.ds(at, Q_BLOCK), :] * jnp.asarray(HD ** (-0.5), BF)
        grad_blk = grad_ref[pl.ds(at, Q_BLOCK), :]
        outs = []
        for head in range(2):
            q_head = head_lanes(q_blk, head)
            grad_head = head_lanes(grad_blk, head)
            scores = contract_last(k_ref[...], q_head)
            scores = scores + jnp.concatenate([bias_ref[...]] * (Q_BLOCK // 128), axis=1)
            probs = jnp.exp(scores - lse_ref[0, pl.ds(head, 1), pl.ds(at, Q_BLOCK)])
            weighed = probs * contract_last(v_ref[...], grad_head)
            delta = jnp.sum(weighed, axis=0, keepdims=True)
            grad_scores = (weighed - probs * delta).astype(BF)
            dk_acc[...] += dot32(grad_scores, q_head)
            dv_acc[...] += dot32(probs.astype(BF), grad_head)
            outs.append(dot32(kt_ref[pl.ds(head * HD, HD), :], grad_scores))
        dq = jnp.concatenate(outs, axis=0).T * (HD ** (-0.5))
        dq_ref[pl.ds(at, Q_BLOCK), :] = dq.astype(BF)

    dk_ref[...] = dk_acc[...].astype(BF)
    dv_ref[...] = dv_acc[...].astype(BF)


def column_spec(rows, first):
    return pl.BlockSpec((rows, PAIR), lambda pair: (0, first + pair))


def attend_chip_forward(qkv, bias, pair):
    rows, half = qkv.shape[0], qkv.shape[1] // 3
    pairs = half // PAIR
    return pl.pallas_call(
        attend_fwd_kernel,
        grid=(1,),
        out_shape=[
            jax.ShapeDtypeStruct((rows, PAIR), BF),
            jax.ShapeDtypeStruct((1, 2, rows), F32),
        ],
        in_specs=[column_spec(rows, idx * pairs + pair) for idx in range(3)]
        + [pl.BlockSpec((rows, 128), lambda step: (0, 0))],
        out_specs=[column_spec(rows, 0), pl.BlockSpec((1, 2, rows), lambda step: (0, 0, 0))],
        scratch_shapes=[pltpu.VMEM((PAIR, rows), BF)],
        cost_estimate=COST,
        compiler_params=pltpu.CompilerParams(vmem_limit_bytes=20 << 20),
    )(qkv, qkv, qkv, bias)


def attend_chip_backward(qkv, bias, lse, grad_ctx, pair):
    rows, half = qkv.shape[0], qkv.shape[1] // 3
    pairs = half // PAIR
    return pl.pallas_call(
        attend_bwd_kernel,
        grid=(1,),
        out_shape=[jax.ShapeDtypeStruct((rows, PAIR), BF)] * 3,
        in_specs=[column_spec(rows, idx * pairs + pair) for idx in range(3)]
        + [
            pl.BlockSpec((rows, 128), lambda step: (0, 0)),
            pl.BlockSpec((1, 2, rows), lambda step: (0, 0, 0)),
            column_spec(rows, pair),
        ],
        out_specs=[column_spec(rows, 0)] * 3,
        scratch_shapes=[
            pltpu.VMEM((PAIR, rows), BF),
            pltpu.VMEM((rows, PAIR), F32),
            pltpu.VMEM((rows, PAIR), F32),
        ],
        cost_estimate=COST,
        compiler_params=pltpu.CompilerParams(vmem_limit_bytes=24 << 20),
    )(qkv, qkv, qkv, bias, lse, grad_ctx)


def pack_kernel(count, moves, vec_at, slab, where_ref, *refs):
    sources, vecs = refs[:count], refs[count : count + 9]
    targets, sems = refs[count + 9 : -1], refs[-1]
    copies = start_moves(moves, where_ref, sources, targets, sems)
    dst, row = vec_at
    width = targets[dst].shape[1]
    rows = [vec[...].reshape(1, slab).astype(F32) for vec in vecs[:8]]
    wide = vecs[8][...].reshape(1, -1).astype(F32)
    count_wide = wide.shape[1] // slab
    rows += [wide[:, :slab]]
    rows += [pltpu.roll(wide, wide.shape[1] - idx * slab, 1)[:, :slab] for idx in range(1, count_wide)]
    rows += [jnp.zeros((4, slab), F32)]
    block = jnp.concatenate(rows, axis=0)
    targets[dst][pl.ds(row, 16), :] = jnp.concatenate(
        [block, jnp.zeros((16, width - slab), F32)], axis=1
    ).astype(BF)
    for copy in copies:
        copy.wait()


def pack_blocks(where, sources, vecs, moves, shapes, vec_at, slab):
    return pl.pallas_call(
        functools.partial(pack_kernel, len(sources), moves, vec_at, slab),
        out_shape=[jax.ShapeDtypeStruct(shape, BF) for shape in shapes],
        in_specs=[pl.BlockSpec(memory_space=pltpu.SMEM)]
        + [pl.BlockSpec(memory_space=pl.ANY)] * len(sources)
        + [pl.BlockSpec(memory_space=pltpu.VMEM)] * len(vecs),
        out_specs=[pl.BlockSpec(memory_space=pltpu.VMEM)] * len(shapes),
        scratch_shapes=[pltpu.SemaphoreType.DMA((len(moves),))],
        cost_estimate=COST,
        compiler_params=pltpu.CompilerParams(vmem_limit_bytes=60 << 20),
    )(where, *sources, *vecs)


def vector_kernel(height, at, slab, where_ref, own_ref, came_ref, block_ref, qkv_ref, up_ref, buf, sems):
    line = where_ref[LINE]
    copies = [pltpu.make_async_copy(own_ref.at[pl.ds(at, 16)], buf.at[line], sems.at[0])]
    for step in range(1, 4):
        copies.append(
            pltpu.make_async_copy(
                came_ref.at[pl.ds((step - 1) * height + at, 16)], buf.at[line ^ step], sems.at[step]
            )
        )
    for copy in copies:
        copy.start()
    for copy in copies:
        copy.wait()
    width = block_ref.shape[1]
    half = width // 2
    joined = jnp.zeros((16, width), F32)
    lane = lax.broadcasted_iota(jnp.int32, (16, width), 1)
    wide = []
    for idx in range(4):
        rows = jnp.where(lane < slab, buf[idx, :, :width].astype(F32), 0.0)
        joined += rows if idx == 0 else pltpu.roll(rows, idx * slab, 1)
        row = rows[8:9]
        for part in range(1, 4):
            row += pltpu.roll(rows[8 + part : 9 + part], part * slab, 1)
        wide.append(row)
    low = where_ref[CORE] == 0
    pick_half = lambda row: jnp.where(low, row[:, :half], row[:, half:])
    block_ref[...] = jnp.concatenate([joined[2:8], jnp.zeros((2, width), F32)], axis=0)
    qkv_ref[...] = jnp.concatenate(
        [pick_half(joined[0:1]), jnp.zeros((1, half), F32), pick_half(joined[1:2])], axis=1
    )
    up_ref[...] = jnp.concatenate([pick_half(row) for row in wide], axis=1)


def join_vectors(where, own, came, at, slab, width):
    height = came.shape[0] // 3
    return pl.pallas_call(
        functools.partial(vector_kernel, height, at, slab),
        out_shape=[
            jax.ShapeDtypeStruct((8, width), F32),
            jax.ShapeDtypeStruct((1, 3 * width // 2), F32),
            jax.ShapeDtypeStruct((1, 2 * width), F32),
        ],
        in_specs=[pl.BlockSpec(memory_space=pltpu.SMEM)] + [pl.BlockSpec(memory_space=pl.ANY)] * 2,
        out_specs=[pl.BlockSpec(memory_space=pltpu.VMEM)] * 3,
        scratch_shapes=[pltpu.VMEM((4, 16, own.shape[1]), BF), pltpu.SemaphoreType.DMA((4,))],
        cost_estimate=COST,
        compiler_params=pltpu.CompilerParams(vmem_limit_bytes=4 << 20),
    )(where, own, came)


def small_kernel(slab, where_ref, one_ref, two_ref, up_ref, qkv_ref, out_ref):
    width = one_ref.shape[1]
    half = width // 2
    low = where_ref[CORE] == 0
    zero = jnp.zeros((1, half), F32)
    on_core = lambda row: jnp.where(
        low, jnp.concatenate([row, zero], axis=1), jnp.concatenate([zero, row], axis=1)
    )
    one, two = one_ref[...], two_ref[...]
    rows = jnp.concatenate(
        [
            on_core(qkv_ref[:, :half]),
            on_core(qkv_ref[:, 2 * half :]),
            one[2:3],
            one[0:1],
            one[1:2],
            two[2:3],
            two[0:1],
            two[1:2],
        ],
        axis=0,
    )
    out_ref[...] = jnp.zeros_like(out_ref)
    for idx in range(4):
        wide = on_core(up_ref[:, idx * half : (idx + 1) * half])
        at = lambda row, part: row if part == 0 else pltpu.roll(row, width - part * slab, 1)
        parts = [at(wide, part)[:, :slab] for part in range(4)]
        block = jnp.concatenate([at(rows, idx)[:, :slab]] + parts + [jnp.zeros((4, slab), F32)], axis=0)
        out_ref[idx, :, 0:slab] = block.astype(BF)


def small_grads(where, sums_one, sums_two, up_sums, qkv_sums, slab):
    vmem = pl.BlockSpec(memory_space=pltpu.VMEM)
    return pl.pallas_call(
        functools.partial(small_kernel, slab),
        out_shape=jax.ShapeDtypeStruct((4, 16, qkv_sums.shape[1]), BF),
        in_specs=[pl.BlockSpec(memory_space=pltpu.SMEM)] + [vmem] * 4,
        out_specs=vmem,
        compiler_params=pltpu.CompilerParams(vmem_limit_bytes=4 << 20),
    )(where, sums_one, sums_two, up_sums, qkv_sums)


def per_device_chip(
    tokens,
    cotangent,
    lengths,
    w_qkv,
    bias_q,
    bias_v,
    w_out,
    bias_out,
    gain_attn,
    shift_attn,
    w_up,
    bias_up,
    w_down,
    bias_down,
    gain_ffn,
    shift_ffn,
):
    quarter, width = tokens.shape[1:]
    half_rows = 2 * quarter
    units = w_up.shape[1] // 2
    slab = w_qkv.shape[0]
    wide = w_down.shape[0]
    half = width // 2
    slab_part, wide_part = slab // 4, wide // 8
    vec_rows = 16
    group = lax.axis_index("grp")
    line = lax.axis_index("shard")
    core = group % 2
    plane = group // 2
    col, row = plane % 2, plane // 2
    parity = line % 2
    where = jnp.stack([core, plane, line, parity]).astype(jnp.int32)

    vecs = [bias_q, bias_v, bias_out, gain_attn, shift_attn, bias_down, gain_ffn, shift_ffn, bias_up]
    sources = [tokens.reshape(half_rows, width), w_qkv]
    moves = []
    moves.append((0, lambda c, p, z, e: e * quarter, 0, quarter, width, 0, 0, 0))
    moves.append((0, lambda c, p, z, e: (1 - e) * quarter, 0, quarter, width, 1, 0, 0))
    slab_at = lambda c, p, z, e: p * slab_part
    for idx in range(3):
        at = lambda c, p, z, e, idx=idx: idx * width + c * half
        moves.append((1, slab_at, at, slab_part, half, 2, 0, idx * half))
    tok_first, tok_second, qkv_piece = pack_blocks(
        where,
        sources,
        vecs,
        moves,
        [(quarter, width)] * 2 + [(slab_part + vec_rows, 3 * half)],
        (2, slab_part),
        slab,
    )
    moves = []
    for idx in range(4):
        at = lambda c, p, z, e, idx=idx: idx * wide + c * (wide // 2)
        moves.append((1, slab_at, at, slab_part, wide // 2, 2, 0, idx * (wide // 2)))
    moves.append((2, slab_at, lambda c, p, z, e: c * half, slab_part, half, 2, 0, units))
    moves.append((3, lambda c, p, z, e: c * (wide // 2) + p * wide_part, 0, wide_part, width, 3, 0, 0))
    moves.append((0, lambda c, p, z, e: e * quarter, 0, quarter, width, 0, 0, 0))
    moves.append((0, lambda c, p, z, e: (1 - e) * quarter, 0, quarter, width, 1, 0, 0))
    cot_first, cot_second, up_piece, down_piece = move_blocks(
        where,
        [after(cotangent.reshape(half_rows, width), qkv_piece), w_up, w_out, w_down],
        moves,
        [(quarter, width)] * 2 + [(slab_part, units + half), (wide_part, width)],
    )
    slab_start = lambda c, p, z, e: z * slab

    qkv_came = along_line(qkv_piece, 1)
    tok_first, tok_second = send_rows(tok_first, tok_second)
    len_other = swap_core(after(lengths, tok_first))
    len_all = jnp.where(core == 0, jnp.concatenate([lengths, len_other]), jnp.concatenate([len_other, lengths]))
    seq_len = len_all[line]
    place = lax.broadcasted_iota(jnp.int32, (4 * quarter, 128), 0)
    place = ((place // quarter) ^ (2 * core + parity)) * quarter + place % quarter
    bias = jnp.where(place < seq_len, 0.0, masked_score).astype(F32)

    qkv_plane = across_plane(qkv_came)
    tok_own = jnp.concatenate(after([tok_first, tok_second], qkv_came), axis=0)
    tok_all = jnp.concatenate([tok_own, swap_core(after(tok_own, *qkv_plane))], axis=0)
    vec_block, qkv_bias, up_bias = join_vectors(where, qkv_piece, after(qkv_came, tok_own), slab_part, slab, width)
    up_came = along_line(after(up_piece, tok_own), 1)
    up_plane = across_plane(up_came)
    down_came = along_line(after(down_piece, up_came), 1)

    moves = []
    for idx in range(3):
        at = lambda c, p, z, e, idx=idx: idx * width + c * half
        moves.append((0, 0, at, slab, half, 0, slab_start, idx * half))
    moves += placed_moves(1, slab_part + vec_rows, slab_part, 0, 3 * half, 0)
    (qkv_weight,) = move_blocks(
        where, [w_qkv, after(qkv_came, up_came)] + qkv_plane, moves, [(width, 3 * half)]
    )

    qkv = (dot32(tok_all, qkv_weight) + qkv_bias).astype(BF)
    pairs = half // PAIR
    contexts, lses = [], []
    for pair in range(pairs):
        qkv_in = qkv
        if pair == 1:
            down_came = after(down_came, contexts[0])
            down_plane = across_plane(down_came)
            cot_first, cot_second = send_rows(*after((cot_first, cot_second), down_came))
            qkv_in = after(qkv, contexts[-1], down_came, up_plane[0])
        elif pair > 1:
            qkv_in = after(qkv, contexts[-1], *up_plane, down_plane[0])
        got = attend_chip_forward(qkv_in, bias, pair)
        contexts.append(got[0])
        lses.append(got[1])
    context = jnp.concatenate(contexts, axis=1)
    context_got = swap_core(context)

    moves = []
    for idx in range(4):
        at = lambda c, p, z, e, idx=idx: idx * wide + c * (wide // 2)
        moves.append((0, 0, at, slab, wide // 2, 0, slab_start, idx * (wide // 2)))
    moves.append((1, 0, lambda c, p, z, e: c * half, slab, half, 1, slab_start, 0))
    moves += placed_moves(2, slab_part, slab_part, 0, units, 0)
    moves += placed_moves(2, slab_part, slab_part, units, half, 1)
    up_weight, out_half = move_blocks(
        where,
        [w_up, w_out, after(up_came, down_came)] + up_plane,
        moves,
        [(width, units), (width, half)],
    )
    out_got = swap_core(out_half)
    moves = [
        (0, lambda c, p, z, e: c * half, 0, half, half, 0, 0, lambda c, p, z, e: c * half),
        (1, lambda c, p, z, e: c * half, 0, half, half, 0, 0, lambda c, p, z, e: (1 - c) * half),
        (2, 0, 0, 4 * quarter, half, 1, 0, lambda c, p, z, e: c * half),
        (3, 0, 0, half_rows, half, 1, half_rows, lambda c, p, z, e: (1 - c) * half),
        (3, half_rows, 0, half_rows, half, 1, 0, lambda c, p, z, e: (1 - c) * half),
    ]
    out_weight, context_all = move_blocks(
        where, [out_half, out_got, context, context_got], moves, [(half, width), (4 * quarter, width)]
    )
    part = dot32(context, out_weight).astype(BF)
    hidden_low, n_one, r_one, act, slope = ffn_up(
        part, after(swap_core(part), cot_first, cot_second), tok_all, vec_block, up_bias, up_weight
    )

    cot_own = jnp.concatenate([cot_first, cot_second], axis=0)
    moves = [(0, lambda c, p, z, e: c * (wide // 2), 0, wide // 2, width, 0, lambda c, p, z, e: z * (wide // 2), 0)]
    moves += placed_moves(1, wide_part, wide_part, 0, width, 0)
    (down_weight,) = move_blocks(where, [w_down, after(down_came, act, cot_own)] + down_plane, moves, [(units, width)])
    part = dot32(act, down_weight).astype(BF)
    cot_all = jnp.concatenate([cot_own, swap_core(cot_own)], axis=0)
    out_first, out_second, dr_two, dffn, sums_two = norm_turn(
        part, swap_core(part), n_one, cot_all, bias, vec_block
    )

    blocks = lambda grad: grad.reshape(4, 2, 2, grad.shape[0] // 16, grad.shape[1])
    g_down = contract_rows(act, dffn).astype(BF)
    down_state, sent = reduce_first([blocks(g_down)], wide_part // 2, col, row)
    dffn = after(dffn, sent)
    dup = (contract_cols(dffn, down_weight) * slope.astype(F32)).astype(BF)
    part = contract_cols(dup, up_weight).astype(BF)
    got = swap_core(part)
    dup_late = after(dup, part)
    g_up = contract_rows(hidden_low, dup_late).astype(BF)
    up_sums = jnp.sum(dup_late.astype(F32), axis=0, keepdims=True)
    dr_one, dattn, dattn_part, sums_one = norm_one_back(
        where, dr_two, part, after(got, g_up), n_one, r_one, vec_block
    )
    grad_ctx = contract_cols(dattn, out_weight).astype(BF)
    g_out = contract_rows(context_all, after(dattn_part, grad_ctx)).astype(BF)
    down_state, sent = reduce_second(after(down_state, g_out), col, row)
    up_state, sent_up = reduce_first([blocks(g_up), blocks(after(g_out, sent))], slab_part // 2, col, row)

    layer_first, layer_second = return_rows(*after((out_first, out_second), g_down))
    layer_out = join_rows(*after((layer_first, layer_second), sent_up), parity)

    dqkv = []
    qkv_in = after(qkv, sent_up, layer_out)
    dqkv.append(attend_chip_backward(qkv_in, bias, lses[0], grad_ctx, 0))
    down_state, sent = reduce_near(after(down_state, dqkv[-1]), line)
    qkv_in = after(qkv, sent)
    dqkv.append(attend_chip_backward(qkv_in, bias, lses[1], grad_ctx, 1))
    up_state, sent = reduce_second(after(up_state, dqkv[-1]), col, row)
    qkv_in = after(qkv, sent)
    for pair in range(2, pairs):
        dqkv.append(attend_chip_backward(qkv_in, bias, lses[pair], grad_ctx, pair))
    dqkv = jnp.concatenate([part[idx] for idx in range(3) for part in dqkv], axis=1)
    down_state, sent = reduce_far(after(down_state, dqkv), line)
    qkv_sums = jnp.sum(dqkv.astype(F32), axis=0, keepdims=True)
    g_qkv = contract_rows(tok_all, after(dqkv, sent)).astype(BF).reshape(4, 4, slab_part, 3 * half)
    small = small_grads(where, sums_one, sums_two, up_sums, qkv_sums, slab)
    small = jnp.pad(small[:, None], ((0, 0), (0, 3), (0, 0), (0, 0)))
    qkv_state, sent = direct_plane(g_qkv, small, plane)
    dtok = contract_cols(after(dqkv, sent), qkv_weight)
    dtok_got = swap_core(dtok[half_rows:].astype(BF))
    up_state, sent_up = reduce_near(after(up_state, dtok), line)
    grad_tok = (dr_one + dtok[:half_rows] + after(dtok_got, sent_up).astype(F32)).astype(BF)
    back_first, back_second = return_rows(grad_tok[:quarter], grad_tok[quarter:])
    down_state = spread_first(after(down_state, grad_tok), True)
    qkv_state, sent = direct_line(after(qkv_state, down_state[0]), line)
    up_state, sent_up = reduce_far(after(up_state, sent), line)
    down_state = spread_second(after(down_state, sent_up), True)
    qkv_state, sent = direct_spread(after(qkv_state, down_state[0]))
    up_state = spread_first(after(up_state, sent), False)
    down_state = spread_core(after(down_state, up_state[0]))
    qkv_state = spread_core(after(qkv_state, down_state[0]))
    up_state = spread_second(after(up_state, qkv_state[0]), False)
    grad_tokens = join_rows(*after((back_first, back_second), up_state[0]), parity)
    up_state = spread_core(after(up_state, grad_tokens))

    down_layout = lambda half_at, part: [(0, width, 0, half_at * (wide // 2) + part * wide_part, 0)]
    (grad_down,) = finish_grad(where, down_state, True, down_layout, wide_part, [(wide, width)])
    up_layout = lambda half_at, part: [
        (idx * (wide // 2), wide // 2, 0, part * slab_part, idx * wide + half_at * (wide // 2)) for idx in range(4)
    ] + [(units, half, 1, part * slab_part, half_at * half)]
    qkv_layout = lambda half_at, part: [
        (idx * half, half, 0, part * slab_part, idx * width + half_at * half) for idx in range(3)
    ]
    grad_qkv, small_sum = finish_grad(
        where, after(qkv_state, grad_down), True, qkv_layout, slab_part, [(slab, 3 * width)], extra=vec_rows
    )
    grad_up, grad_out = finish_grad(
        where, after(up_state, grad_qkv), False, up_layout, slab_part, [(slab, 2 * units), (slab, width)]
    )
    vec_of = lambda idx: small_sum[idx, :slab]
    return (
        layer_out,
        grad_tokens,
        grad_qkv,
        vec_of(0),
        vec_of(1),
        grad_out,
        vec_of(2),
        vec_of(3),
        vec_of(4),
        grad_up,
        small_sum[8 : 8 + wide // slab, :slab].reshape(wide),
        grad_down,
        vec_of(5),
        vec_of(6),
        vec_of(7),
    )


def solution(mesh):
    placed = (
        P("grp", "shard", None),
        P("grp", "shard", None),
        P("grp"),
        P("shard", None),
        P("shard"),
        P("shard"),
        P("shard", None),
        P("shard"),
        P("shard"),
        P("shard"),
        P("shard", None),
        P("shard"),
        P("shard", None),
        P("shard"),
        P("shard"),
        P("shard"),
    )
    plan = per_device_chip if dict(mesh.shape) == {"grp": 8, "shard": 4} else per_device
    return jax.shard_map(
        plan,
        mesh=mesh,
        in_specs=placed,
        out_specs=(
            P("grp", "shard", None),
            P("grp", "shard", None),
            P("shard", None),
            P("shard"),
            P("shard"),
            P("shard", None),
            P("shard"),
            P("shard"),
            P("shard"),
            P("shard", None),
            P("shard"),
            P("shard", None),
            P("shard"),
            P("shard"),
            P("shard"),
        ),
        check_vma=False,
    )
```

```python
import functools
import math

import jax
import jax.numpy as jnp
from jax import lax
from jax.experimental import pallas as pl
from jax.experimental.pallas import tpu as pltpu
from jax.sharding import PartitionSpec as P


H = 12
HD = 64


eps = 1e-12
masked_score = -1000000000.0


def layer_norm(values_in, gain_vec, shift_vec):
    row_mean = jnp.mean(values_in, axis=-1, keepdims=True)
    centered = values_in - row_mean
    variance = jnp.mean(centered * centered, axis=-1, keepdims=True)
    return centered * lax.rsqrt(variance + eps) * gain_vec + shift_vec


def gelu_exact(values_in):
    return jax.nn.gelu(values_in, approximate=False)


def contract_cols(left_mat, right_mat):
    return lax.dot_general(
        left_mat, right_mat, (((1,), (1,)), ((), ())), preferred_element_type=jnp.float32
    )


def contract_rows(left_mat, right_mat):
    return lax.dot_general(
        left_mat, right_mat, (((0,), (0,)), ((), ())), preferred_element_type=jnp.float32
    )


def column_sums(matrix):
    return jnp.sum(matrix.astype(jnp.float32), axis=0)


def unpack(weights_full):
    (
        qkv_weight,
        query_bias,
        value_bias,
        out_weight,
        out_bias,
        gain_one,
        shift_one,
        up_weight,
        up_bias,
        down_weight,
        down_bias,
        gain_two,
        shift_two,
    ) = weights_full
    as_float = lambda vector: vector.astype(jnp.float32)
    return (
        qkv_weight,
        as_float(query_bias),
        as_float(value_bias),
        out_weight,
        as_float(out_bias),
        as_float(gain_one),
        as_float(shift_one),
        up_weight,
        as_float(up_bias),
        down_weight,
        as_float(down_bias),
        as_float(gain_two),
        as_float(shift_two),
    )


def head_scores(queries, keys, key_mask, head_idx):
    col_start = head_idx * HD
    q_head = lax.dynamic_slice_in_dim(queries, col_start, HD, 1)
    k_head = lax.dynamic_slice_in_dim(keys, col_start, HD, 1)
    scores = contract_cols(q_head, k_head) * HD ** (-0.5)
    return (q_head, k_head, jnp.where(key_mask[None, :], scores, masked_score))


def attend_forward(queries, keys, values, key_mask):
    row_count, width = queries.shape

    def one_head(head_idx, carry):
        context, lse_rows = carry
        q_head, k_head, scores = head_scores(queries, keys, key_mask, head_idx)
        v_head = lax.dynamic_slice_in_dim(values, head_idx * HD, HD, 1)
        row_max = jnp.max(scores, axis=1, keepdims=True)
        exp_scores = jnp.exp(scores - row_max)
        row_total = jnp.sum(exp_scores, axis=1, keepdims=True)
        prob_low = (exp_scores / row_total).astype(jnp.bfloat16)
        head_out = jnp.dot(prob_low, v_head, preferred_element_type=jnp.float32)
        context = lax.dynamic_update_slice_in_dim(context, head_out, head_idx * HD, 1)
        lse_rows = lax.dynamic_update_slice_in_dim(
            lse_rows, row_max + jnp.log(row_total), head_idx, 1
        )
        return (context, lse_rows)

    start_state = (
        jnp.zeros((row_count, width), jnp.float32),
        jnp.zeros((row_count, H), jnp.float32),
    )
    return lax.fori_loop(0, H, one_head, start_state)


def attend_backward(queries, keys, values, key_mask, lse_rows, grad_context):
    row_count, width = queries.shape
    slot_count = keys.shape[0]

    def one_head(head_idx, carry):
        grad_q, grad_k, grad_v = carry
        col_start = head_idx * HD
        q_head, k_head, scores = head_scores(queries, keys, key_mask, head_idx)
        v_head = lax.dynamic_slice_in_dim(values, col_start, HD, 1)
        grad_head = lax.dynamic_slice_in_dim(grad_context, col_start, HD, 1)
        probs = jnp.exp(scores - lax.dynamic_slice_in_dim(lse_rows, head_idx, 1, 1))
        grad_probs = contract_cols(grad_head, v_head)
        delta = jnp.sum(probs * grad_probs, axis=1, keepdims=True)
        grad_scores = (probs * (grad_probs - delta)).astype(jnp.bfloat16)
        head_gq = jnp.dot(grad_scores, k_head, preferred_element_type=jnp.float32) * HD ** (-0.5)
        head_gk = contract_rows(grad_scores, q_head) * HD ** (-0.5)
        head_gv = contract_rows(probs.astype(jnp.bfloat16), grad_head)
        grad_q = lax.dynamic_update_slice_in_dim(grad_q, head_gq, col_start, 1)
        grad_k = lax.dynamic_update_slice_in_dim(grad_k, head_gk, col_start, 1)
        grad_v = lax.dynamic_update_slice_in_dim(grad_v, head_gv, col_start, 1)
        return (grad_q, grad_k, grad_v)

    start_state = (
        jnp.zeros((row_count, width), jnp.float32),
        jnp.zeros((slot_count, width), jnp.float32),
        jnp.zeros((slot_count, width), jnp.float32),
    )
    return lax.fori_loop(0, H, one_head, start_state)


def per_device(
    tokens,
    cotangent,
    lengths,
    w_qkv,
    bias_q,
    bias_v,
    w_out,
    bias_out,
    gain_attn,
    shift_attn,
    w_up,
    bias_up,
    w_down,
    bias_down,
    gain_ffn,
    shift_ffn,
):
    batch_count, row_count, width = tokens.shape
    dev_count = lax.axis_size("shard")
    slot_count = row_count * dev_count
    first_row = lax.axis_index("shard") * row_count
    key_place = jnp.arange(slot_count, dtype=jnp.int32)
    row_place = first_row + jnp.arange(row_count, dtype=jnp.int32)
    sharded = (
        w_qkv,
        bias_q,
        bias_v,
        w_out,
        bias_out,
        gain_attn,
        shift_attn,
        w_up,
        bias_up,
        w_down,
        bias_down,
        gain_ffn,
        shift_ffn,
    )
    totals = [
        jnp.zeros((piece.shape[0] * dev_count,) + piece.shape[1:], jnp.float32) for piece in sharded
    ]
    layer_rows = []
    grad_rows = []
    for batch_idx in range(batch_count):
        weights_full = unpack(
            (
                lax.all_gather(w_qkv, "shard", axis=0, tiled=True),
                lax.all_gather(bias_q, "shard", axis=0, tiled=True),
                lax.all_gather(bias_v, "shard", axis=0, tiled=True),
                lax.all_gather(w_out, "shard", axis=0, tiled=True),
                lax.all_gather(bias_out, "shard", axis=0, tiled=True),
                lax.all_gather(gain_attn, "shard", axis=0, tiled=True),
                lax.all_gather(shift_attn, "shard", axis=0, tiled=True),
                lax.all_gather(w_up, "shard", axis=0, tiled=True),
                lax.all_gather(bias_up, "shard", axis=0, tiled=True),
                lax.all_gather(w_down, "shard", axis=0, tiled=True),
                lax.all_gather(bias_down, "shard", axis=0, tiled=True),
                lax.all_gather(gain_ffn, "shard", axis=0, tiled=True),
                lax.all_gather(shift_ffn, "shard", axis=0, tiled=True),
            )
        )
        (
            qkv_weight,
            query_bias,
            value_bias,
            out_weight,
            out_bias,
            gain_one,
            shift_one,
            up_weight,
            up_bias,
            down_weight,
            down_bias,
            gain_two,
            shift_two,
        ) = weights_full
        seq_in = tokens[batch_idx]
        seq_len = lengths[batch_idx]
        key_mask = key_place < seq_len
        own_valid = row_place < seq_len
        row_mask = own_valid.astype(jnp.float32)[:, None]
        qkv_bias = jnp.concatenate([query_bias, jnp.zeros_like(query_bias), value_bias])
        qkv_low = (
            jnp.dot(seq_in, qkv_weight, preferred_element_type=jnp.float32) + qkv_bias
        ).astype(jnp.bfloat16)
        queries = qkv_low[:, :width]
        key_part = qkv_low[:, width : 2 * width]
        value_part = qkv_low[:, 2 * width :]
        keys_all, values_all = (
            lax.all_gather(key_part, "shard", axis=0, tiled=True),
            lax.all_gather(value_part, "shard", axis=0, tiled=True),
        )
        context, lse_rows = attend_forward(queries, keys_all, values_all, key_mask)
        context_low = context.astype(jnp.bfloat16)
        attn_out = jnp.dot(context_low, out_weight, preferred_element_type=jnp.float32) + out_bias
        hidden, norm_one_back = jax.vjp(
            layer_norm, seq_in.astype(jnp.float32) + attn_out, gain_one, shift_one
        )
        hidden_low = hidden.astype(jnp.bfloat16)
        up_proj = jnp.dot(hidden_low, up_weight, preferred_element_type=jnp.float32) + up_bias
        activation, gelu_back = jax.vjp(gelu_exact, up_proj)
        act_low = activation.astype(jnp.bfloat16)
        ffn_out = jnp.dot(act_low, down_weight, preferred_element_type=jnp.float32) + down_bias
        normed, norm_two_back = jax.vjp(layer_norm, hidden + ffn_out, gain_two, shift_two)
        layer_rows.append((normed * row_mask).astype(jnp.bfloat16))
        weights_full = unpack(
            (
                lax.all_gather(w_qkv, "shard", axis=0, tiled=True),
                lax.all_gather(bias_q, "shard", axis=0, tiled=True),
                lax.all_gather(bias_v, "shard", axis=0, tiled=True),
                lax.all_gather(w_out, "shard", axis=0, tiled=True),
                lax.all_gather(bias_out, "shard", axis=0, tiled=True),
                lax.all_gather(gain_attn, "shard", axis=0, tiled=True),
                lax.all_gather(shift_attn, "shard", axis=0, tiled=True),
                lax.all_gather(w_up, "shard", axis=0, tiled=True),
                lax.all_gather(bias_up, "shard", axis=0, tiled=True),
                lax.all_gather(w_down, "shard", axis=0, tiled=True),
                lax.all_gather(bias_down, "shard", axis=0, tiled=True),
                lax.all_gather(gain_ffn, "shard", axis=0, tiled=True),
                lax.all_gather(shift_ffn, "shard", axis=0, tiled=True),
            )
        )
        (
            qkv_weight,
            query_bias,
            value_bias,
            out_weight,
            out_bias,
            gain_one,
            shift_one,
            up_weight,
            up_bias,
            down_weight,
            down_bias,
            gain_two,
            shift_two,
        ) = weights_full
        grad_out = cotangent[batch_idx].astype(jnp.float32) * row_mask
        grad_res_two, grad_gain_two, grad_shift_two = norm_two_back(grad_out)
        grad_ffn_low = grad_res_two.astype(jnp.bfloat16)
        grad_act = contract_cols(grad_ffn_low, down_weight)
        (grad_up,) = gelu_back(grad_act)
        grad_up_low = grad_up.astype(jnp.bfloat16)
        grad_hidden = grad_res_two + contract_cols(grad_up_low, up_weight)
        grad_res_one, grad_gain_one, grad_shift_one = norm_one_back(grad_hidden)
        grad_attn_low = grad_res_one.astype(jnp.bfloat16)
        grad_ctx_low = contract_cols(grad_attn_low, out_weight).astype(jnp.bfloat16)
        keys_all, values_all = (
            lax.all_gather(key_part, "shard", axis=0, tiled=True),
            lax.all_gather(value_part, "shard", axis=0, tiled=True),
        )
        grad_q, grad_keys_all, grad_values_all = attend_backward(
            queries, keys_all, values_all, key_mask, lse_rows, grad_ctx_low
        )
        grad_keys, grad_values = (
            lax.psum_scatter(
                grad_keys_all.astype(jnp.bfloat16), "shard", scatter_dimension=0, tiled=True
            ).astype(jnp.float32),
            lax.psum_scatter(
                grad_values_all.astype(jnp.bfloat16), "shard", scatter_dimension=0, tiled=True
            ).astype(jnp.float32),
        )
        grad_qkv_low = jnp.concatenate([grad_q, grad_keys, grad_values], axis=1).astype(
            jnp.bfloat16
        )
        grad_input = grad_res_one + contract_cols(grad_qkv_low, qkv_weight)
        grad_rows.append(grad_input.astype(jnp.bfloat16))
        terms = (
            contract_rows(seq_in, grad_qkv_low),
            column_sums(grad_qkv_low[:, :width]),
            column_sums(grad_qkv_low[:, 2 * width :]),
            contract_rows(context_low, grad_attn_low),
            column_sums(grad_attn_low),
            grad_gain_one,
            grad_shift_one,
            contract_rows(hidden_low, grad_up_low),
            column_sums(grad_up_low),
            contract_rows(act_low, grad_ffn_low),
            column_sums(grad_ffn_low),
            grad_gain_two,
            grad_shift_two,
        )
        totals = [running + fresh for running, fresh in zip(totals, terms)]
    grad_local = (
        lax.psum_scatter(
            totals[0].astype(jnp.bfloat16), "shard", scatter_dimension=0, tiled=True
        ).astype(jnp.float32),
        lax.psum_scatter(
            totals[1].astype(jnp.bfloat16), "shard", scatter_dimension=0, tiled=True
        ).astype(jnp.float32),
        lax.psum_scatter(
            totals[2].astype(jnp.bfloat16), "shard", scatter_dimension=0, tiled=True
        ).astype(jnp.float32),
        lax.psum_scatter(
            totals[3].astype(jnp.bfloat16), "shard", scatter_dimension=0, tiled=True
        ).astype(jnp.float32),
        lax.psum_scatter(
            totals[4].astype(jnp.bfloat16), "shard", scatter_dimension=0, tiled=True
        ).astype(jnp.float32),
        lax.psum_scatter(
            totals[5].astype(jnp.bfloat16), "shard", scatter_dimension=0, tiled=True
        ).astype(jnp.float32),
        lax.psum_scatter(
            totals[6].astype(jnp.bfloat16), "shard", scatter_dimension=0, tiled=True
        ).astype(jnp.float32),
        lax.psum_scatter(
            totals[7].astype(jnp.bfloat16), "shard", scatter_dimension=0, tiled=True
        ).astype(jnp.float32),
        lax.psum_scatter(
            totals[8].astype(jnp.bfloat16), "shard", scatter_dimension=0, tiled=True
        ).astype(jnp.float32),
        lax.psum_scatter(
            totals[9].astype(jnp.bfloat16), "shard", scatter_dimension=0, tiled=True
        ).astype(jnp.float32),
        lax.psum_scatter(
            totals[10].astype(jnp.bfloat16), "shard", scatter_dimension=0, tiled=True
        ).astype(jnp.float32),
        lax.psum_scatter(
            totals[11].astype(jnp.bfloat16), "shard", scatter_dimension=0, tiled=True
        ).astype(jnp.float32),
        lax.psum_scatter(
            totals[12].astype(jnp.bfloat16), "shard", scatter_dimension=0, tiled=True
        ).astype(jnp.float32),
    )
    grad_total = (
        lax.psum(grad_local[0].astype(jnp.bfloat16), "grp").astype(jnp.float32),
        lax.psum(grad_local[1].astype(jnp.bfloat16), "grp").astype(jnp.float32),
        lax.psum(grad_local[2].astype(jnp.bfloat16), "grp").astype(jnp.float32),
        lax.psum(grad_local[3].astype(jnp.bfloat16), "grp").astype(jnp.float32),
        lax.psum(grad_local[4].astype(jnp.bfloat16), "grp").astype(jnp.float32),
        lax.psum(grad_local[5].astype(jnp.bfloat16), "grp").astype(jnp.float32),
        lax.psum(grad_local[6].astype(jnp.bfloat16), "grp").astype(jnp.float32),
        lax.psum(grad_local[7].astype(jnp.bfloat16), "grp").astype(jnp.float32),
        lax.psum(grad_local[8].astype(jnp.bfloat16), "grp").astype(jnp.float32),
        lax.psum(grad_local[9].astype(jnp.bfloat16), "grp").astype(jnp.float32),
        lax.psum(grad_local[10].astype(jnp.bfloat16), "grp").astype(jnp.float32),
        lax.psum(grad_local[11].astype(jnp.bfloat16), "grp").astype(jnp.float32),
        lax.psum(grad_local[12].astype(jnp.bfloat16), "grp").astype(jnp.float32),
    )
    return (
        jnp.stack(layer_rows),
        jnp.stack(grad_rows),
        grad_total[0],
        grad_total[1],
        grad_total[2],
        grad_total[3],
        grad_total[4],
        grad_total[5],
        grad_total[6],
        grad_total[7],
        grad_total[8],
        grad_total[9],
        grad_total[10],
        grad_total[11],
        grad_total[12],
    )


BF = jnp.bfloat16
GRANT = 60 << 20
COST = pl.CostEstimate(flops=1024, bytes_accessed=1024, transcendentals=0)
F32 = jnp.float32


def swap_core(value):
    return lax.ppermute(value, "grp", [(i, i ^ 1) for i in range(8)])


def swap_x(value):
    return lax.ppermute(value, "grp", [(i, i ^ 2) for i in range(8)])


def swap_y(value):
    return lax.ppermute(value, "grp", [(i, i ^ 4) for i in range(8)])


def swap_z(value, flip):
    return lax.ppermute(value, "shard", [(i, i ^ flip) for i in range(4)])


def swap_xy(value):
    return lax.ppermute(value, "grp", [(i, i ^ 6) for i in range(8)])


def dot32(left_mat, right_mat):
    return jnp.dot(left_mat, right_mat, preferred_element_type=F32)


def after(values, *others):
    return lax.optimization_barrier((values, others))[0]


def sequence_perm(flip):
    pairs = []
    for grp in range(8):
        for line in range(4):
            dst_grp = (grp & 6) | (line // 2)
            dst_line = 2 * (grp & 1) + ((line % 2) ^ flip)
            pairs.append((grp * 4 + line, dst_grp * 4 + dst_line))
    return pairs


def send_first(block):
    return lax.ppermute(block, ("grp", "shard"), sequence_perm(0))


def send_second(block):
    return lax.ppermute(block, ("grp", "shard"), sequence_perm(1))


def send_rows(first, second):
    return send_first(first), send_second(second)


def return_rows(first, second):
    back = lambda flip: [(dst, src) for src, dst in sequence_perm(flip)]
    first = lax.ppermute(first, ("grp", "shard"), back(0))
    second = lax.ppermute(second, ("grp", "shard"), back(1))
    return first, second


def join_rows(first, second, parity):
    return jnp.where(parity == 0, jnp.stack([first, second]), jnp.stack([second, first]))


CORE, PLANE, LINE, PARITY = range(4)


def start_moves(moves, where_ref, sources, targets, sems):
    where = [where_ref[idx] for idx in range(4)]
    place = lambda at, unit: at if isinstance(at, int) else pl.multiple_of(at(*where), unit)
    copies = []
    for idx, (src, src_row, src_col, rows, cols, dst, dst_row, dst_col) in enumerate(moves):
        copies.append(
            pltpu.make_async_copy(
                sources[src].at[pl.ds(place(src_row, 8), rows), pl.ds(place(src_col, 128), cols)],
                targets[dst].at[pl.ds(place(dst_row, 8), rows), pl.ds(place(dst_col, 128), cols)],
                sems.at[idx],
            )
        )
    for copy in copies:
        copy.start()
    return copies


def move_kernel(count, moves, where_ref, *refs):
    for copy in start_moves(moves, where_ref, refs[:count], refs[count:-1], refs[-1]):
        copy.wait()


def move_blocks(where, sources, moves, shapes, grant=16 << 20):
    moved = sum(move[3] * move[4] for move in moves) * 2
    return pl.pallas_call(
        functools.partial(move_kernel, len(sources), moves),
        out_shape=[jax.ShapeDtypeStruct(shape, sources[0].dtype) for shape in shapes],
        in_specs=[pl.BlockSpec(memory_space=pltpu.SMEM)]
        + [pl.BlockSpec(memory_space=pl.ANY)] * len(sources),
        out_specs=[pl.BlockSpec(memory_space=pltpu.VMEM)] * len(shapes),
        scratch_shapes=[pltpu.SemaphoreType.DMA((len(moves),))],
        cost_estimate=COST,
        compiler_params=pltpu.CompilerParams(vmem_limit_bytes=grant),
    )(where, *sources)


def join_blocks(where, parts):
    moves, at = [], 0
    for idx, part in enumerate(parts):
        moves.append((idx, 0, 0, part.shape[0], part.shape[1], 0, at, 0))
        at += part.shape[0]
    return move_blocks(where, list(parts), moves, [(at, parts[0].shape[1])])[0]


def along_line(piece):
    return [swap_z(piece, flip) for flip in (1, 2, 3)]


def across_plane(came):
    return [swap_x(came), swap_y(came), swap_xy(came)]


def placed_moves(first_src, height, piece_rows, col, cols, dst):
    moves = []
    for flip in range(4):
        for step in range(1, 4):
            at = lambda core, plane, line, parity, flip=flip, step=step: (
                (line ^ step) * (4 * piece_rows) + (plane ^ flip) * piece_rows
            )
            moves.append((first_src + flip, (step - 1) * height, col, piece_rows, cols, dst, at, 0))
    return moves


def pick(arr, idx, axis):
    return lax.dynamic_index_in_dim(arr, idx, axis, keepdims=False)


def add_low(left, right):
    return (left.astype(F32) + right.astype(F32)).astype(BF)


def reduce_first(grads, cut, col, row, small=None):
    join = lambda arrs: arrs[0] if len(arrs) == 1 else jnp.concatenate(arrs, axis=-1)
    below = lambda arr, idx, axis: arr if small is None else jnp.concatenate([arr, pick(small, idx, axis)], axis=-2)
    low_part = lambda idx: join([pick(grad[:, :, :, :cut], idx, 2) for grad in grads])
    high_part = lambda idx: below(join([pick(grad[:, :, :, cut:], idx, 1) for grad in grads]), idx, 1)
    sent = (low_part(1 - col), high_part(1 - row))
    return (low_part(col), high_part(row), swap_x(sent[0]), swap_y(sent[1])), sent


def reduce_second(state, col, row):
    low, high, low_got, high_got = state
    low, high = add_low(low, low_got), add_low(high, high_got)
    sent = (pick(low, 1 - row, 1), pick(high, 1 - col, 1))
    return (pick(low, row, 1), pick(high, col, 1), swap_y(sent[0]), swap_x(sent[1])), sent


def reduce_near(state, line):
    low, high, low_got, high_got = state
    mine = jnp.concatenate([add_low(low, low_got), add_low(high, high_got)], axis=1)
    pairs = mine.reshape((2, 2) + mine.shape[1:])
    sent = pick(pairs, 1 - line % 2, 1)
    return (pick(pairs, line % 2, 1), swap_z(sent, 1)), sent


def reduce_far(state, line):
    mine = add_low(*state)
    sent = pick(mine, 1 - line // 2, 0)
    return (pick(mine, line // 2, 0), swap_z(sent, 2)), sent


def blocks_kernel(where_ref, grad_ref, small_ref, *refs):
    outs, sem = refs[:-1], refs[-1]
    plane = where_ref[PLANE]
    rows = grad_ref.shape[2]
    copies = [
        pltpu.make_async_copy(grad_ref.at[idx, plane ^ flip], out.at[idx, pl.ds(0, rows)], sem.at[flip, idx])
        for flip, out in enumerate(outs)
        for idx in range(4)
    ]
    for copy in copies:
        copy.start()
    small = small_ref[...]
    for flip, out in enumerate(outs):
        out[:, pl.ds(rows, small.shape[1]), :] = jnp.where(plane == flip, small, jnp.zeros_like(small))
    for copy in copies:
        copy.wait()


def direct_plane(where, grad, small):
    shape = (4, grad.shape[2] + small.shape[1], grad.shape[3])
    vmem = pl.BlockSpec(memory_space=pltpu.VMEM)
    blocks = pl.pallas_call(
        blocks_kernel,
        out_shape=[jax.ShapeDtypeStruct(shape, BF)] * 4,
        in_specs=[pl.BlockSpec(memory_space=pltpu.SMEM), pl.BlockSpec(memory_space=pl.ANY), vmem],
        out_specs=[vmem] * 4,
        scratch_shapes=[pltpu.SemaphoreType.DMA((4, 4))],
        cost_estimate=COST,
        compiler_params=pltpu.CompilerParams(vmem_limit_bytes=16 << 20),
    )(where, grad, small)
    got = [swap_x(blocks[1]), swap_y(blocks[2]), swap_xy(blocks[3])]
    return [blocks[0]] + got, blocks[1:]


def line_near(state, line):
    mine = sum(part.astype(F32) for part in state).astype(BF)
    pairs = mine.reshape((2, 2) + mine.shape[1:])
    sent = pick(pairs, 1 - line % 2, 1)
    return (pick(pairs, line % 2, 1), swap_z(sent, 1)), sent


def direct_line(state, line):
    mine = sum(part.astype(F32) for part in state).astype(BF)
    sent = [pick(mine, line ^ flip, 0) for flip in range(4)]
    return [sent[0]] + [swap_z(sent[flip], flip) for flip in (1, 2, 3)], sent


def direct_spread(state):
    piece = sum(part.astype(F32) for part in state).astype(BF)
    return [piece] + across_plane(piece), piece


def final_kernel(layout, rows, extra, flips, where_ref, mine_ref, other_ref, *outs):
    plane = where_ref[PLANE]
    height = mine_ref.shape[0] // 4

    def put(core):
        for source, half in ((mine_ref, core), (other_ref, 1 - core)):
            for at in range(4):
                part = plane ^ flips[at]
                for src_col, cols, dst, row_of, dst_col in layout(half):
                    row = pl.multiple_of(row_of(part), 16)
                    outs[dst][pl.ds(row, rows), pl.ds(dst_col, cols)] = source[
                        pl.ds(at * height, rows), pl.ds(src_col, cols)
                    ].astype(F32)

    for core in range(2):
        pl.when(where_ref[CORE] == core)(functools.partial(put, core))
    if extra:
        outs[-1][...] = jnp.zeros_like(outs[-1])
        for at in range(4):

            @pl.when(plane == flips[at])
            def _(at=at):
                here = pl.ds(at * height + rows, extra)
                outs[-1][...] = mine_ref[here, :].astype(F32) + other_ref[here, :].astype(F32)


def spread_first(state, through_x):
    piece = add_low(*state)
    return piece, (swap_x if through_x else swap_y)(piece)


def spread_second(state, through_x):
    both = jnp.concatenate(state, axis=0)
    return both, (swap_y if through_x else swap_x)(both)


def spread_core(state):
    mine = jnp.concatenate(state, axis=0)
    return mine, swap_core(mine)


def finish_grad(where, state, through_x, layout, rows, shapes, extra=0):
    mine, other = state
    mine_flips = (0, 1, 2, 3) if through_x else (0, 2, 1, 3)
    shapes = list(shapes) + ([(extra, mine.shape[1])] if extra else [])
    vmem = pl.BlockSpec(memory_space=pltpu.VMEM)
    return pl.pallas_call(
        functools.partial(final_kernel, layout, rows, extra, mine_flips),
        out_shape=[jax.ShapeDtypeStruct(shape, F32) for shape in shapes],
        in_specs=[pl.BlockSpec(memory_space=pltpu.SMEM), vmem, vmem],
        out_specs=[vmem] * len(shapes),
        cost_estimate=COST,
        compiler_params=pltpu.CompilerParams(vmem_limit_bytes=16 << 20),
    )(where, mine, other)


ROWS = 256


def row_spec(width, shift=0, steps=1):
    if shift:
        return pl.BlockSpec((ROWS, width), lambda blk: ((blk + shift) % steps, 0))
    return pl.BlockSpec((ROWS, width), lambda blk: (blk, 0))


def whole_spec(rows, width):
    return pl.BlockSpec((rows, width), lambda blk: (0, 0))


def mean_last(values):
    return jnp.mean(values, axis=-1, keepdims=True)


def norm_parts(values):
    centered = values - mean_last(values)
    scale = lax.rsqrt(mean_last(centered * centered) + eps)
    return centered * scale, scale


def norm_back(grad_normed, normed, scale):
    return scale * (grad_normed - mean_last(grad_normed) - normed * mean_last(grad_normed * normed))


def up_kernel(part_ref, got_ref, tok_ref, vec_ref, bias_ref, w_ref, low_ref, n_ref, r_ref, act_ref, slope_ref):
    vec = vec_ref[...]
    attn_out = part_ref[...].astype(F32) + got_ref[...].astype(F32) + vec[0:1]
    normed, scale = norm_parts(tok_ref[...].astype(F32) + attn_out)
    hidden = (normed * vec[1:2] + vec[2:3]).astype(BF)
    n_ref[...] = normed
    r_ref[...] = jnp.broadcast_to(scale, r_ref.shape)
    low_ref[...] = hidden
    for at in range(0, w_ref.shape[1], 384):
        cols = pl.ds(at, 384)
        up = dot32(hidden, w_ref[:, cols]) + bias_ref[:, cols]
        cdf = 0.5 + 0.5 * lax.erf(up * 0.5**0.5)
        act_ref[:, cols] = (up * cdf).astype(BF)
        slope = cdf + up * (jnp.exp(up * up * -0.5) * (2 * math.pi) ** -0.5)
        slope_ref[:, cols] = slope.astype(BF)


def ffn_up(part, got, tokens, vectors, up_bias, weight):
    rows, width = part.shape
    units = weight.shape[1]
    steps = rows // ROWS
    return pl.pallas_call(
        up_kernel,
        grid=(steps,),
        out_shape=[
            jax.ShapeDtypeStruct((rows, width), BF),
            jax.ShapeDtypeStruct((rows, width), F32),
            jax.ShapeDtypeStruct((rows, 128), F32),
            jax.ShapeDtypeStruct((rows, units), BF),
            jax.ShapeDtypeStruct((rows, units), BF),
        ],
        in_specs=[
            row_spec(width),
            row_spec(width, steps // 2, steps),
            row_spec(width),
            whole_spec(8, width),
            whole_spec(1, units),
            whole_spec(width, units),
        ],
        out_specs=[row_spec(width), row_spec(width), row_spec(128), row_spec(units), row_spec(units)],
        cost_estimate=COST,
        compiler_params=pltpu.CompilerParams(vmem_limit_bytes=20 << 20),
    )(part, got, tokens, vectors, up_bias, weight)


def turn_kernel(
    half_steps, part_ref, got_ref, n_ref, cot_ref, bias_ref, vec_ref, first_ref, second_ref, dr_ref, low_ref, sum_ref
):
    blk = pl.program_id(0)
    vec = vec_ref[...]
    hidden = n_ref[...] * vec[1:2] + vec[2:3]
    ffn_out = part_ref[...].astype(F32) + got_ref[...].astype(F32) + vec[3:4]
    normed, scale = norm_parts(hidden + ffn_out)
    mask = jnp.where(bias_ref[:, 0:1] < 0.0, 0.0, 1.0)
    result = ((normed * vec[4:5] + vec[5:6]) * mask).astype(BF)
    dy = cot_ref[...].astype(F32) * mask
    dr = norm_back(dy * vec[4:5], normed, scale)
    dr_low = dr.astype(BF)
    dr_ref[...] = dr
    low_ref[...] = dr_low

    @pl.when(blk == 0)
    def _():
        sum_ref[...] = jnp.zeros_like(sum_ref)
        first_ref[...] = result

    @pl.when(blk == 1)
    def _():
        second_ref[...] = result

    @pl.when(blk < half_steps)
    def _():
        sum_ref[0:1] += jnp.sum(dy * normed, axis=0, keepdims=True)
        sum_ref[1:2] += jnp.sum(dy, axis=0, keepdims=True)
        sum_ref[2:3] += jnp.sum(dr_low.astype(F32), axis=0, keepdims=True)


def norm_turn(part, got, n_one, cot, bias, vectors):
    rows, width = part.shape
    steps = rows // ROWS
    return pl.pallas_call(
        functools.partial(turn_kernel, steps // 2),
        grid=(steps,),
        out_shape=[jax.ShapeDtypeStruct((ROWS, width), BF)] * 2
        + [
            jax.ShapeDtypeStruct((rows, width), F32),
            jax.ShapeDtypeStruct((rows, width), BF),
            jax.ShapeDtypeStruct((8, width), F32),
        ],
        in_specs=[
            row_spec(width),
            row_spec(width, steps // 2, steps),
            row_spec(width),
            row_spec(width),
            row_spec(128),
            whole_spec(8, width),
        ],
        out_specs=[whole_spec(ROWS, width)] * 2 + [row_spec(width), row_spec(width), whole_spec(8, width)],
        cost_estimate=COST,
        compiler_params=pltpu.CompilerParams(vmem_limit_bytes=28 << 20),
    )(part, got, n_one, cot, bias, vectors)


def back_kernel(
    half_steps, where_ref, dr_ref, part_ref, got_ref, n_ref, r_ref, vec_ref, own_ref, low_ref, part_low_ref, sum_ref
):
    blk = pl.program_id(0)
    vec = vec_ref[...]
    normed = n_ref[...]
    dhidden = dr_ref[...] + (part_ref[...].astype(F32) + got_ref[...].astype(F32))
    dr = norm_back(dhidden * vec[1:2], normed, r_ref[:, 0:1])
    dr_low = dr.astype(BF)
    low_ref[...] = dr_low
    half = dr.shape[1] // 2
    part_low_ref[...] = jnp.where(where_ref[CORE] == 0, dr_low[:, :half], dr_low[:, half:])

    @pl.when(blk == 0)
    def _():
        sum_ref[...] = jnp.zeros_like(sum_ref)

    @pl.when(blk < half_steps)
    def _():
        own_ref[...] = dr
        sum_ref[0:1] += jnp.sum(dhidden * normed, axis=0, keepdims=True)
        sum_ref[1:2] += jnp.sum(dhidden, axis=0, keepdims=True)
        sum_ref[2:3] += jnp.sum(dr_low.astype(F32), axis=0, keepdims=True)


def norm_one_back(where, dr_two, part, got, n_one, r_one, vectors):
    rows, width = part.shape
    steps = rows // ROWS
    return pl.pallas_call(
        functools.partial(back_kernel, steps // 2),
        grid=(steps,),
        out_shape=[
            jax.ShapeDtypeStruct((rows // 2, width), F32),
            jax.ShapeDtypeStruct((rows, width), BF),
            jax.ShapeDtypeStruct((rows, width // 2), BF),
            jax.ShapeDtypeStruct((8, width), F32),
        ],
        in_specs=[
            pl.BlockSpec(memory_space=pltpu.SMEM),
            row_spec(width),
            row_spec(width),
            row_spec(width, steps // 2, steps),
            row_spec(width),
            row_spec(128),
            whole_spec(8, width),
        ],
        out_specs=[
            pl.BlockSpec((ROWS, width), lambda blk: (jnp.minimum(blk, steps // 2 - 1), 0)),
            row_spec(width),
            row_spec(width // 2),
            whole_spec(8, width),
        ],
        cost_estimate=COST,
        compiler_params=pltpu.CompilerParams(vmem_limit_bytes=28 << 20),
    )(where, dr_two, part, got, n_one, r_one, vectors)


Q_BLOCK = 256
PAIR = 128


def contract_last(left_mat, right_mat):
    return lax.dot_general(
        left_mat, right_mat, (((1,), (1,)), ((), ())), preferred_element_type=F32
    )


def head_lanes(block, head):
    lane = lax.broadcasted_iota(jnp.int32, block.shape, 1)
    return jnp.where((lane // HD) == head, block, jnp.zeros_like(block))


def attend_fwd_kernel(q_ref, k_ref, v_ref, bias_ref, ctx_ref, lse_ref, vt_ref):
    vt_ref[...] = v_ref[...].T

    @pl.loop(0, q_ref.shape[0] // Q_BLOCK)
    def _(blk):
        at = pl.multiple_of(blk * Q_BLOCK, Q_BLOCK)
        q_blk = q_ref[pl.ds(at, Q_BLOCK), :] * jnp.asarray(HD ** (-0.5), BF)
        outs = []
        for head in range(2):
            scores = contract_last(k_ref[...], head_lanes(q_blk, head))
            scores = scores + jnp.concatenate([bias_ref[...]] * (Q_BLOCK // 128), axis=1)
            top = jnp.max(scores, axis=0, keepdims=True)
            exps = jnp.exp(scores - top)
            total = jnp.sum(exps, axis=0, keepdims=True)
            out = dot32(vt_ref[pl.ds(head * HD, HD), :], exps.astype(BF))
            outs.append(out * (1.0 / total))
            lse_ref[0, pl.ds(head, 1), pl.ds(at, Q_BLOCK)] = top + jnp.log(total)
        ctx_ref[pl.ds(at, Q_BLOCK), :] = jnp.concatenate(outs, axis=0).T.astype(BF)


def attend_bwd_kernel(
    q_ref, k_ref, v_ref, bias_ref, lse_ref, grad_ref, dq_ref, dk_ref, dv_ref, kt_ref, dk_acc, dv_acc
):
    kt_ref[...] = k_ref[...].T
    dk_acc[...] = jnp.zeros_like(dk_acc)
    dv_acc[...] = jnp.zeros_like(dv_acc)

    @pl.loop(0, q_ref.shape[0] // Q_BLOCK)
    def _(blk):
        at = pl.multiple_of(blk * Q_BLOCK, Q_BLOCK)
        q_blk = q_ref[pl.ds(at, Q_BLOCK), :] * jnp.asarray(HD ** (-0.5), BF)
        grad_blk = grad_ref[pl.ds(at, Q_BLOCK), :]
        outs = []
        for head in range(2):
            q_head = head_lanes(q_blk, head)
            grad_head = head_lanes(grad_blk, head)
            scores = contract_last(k_ref[...], q_head)
            scores = scores + jnp.concatenate([bias_ref[...]] * (Q_BLOCK // 128), axis=1)
            probs = jnp.exp(scores - lse_ref[0, pl.ds(head, 1), pl.ds(at, Q_BLOCK)])
            weighed = probs * contract_last(v_ref[...], grad_head)
            delta = jnp.sum(weighed, axis=0, keepdims=True)
            grad_scores = (weighed - probs * delta).astype(BF)
            dk_acc[...] += dot32(grad_scores, q_head)
            dv_acc[...] += dot32(probs.astype(BF), grad_head)
            outs.append(dot32(kt_ref[pl.ds(head * HD, HD), :], grad_scores))
        dq = jnp.concatenate(outs, axis=0).T * (HD ** (-0.5))
        dq_ref[pl.ds(at, Q_BLOCK), :] = dq.astype(BF)

    dk_ref[...] = dk_acc[...].astype(BF)
    dv_ref[...] = dv_acc[...].astype(BF)


def column_spec(rows, first):
    return pl.BlockSpec((rows, PAIR), lambda pair: (0, first + pair))


def attend_chip_forward(qkv, bias, pair):
    rows, half = qkv.shape[0], qkv.shape[1] // 3
    pairs = half // PAIR
    return pl.pallas_call(
        attend_fwd_kernel,
        grid=(1,),
        out_shape=[
            jax.ShapeDtypeStruct((rows, PAIR), BF),
            jax.ShapeDtypeStruct((1, 2, rows), F32),
        ],
        in_specs=[column_spec(rows, idx * pairs + pair) for idx in range(3)]
        + [pl.BlockSpec((rows, 128), lambda step: (0, 0))],
        out_specs=[column_spec(rows, 0), pl.BlockSpec((1, 2, rows), lambda step: (0, 0, 0))],
        scratch_shapes=[pltpu.VMEM((PAIR, rows), BF)],
        cost_estimate=COST,
        compiler_params=pltpu.CompilerParams(vmem_limit_bytes=20 << 20),
    )(qkv, qkv, qkv, bias)


def attend_chip_backward(qkv, bias, lse, grad_ctx, pair):
    rows, half = qkv.shape[0], qkv.shape[1] // 3
    pairs = half // PAIR
    return pl.pallas_call(
        attend_bwd_kernel,
        grid=(1,),
        out_shape=[jax.ShapeDtypeStruct((rows, PAIR), BF)] * 3,
        in_specs=[column_spec(rows, idx * pairs + pair) for idx in range(3)]
        + [
            pl.BlockSpec((rows, 128), lambda step: (0, 0)),
            pl.BlockSpec((1, 2, rows), lambda step: (0, 0, 0)),
            column_spec(rows, pair),
        ],
        out_specs=[column_spec(rows, 0)] * 3,
        scratch_shapes=[
            pltpu.VMEM((PAIR, rows), BF),
            pltpu.VMEM((rows, PAIR), F32),
            pltpu.VMEM((rows, PAIR), F32),
        ],
        cost_estimate=COST,
        compiler_params=pltpu.CompilerParams(vmem_limit_bytes=24 << 20),
    )(qkv, qkv, qkv, bias, lse, grad_ctx)


def pack_kernel(count, moves, vec_at, slab, where_ref, *refs):
    sources, vecs = refs[:count], refs[count : count + 9]
    targets, sems = refs[count + 9 : -1], refs[-1]
    copies = start_moves(moves, where_ref, sources, targets, sems)
    dst, row = vec_at
    width = targets[dst].shape[1]
    rows = [vec[...].reshape(1, slab).astype(F32) for vec in vecs[:8]]
    wide = vecs[8][...].reshape(1, -1).astype(F32)
    count_wide = wide.shape[1] // slab
    rows += [wide[:, :slab]]
    rows += [pltpu.roll(wide, wide.shape[1] - idx * slab, 1)[:, :slab] for idx in range(1, count_wide)]
    rows += [jnp.zeros((4, slab), F32)]
    block = jnp.concatenate(rows, axis=0)
    targets[dst][pl.ds(row, 16), :] = jnp.concatenate(
        [block, jnp.zeros((16, width - slab), F32)], axis=1
    ).astype(BF)
    for copy in copies:
        copy.wait()


def pack_blocks(where, sources, vecs, moves, shapes, vec_at, slab):
    return pl.pallas_call(
        functools.partial(pack_kernel, len(sources), moves, vec_at, slab),
        out_shape=[jax.ShapeDtypeStruct(shape, BF) for shape in shapes],
        in_specs=[pl.BlockSpec(memory_space=pltpu.SMEM)]
        + [pl.BlockSpec(memory_space=pl.ANY)] * len(sources)
        + [pl.BlockSpec(memory_space=pltpu.VMEM)] * len(vecs),
        out_specs=[pl.BlockSpec(memory_space=pltpu.VMEM)] * len(shapes),
        scratch_shapes=[pltpu.SemaphoreType.DMA((len(moves),))],
        cost_estimate=COST,
        compiler_params=pltpu.CompilerParams(vmem_limit_bytes=60 << 20),
    )(where, *sources, *vecs)


def vector_kernel(height, at, slab, where_ref, own_ref, came_ref, block_ref, qkv_ref, up_ref, buf, sems):
    line = where_ref[LINE]
    copies = [pltpu.make_async_copy(own_ref.at[pl.ds(at, 16)], buf.at[line], sems.at[0])]
    for step in range(1, 4):
        copies.append(
            pltpu.make_async_copy(
                came_ref.at[pl.ds((step - 1) * height + at, 16)], buf.at[line ^ step], sems.at[step]
            )
        )
    for copy in copies:
        copy.start()
    for copy in copies:
        copy.wait()
    width = block_ref.shape[1]
    half = width // 2
    joined = jnp.zeros((16, width), F32)
    lane = lax.broadcasted_iota(jnp.int32, (16, width), 1)
    wide = []
    for idx in range(4):
        rows = jnp.where(lane < slab, buf[idx, :, :width].astype(F32), 0.0)
        joined += rows if idx == 0 else pltpu.roll(rows, idx * slab, 1)
        row = rows[8:9]
        for part in range(1, 4):
            row += pltpu.roll(rows[8 + part : 9 + part], part * slab, 1)
        wide.append(row)
    low = where_ref[CORE] == 0
    pick_half = lambda row: jnp.where(low, row[:, :half], row[:, half:])
    block_ref[...] = jnp.concatenate([joined[2:8], jnp.zeros((2, width), F32)], axis=0)
    qkv_ref[...] = jnp.concatenate(
        [pick_half(joined[0:1]), jnp.zeros((1, half), F32), pick_half(joined[1:2])], axis=1
    )
    up_ref[...] = jnp.concatenate([pick_half(row) for row in wide], axis=1)


def join_vectors(where, own, came, at, slab, width):
    height = came.shape[0] // 3
    return pl.pallas_call(
        functools.partial(vector_kernel, height, at, slab),
        out_shape=[
            jax.ShapeDtypeStruct((8, width), F32),
            jax.ShapeDtypeStruct((1, 3 * width // 2), F32),
            jax.ShapeDtypeStruct((1, 2 * width), F32),
        ],
        in_specs=[pl.BlockSpec(memory_space=pltpu.SMEM)] + [pl.BlockSpec(memory_space=pl.ANY)] * 2,
        out_specs=[pl.BlockSpec(memory_space=pltpu.VMEM)] * 3,
        scratch_shapes=[pltpu.VMEM((4, 16, own.shape[1]), BF), pltpu.SemaphoreType.DMA((4,))],
        cost_estimate=COST,
        compiler_params=pltpu.CompilerParams(vmem_limit_bytes=4 << 20),
    )(where, own, came)


def small_kernel(slab, where_ref, one_ref, two_ref, up_ref, qkv_ref, out_ref):
    width = one_ref.shape[1]
    half = width // 2
    low = where_ref[CORE] == 0
    zero = jnp.zeros((1, half), F32)
    on_core = lambda row: jnp.where(
        low, jnp.concatenate([row, zero], axis=1), jnp.concatenate([zero, row], axis=1)
    )
    one, two = one_ref[...], two_ref[...]
    rows = jnp.concatenate(
        [
            on_core(qkv_ref[:, :half]),
            on_core(qkv_ref[:, 2 * half :]),
            one[2:3],
            one[0:1],
            one[1:2],
            two[2:3],
            two[0:1],
            two[1:2],
        ],
        axis=0,
    )
    out_ref[...] = jnp.zeros_like(out_ref)
    for idx in range(4):
        wide = on_core(up_ref[:, idx * half : (idx + 1) * half])
        at = lambda row, part: row if part == 0 else pltpu.roll(row, width - part * slab, 1)
        parts = [at(wide, part)[:, :slab] for part in range(4)]
        block = jnp.concatenate([at(rows, idx)[:, :slab]] + parts + [jnp.zeros((4, slab), F32)], axis=0)
        out_ref[idx, :, 0:slab] = block.astype(BF)


def small_grads(where, sums_one, sums_two, up_sums, qkv_sums, slab):
    vmem = pl.BlockSpec(memory_space=pltpu.VMEM)
    return pl.pallas_call(
        functools.partial(small_kernel, slab),
        out_shape=jax.ShapeDtypeStruct((4, 16, qkv_sums.shape[1]), BF),
        in_specs=[pl.BlockSpec(memory_space=pltpu.SMEM)] + [vmem] * 4,
        out_specs=vmem,
        compiler_params=pltpu.CompilerParams(vmem_limit_bytes=4 << 20),
    )(where, sums_one, sums_two, up_sums, qkv_sums)


def per_device_chip(
    tokens,
    cotangent,
    lengths,
    w_qkv,
    bias_q,
    bias_v,
    w_out,
    bias_out,
    gain_attn,
    shift_attn,
    w_up,
    bias_up,
    w_down,
    bias_down,
    gain_ffn,
    shift_ffn,
):
    quarter, width = tokens.shape[1:]
    half_rows = 2 * quarter
    units = w_up.shape[1] // 2
    slab = w_qkv.shape[0]
    wide = w_down.shape[0]
    half = width // 2
    slab_part, wide_part = slab // 4, wide // 8
    vec_rows = 16
    group = lax.axis_index("grp")
    line = lax.axis_index("shard")
    core = group % 2
    plane = group // 2
    col, row = plane % 2, plane // 2
    parity = line % 2
    where = jnp.stack([core, plane, line, parity]).astype(jnp.int32)

    vecs = [bias_q, bias_v, bias_out, gain_attn, shift_attn, bias_down, gain_ffn, shift_ffn, bias_up]
    moves = []
    slab_at = lambda c, p, z, e: p * slab_part
    for idx in range(3):
        at = lambda c, p, z, e, idx=idx: idx * width + c * half
        moves.append((0, slab_at, at, slab_part, half, 0, 0, idx * half))
    (qkv_piece,) = pack_blocks(
        where, [w_qkv], vecs, moves, [(slab_part + vec_rows, 3 * half)], (0, slab_part), slab
    )
    qkv_parts = along_line(qkv_piece)
    moves = []
    for idx in range(2):
        moves.append((idx, lambda c, p, z, e: e * quarter, 0, quarter, width, 2 * idx, 0, 0))
        moves.append((idx, lambda c, p, z, e: (1 - e) * quarter, 0, quarter, width, 2 * idx + 1, 0, 0))
    for idx in range(4):
        at = lambda c, p, z, e, idx=idx: idx * wide + c * (wide // 2)
        moves.append((2, slab_at, at, slab_part, wide // 2, 4, 0, idx * (wide // 2)))
    moves.append((3, slab_at, lambda c, p, z, e: c * half, slab_part, half, 4, 0, units))
    moves.append((4, lambda c, p, z, e: c * (wide // 2) + p * wide_part, 0, wide_part, width, 5, 0, 0))
    tok_first, tok_second, cot_first, cot_second, up_piece, down_piece = move_blocks(
        where,
        [after(tokens.reshape(half_rows, width), qkv_parts[0]), cotangent.reshape(half_rows, width), w_up, w_out, w_down],
        moves,
        [(quarter, width)] * 4 + [(slab_part, units + half), (wide_part, width)],
        grant=GRANT,
    )
    slab_start = lambda c, p, z, e: z * slab

    stack = lambda parts: join_blocks(where, parts)
    len_other = swap_core(lengths)
    len_all = jnp.where(core == 0, jnp.concatenate([lengths, len_other]), jnp.concatenate([len_other, lengths]))
    seq_len = len_all[line]
    place = lax.broadcasted_iota(jnp.int32, (4 * quarter, 128), 0)
    place = ((place // quarter) ^ (2 * core + parity)) * quarter + place % quarter
    bias = jnp.where(place < seq_len, 0.0, masked_score).astype(F32)
    tok_first, tok_second = send_rows(tok_first, tok_second)
    qkv_came = stack(after(qkv_parts, bias, down_piece))
    qkv_plane = across_plane(qkv_came)
    vec_block, qkv_bias, up_bias = join_vectors(where, qkv_piece, qkv_came, slab_part, slab, width)
    tok_own = stack(after([tok_first, tok_second], vec_block, *qkv_plane))
    up_parts = along_line(after(up_piece, tok_own))
    tok_all = stack([tok_own, swap_core(tok_own)])

    moves = []
    for idx in range(3):
        at = lambda c, p, z, e, idx=idx: idx * width + c * half
        moves.append((0, 0, at, slab, half, 0, slab_start, idx * half))
    moves += placed_moves(1, slab_part + vec_rows, slab_part, 0, 3 * half, 0)
    (qkv_weight,) = move_blocks(
        where, [w_qkv, after(qkv_came, vec_block)] + qkv_plane, moves, [(width, 3 * half)]
    )

    qkv = (dot32(tok_all, qkv_weight) + qkv_bias).astype(BF)
    pairs = half // PAIR
    contexts, lses = [], []
    for pair in range(pairs):
        qkv_in = after(qkv, contexts[-1]) if contexts else qkv
        if pair == 1:
            up_came = stack(after(up_parts, contexts[0]))
            up_plane = across_plane(up_came)
            down_far = swap_z(after(down_piece, up_came), 2)
            qkv_in = after(qkv, up_came)
        elif pair == 2:
            down_two = stack(after([down_piece, down_far], contexts[1]))
            down_near = swap_z(down_two, 1)
            cot_first = send_first(after(cot_first, down_two))
            qkv_in = after(qkv, down_two)
        got = attend_chip_forward(qkv_in, bias, pair)
        contexts.append(got[0])
        lses.append(got[1])
    context = jnp.concatenate(contexts, axis=1)
    down_near = after(down_near, context)
    down_came = stack([down_near[:wide_part], down_far, down_near[wide_part:]])
    cot_second = send_second(after(cot_second, down_came))

    moves = []
    for idx in range(4):
        at = lambda c, p, z, e, idx=idx: idx * wide + c * (wide // 2)
        moves.append((0, 0, at, slab, wide // 2, 0, slab_start, idx * (wide // 2)))
    moves.append((1, 0, lambda c, p, z, e: c * half, slab, half, 1, slab_start, 0))
    moves += placed_moves(2, slab_part, slab_part, 0, units, 0)
    moves += placed_moves(2, slab_part, slab_part, units, half, 1)
    up_weight, out_half = move_blocks(
        where,
        [w_up, w_out, after(up_came, down_came)] + up_plane,
        moves,
        [(width, units), (width, half)],
    )
    out_got = swap_core(out_half)
    down_plane = across_plane(after(down_came, out_half))
    moves = [
        (0, lambda c, p, z, e: c * half, 0, half, half, 0, 0, lambda c, p, z, e: c * half),
        (1, lambda c, p, z, e: c * half, 0, half, half, 0, 0, lambda c, p, z, e: (1 - c) * half),
    ]
    (out_weight,) = move_blocks(where, [out_half, out_got], moves, [(half, width)])
    part = dot32(context, out_weight).astype(BF)
    got = swap_core(part)
    cot_own = stack([cot_first, cot_second])
    hidden_low, n_one, r_one, act, slope = ffn_up(part, after(got, cot_own), tok_all, vec_block, up_bias, up_weight)

    moves = [(0, lambda c, p, z, e: c * (wide // 2), 0, wide // 2, width, 0, lambda c, p, z, e: z * (wide // 2), 0)]
    moves += placed_moves(1, wide_part, wide_part, 0, width, 0)
    (down_weight,) = move_blocks(where, [w_down, after(down_came, act)] + down_plane, moves, [(units, width)])
    part = dot32(act, down_weight).astype(BF)
    cot_all = stack([cot_own, swap_core(cot_own)])
    out_first, out_second, dr_two, dffn, sums_two = norm_turn(
        part, swap_core(part), n_one, cot_all, bias, vec_block
    )

    blocks = lambda grad: grad.reshape(4, 2, 2, grad.shape[0] // 16, grad.shape[1])
    g_down = contract_rows(act, dffn).astype(BF)
    down_state, sent = reduce_first([blocks(g_down)], wide_part // 2, col, row)
    dffn = after(dffn, sent)
    dup = (contract_cols(dffn, down_weight) * slope.astype(F32)).astype(BF)
    part = contract_cols(dup, up_weight).astype(BF)
    got = swap_core(part)
    dup_late = after(dup, part)
    g_up = contract_rows(hidden_low, dup_late).astype(BF)
    up_sums = jnp.sum(dup_late.astype(F32), axis=0, keepdims=True)
    dr_one, dattn, dattn_part, sums_one = norm_one_back(
        where, dr_two, part, after(got, g_up), n_one, r_one, vec_block
    )
    grad_ctx = contract_cols(dattn, out_weight).astype(BF)
    moves = [
        (0, 0, 0, 4 * quarter, half, 0, 0, lambda c, p, z, e: c * half),
        (1, 0, 0, half_rows, half, 0, half_rows, lambda c, p, z, e: (1 - c) * half),
        (1, half_rows, 0, half_rows, half, 0, 0, lambda c, p, z, e: (1 - c) * half),
    ]
    (context_all,) = move_blocks(
        where, [context, swap_core(after(context, dr_two))], moves, [(4 * quarter, width)]
    )
    g_out = contract_rows(context_all, after(dattn_part, grad_ctx)).astype(BF)
    down_state, sent = reduce_second(after(down_state, g_out), col, row)
    up_state, sent_up = reduce_first([blocks(g_up), blocks(after(g_out, sent))], slab_part // 2, col, row)

    layer_first, layer_second = return_rows(*after((out_first, out_second), g_down))
    layer_out = join_rows(*after((layer_first, layer_second), sent_up), parity)

    dqkv = []
    qkv_in = after(qkv, sent_up, layer_out)
    dqkv.append(attend_chip_backward(qkv_in, bias, lses[0], grad_ctx, 0))
    down_state, sent = reduce_near(after(down_state, dqkv[-1]), line)
    qkv_in = after(qkv, sent)
    dqkv.append(attend_chip_backward(qkv_in, bias, lses[1], grad_ctx, 1))
    up_state, sent_up = reduce_second(after(up_state, dqkv[-1]), col, row)
    down_state, sent = reduce_far(after(down_state, sent_up), line)
    qkv_in = after(qkv, sent)
    for pair in range(2, pairs):
        dqkv.append(attend_chip_backward(qkv_in, bias, lses[pair], grad_ctx, pair))
    down_state = spread_first(after(down_state, dqkv[-1]), True)
    up_state, sent_up = reduce_near(after(up_state, down_state[0]), line)
    dqkv = jnp.concatenate([part[idx] for idx in range(3) for part in dqkv], axis=1)
    dqkv = after(dqkv, sent_up)
    dtok_low = contract_cols(dqkv[half_rows:], qkv_weight).astype(BF)
    dtok_got = swap_core(dtok_low)
    grad_tok = contract_cols(after(dqkv[:half_rows], dtok_low), qkv_weight) + dr_one
    down_state = spread_second(after(down_state, grad_tok), True)
    dqkv = after(dqkv, down_state[0])
    qkv_sums = jnp.sum(dqkv.astype(F32), axis=0, keepdims=True)
    small = small_grads(where, sums_one, sums_two, up_sums, qkv_sums, slab)
    g_qkv = contract_rows(tok_all, dqkv).astype(BF).reshape(4, 4, slab_part, 3 * half)
    qkv_state, sent = direct_plane(where, g_qkv, small)
    grad_tok = (after(grad_tok, sent) + dtok_got.astype(F32)).astype(BF)
    up_state, sent_up = reduce_far(after(up_state, grad_tok), line)
    down_state = spread_core(after(down_state, sent_up))
    back_first, back_second = return_rows(*after((grad_tok[:quarter], grad_tok[quarter:]), down_state[0]))
    up_state = spread_first(after(up_state, down_state[0]), False)
    qkv_state, sent = line_near(after(qkv_state, up_state[0]), line)
    up_state = spread_second(after(up_state, sent), False)
    qkv_state, sent = reduce_far(after(qkv_state, up_state[0]), line)
    grad_tokens = join_rows(*after((back_first, back_second), sent), parity)
    up_state = spread_core(after(up_state, grad_tokens))
    qkv_state, sent = direct_spread(after(qkv_state, up_state[0]))
    qkv_state = spread_core(after(qkv_state, sent))

    down_layout = lambda half_at: [(0, width, 0, lambda part: half_at * (wide // 2) + part * wide_part, 0)]
    (grad_down,) = finish_grad(where, down_state, True, down_layout, wide_part, [(wide, width)])
    slab_row = lambda part: part * slab_part
    up_layout = lambda half_at: [
        (idx * (wide // 2), wide // 2, 0, slab_row, idx * wide + half_at * (wide // 2)) for idx in range(4)
    ] + [(units, half, 1, slab_row, half_at * half)]
    qkv_layout = lambda half_at: [
        (idx * half, half, 0, slab_row, idx * width + half_at * half) for idx in range(3)
    ]
    grad_qkv, small_sum = finish_grad(
        where, after(qkv_state, grad_down), True, qkv_layout, slab_part, [(slab, 3 * width)], extra=vec_rows
    )
    grad_up, grad_out = finish_grad(
        where, after(up_state, grad_qkv), False, up_layout, slab_part, [(slab, 2 * units), (slab, width)]
    )
    vec_of = lambda idx: small_sum[idx, :slab]
    return (
        layer_out,
        grad_tokens,
        grad_qkv,
        vec_of(0),
        vec_of(1),
        grad_out,
        vec_of(2),
        vec_of(3),
        vec_of(4),
        grad_up,
        small_sum[8 : 8 + wide // slab, :slab].reshape(wide),
        grad_down,
        vec_of(5),
        vec_of(6),
        vec_of(7),
    )


def solution(mesh):
    placed = (
        P("grp", "shard", None),
        P("grp", "shard", None),
        P("grp"),
        P("shard", None),
        P("shard"),
        P("shard"),
        P("shard", None),
        P("shard"),
        P("shard"),
        P("shard"),
        P("shard", None),
        P("shard"),
        P("shard", None),
        P("shard"),
        P("shard"),
        P("shard"),
    )
    plan = per_device_chip if dict(mesh.shape) == {"grp": 8, "shard": 4} else per_device
    return jax.shard_map(
        plan,
        mesh=mesh,
        in_specs=placed,
        out_specs=(
            P("grp", "shard", None),
            P("grp", "shard", None),
            P("shard", None),
            P("shard"),
            P("shard"),
            P("shard", None),
            P("shard"),
            P("shard"),
            P("shard"),
            P("shard", None),
            P("shard"),
            P("shard", None),
            P("shard"),
            P("shard"),
            P("shard"),
        ),
        check_vma=False,
    )
```

```python
import functools
import math

import jax
import jax.numpy as jnp
from jax import lax
from jax.experimental import pallas as pl
from jax.experimental.pallas import tpu as pltpu
from jax.sharding import PartitionSpec as P


H = 12
HD = 64


eps = 1e-12
masked_score = -1000000000.0


def layer_norm(values_in, gain_vec, shift_vec):
    row_mean = jnp.mean(values_in, axis=-1, keepdims=True)
    centered = values_in - row_mean
    variance = jnp.mean(centered * centered, axis=-1, keepdims=True)
    return centered * lax.rsqrt(variance + eps) * gain_vec + shift_vec


def gelu_exact(values_in):
    return jax.nn.gelu(values_in, approximate=False)


def contract_cols(left_mat, right_mat):
    return lax.dot_general(
        left_mat, right_mat, (((1,), (1,)), ((), ())), preferred_element_type=jnp.float32
    )


def contract_rows(left_mat, right_mat):
    return lax.dot_general(
        left_mat, right_mat, (((0,), (0,)), ((), ())), preferred_element_type=jnp.float32
    )


def column_sums(matrix):
    return jnp.sum(matrix.astype(jnp.float32), axis=0)


def unpack(weights_full):
    (
        qkv_weight,
        query_bias,
        value_bias,
        out_weight,
        out_bias,
        gain_one,
        shift_one,
        up_weight,
        up_bias,
        down_weight,
        down_bias,
        gain_two,
        shift_two,
    ) = weights_full
    as_float = lambda vector: vector.astype(jnp.float32)
    return (
        qkv_weight,
        as_float(query_bias),
        as_float(value_bias),
        out_weight,
        as_float(out_bias),
        as_float(gain_one),
        as_float(shift_one),
        up_weight,
        as_float(up_bias),
        down_weight,
        as_float(down_bias),
        as_float(gain_two),
        as_float(shift_two),
    )


def head_scores(queries, keys, key_mask, head_idx):
    col_start = head_idx * HD
    q_head = lax.dynamic_slice_in_dim(queries, col_start, HD, 1)
    k_head = lax.dynamic_slice_in_dim(keys, col_start, HD, 1)
    scores = contract_cols(q_head, k_head) * HD ** (-0.5)
    return (q_head, k_head, jnp.where(key_mask[None, :], scores, masked_score))


def attend_forward(queries, keys, values, key_mask):
    row_count, width = queries.shape

    def one_head(head_idx, carry):
        context, lse_rows = carry
        q_head, k_head, scores = head_scores(queries, keys, key_mask, head_idx)
        v_head = lax.dynamic_slice_in_dim(values, head_idx * HD, HD, 1)
        row_max = jnp.max(scores, axis=1, keepdims=True)
        exp_scores = jnp.exp(scores - row_max)
        row_total = jnp.sum(exp_scores, axis=1, keepdims=True)
        prob_low = (exp_scores / row_total).astype(jnp.bfloat16)
        head_out = jnp.dot(prob_low, v_head, preferred_element_type=jnp.float32)
        context = lax.dynamic_update_slice_in_dim(context, head_out, head_idx * HD, 1)
        lse_rows = lax.dynamic_update_slice_in_dim(
            lse_rows, row_max + jnp.log(row_total), head_idx, 1
        )
        return (context, lse_rows)

    start_state = (
        jnp.zeros((row_count, width), jnp.float32),
        jnp.zeros((row_count, H), jnp.float32),
    )
    return lax.fori_loop(0, H, one_head, start_state)


def attend_backward(queries, keys, values, key_mask, lse_rows, grad_context):
    row_count, width = queries.shape
    slot_count = keys.shape[0]

    def one_head(head_idx, carry):
        grad_q, grad_k, grad_v = carry
        col_start = head_idx * HD
        q_head, k_head, scores = head_scores(queries, keys, key_mask, head_idx)
        v_head = lax.dynamic_slice_in_dim(values, col_start, HD, 1)
        grad_head = lax.dynamic_slice_in_dim(grad_context, col_start, HD, 1)
        probs = jnp.exp(scores - lax.dynamic_slice_in_dim(lse_rows, head_idx, 1, 1))
        grad_probs = contract_cols(grad_head, v_head)
        delta = jnp.sum(probs * grad_probs, axis=1, keepdims=True)
        grad_scores = (probs * (grad_probs - delta)).astype(jnp.bfloat16)
        head_gq = jnp.dot(grad_scores, k_head, preferred_element_type=jnp.float32) * HD ** (-0.5)
        head_gk = contract_rows(grad_scores, q_head) * HD ** (-0.5)
        head_gv = contract_rows(probs.astype(jnp.bfloat16), grad_head)
        grad_q = lax.dynamic_update_slice_in_dim(grad_q, head_gq, col_start, 1)
        grad_k = lax.dynamic_update_slice_in_dim(grad_k, head_gk, col_start, 1)
        grad_v = lax.dynamic_update_slice_in_dim(grad_v, head_gv, col_start, 1)
        return (grad_q, grad_k, grad_v)

    start_state = (
        jnp.zeros((row_count, width), jnp.float32),
        jnp.zeros((slot_count, width), jnp.float32),
        jnp.zeros((slot_count, width), jnp.float32),
    )
    return lax.fori_loop(0, H, one_head, start_state)


def per_device(
    tokens,
    cotangent,
    lengths,
    w_qkv,
    bias_q,
    bias_v,
    w_out,
    bias_out,
    gain_attn,
    shift_attn,
    w_up,
    bias_up,
    w_down,
    bias_down,
    gain_ffn,
    shift_ffn,
):
    batch_count, row_count, width = tokens.shape
    dev_count = lax.axis_size("shard")
    slot_count = row_count * dev_count
    first_row = lax.axis_index("shard") * row_count
    key_place = jnp.arange(slot_count, dtype=jnp.int32)
    row_place = first_row + jnp.arange(row_count, dtype=jnp.int32)
    sharded = (
        w_qkv,
        bias_q,
        bias_v,
        w_out,
        bias_out,
        gain_attn,
        shift_attn,
        w_up,
        bias_up,
        w_down,
        bias_down,
        gain_ffn,
        shift_ffn,
    )
    totals = [
        jnp.zeros((piece.shape[0] * dev_count,) + piece.shape[1:], jnp.float32) for piece in sharded
    ]
    layer_rows = []
    grad_rows = []
    for batch_idx in range(batch_count):
        weights_full = unpack(
            (
                lax.all_gather(w_qkv, "shard", axis=0, tiled=True),
                lax.all_gather(bias_q, "shard", axis=0, tiled=True),
                lax.all_gather(bias_v, "shard", axis=0, tiled=True),
                lax.all_gather(w_out, "shard", axis=0, tiled=True),
                lax.all_gather(bias_out, "shard", axis=0, tiled=True),
                lax.all_gather(gain_attn, "shard", axis=0, tiled=True),
                lax.all_gather(shift_attn, "shard", axis=0, tiled=True),
                lax.all_gather(w_up, "shard", axis=0, tiled=True),
                lax.all_gather(bias_up, "shard", axis=0, tiled=True),
                lax.all_gather(w_down, "shard", axis=0, tiled=True),
                lax.all_gather(bias_down, "shard", axis=0, tiled=True),
                lax.all_gather(gain_ffn, "shard", axis=0, tiled=True),
                lax.all_gather(shift_ffn, "shard", axis=0, tiled=True),
            )
        )
        (
            qkv_weight,
            query_bias,
            value_bias,
            out_weight,
            out_bias,
            gain_one,
            shift_one,
            up_weight,
            up_bias,
            down_weight,
            down_bias,
            gain_two,
            shift_two,
        ) = weights_full
        seq_in = tokens[batch_idx]
        seq_len = lengths[batch_idx]
        key_mask = key_place < seq_len
        own_valid = row_place < seq_len
        row_mask = own_valid.astype(jnp.float32)[:, None]
        qkv_bias = jnp.concatenate([query_bias, jnp.zeros_like(query_bias), value_bias])
        qkv_low = (
            jnp.dot(seq_in, qkv_weight, preferred_element_type=jnp.float32) + qkv_bias
        ).astype(jnp.bfloat16)
        queries = qkv_low[:, :width]
        key_part = qkv_low[:, width : 2 * width]
        value_part = qkv_low[:, 2 * width :]
        keys_all, values_all = (
            lax.all_gather(key_part, "shard", axis=0, tiled=True),
            lax.all_gather(value_part, "shard", axis=0, tiled=True),
        )
        context, lse_rows = attend_forward(queries, keys_all, values_all, key_mask)
        context_low = context.astype(jnp.bfloat16)
        attn_out = jnp.dot(context_low, out_weight, preferred_element_type=jnp.float32) + out_bias
        hidden, norm_one_back = jax.vjp(
            layer_norm, seq_in.astype(jnp.float32) + attn_out, gain_one, shift_one
        )
        hidden_low = hidden.astype(jnp.bfloat16)
        up_proj = jnp.dot(hidden_low, up_weight, preferred_element_type=jnp.float32) + up_bias
        activation, gelu_back = jax.vjp(gelu_exact, up_proj)
        act_low = activation.astype(jnp.bfloat16)
        ffn_out = jnp.dot(act_low, down_weight, preferred_element_type=jnp.float32) + down_bias
        normed, norm_two_back = jax.vjp(layer_norm, hidden + ffn_out, gain_two, shift_two)
        layer_rows.append((normed * row_mask).astype(jnp.bfloat16))
        weights_full = unpack(
            (
                lax.all_gather(w_qkv, "shard", axis=0, tiled=True),
                lax.all_gather(bias_q, "shard", axis=0, tiled=True),
                lax.all_gather(bias_v, "shard", axis=0, tiled=True),
                lax.all_gather(w_out, "shard", axis=0, tiled=True),
                lax.all_gather(bias_out, "shard", axis=0, tiled=True),
                lax.all_gather(gain_attn, "shard", axis=0, tiled=True),
                lax.all_gather(shift_attn, "shard", axis=0, tiled=True),
                lax.all_gather(w_up, "shard", axis=0, tiled=True),
                lax.all_gather(bias_up, "shard", axis=0, tiled=True),
                lax.all_gather(w_down, "shard", axis=0, tiled=True),
                lax.all_gather(bias_down, "shard", axis=0, tiled=True),
                lax.all_gather(gain_ffn, "shard", axis=0, tiled=True),
                lax.all_gather(shift_ffn, "shard", axis=0, tiled=True),
            )
        )
        (
            qkv_weight,
            query_bias,
            value_bias,
            out_weight,
            out_bias,
            gain_one,
            shift_one,
            up_weight,
            up_bias,
            down_weight,
            down_bias,
            gain_two,
            shift_two,
        ) = weights_full
        grad_out = cotangent[batch_idx].astype(jnp.float32) * row_mask
        grad_res_two, grad_gain_two, grad_shift_two = norm_two_back(grad_out)
        grad_ffn_low = grad_res_two.astype(jnp.bfloat16)
        grad_act = contract_cols(grad_ffn_low, down_weight)
        (grad_up,) = gelu_back(grad_act)
        grad_up_low = grad_up.astype(jnp.bfloat16)
        grad_hidden = grad_res_two + contract_cols(grad_up_low, up_weight)
        grad_res_one, grad_gain_one, grad_shift_one = norm_one_back(grad_hidden)
        grad_attn_low = grad_res_one.astype(jnp.bfloat16)
        grad_ctx_low = contract_cols(grad_attn_low, out_weight).astype(jnp.bfloat16)
        keys_all, values_all = (
            lax.all_gather(key_part, "shard", axis=0, tiled=True),
            lax.all_gather(value_part, "shard", axis=0, tiled=True),
        )
        grad_q, grad_keys_all, grad_values_all = attend_backward(
            queries, keys_all, values_all, key_mask, lse_rows, grad_ctx_low
        )
        grad_keys, grad_values = (
            lax.psum_scatter(
                grad_keys_all.astype(jnp.bfloat16), "shard", scatter_dimension=0, tiled=True
            ).astype(jnp.float32),
            lax.psum_scatter(
                grad_values_all.astype(jnp.bfloat16), "shard", scatter_dimension=0, tiled=True
            ).astype(jnp.float32),
        )
        grad_qkv_low = jnp.concatenate([grad_q, grad_keys, grad_values], axis=1).astype(
            jnp.bfloat16
        )
        grad_input = grad_res_one + contract_cols(grad_qkv_low, qkv_weight)
        grad_rows.append(grad_input.astype(jnp.bfloat16))
        terms = (
            contract_rows(seq_in, grad_qkv_low),
            column_sums(grad_qkv_low[:, :width]),
            column_sums(grad_qkv_low[:, 2 * width :]),
            contract_rows(context_low, grad_attn_low),
            column_sums(grad_attn_low),
            grad_gain_one,
            grad_shift_one,
            contract_rows(hidden_low, grad_up_low),
            column_sums(grad_up_low),
            contract_rows(act_low, grad_ffn_low),
            column_sums(grad_ffn_low),
            grad_gain_two,
            grad_shift_two,
        )
        totals = [running + fresh for running, fresh in zip(totals, terms)]
    grad_local = (
        lax.psum_scatter(
            totals[0].astype(jnp.bfloat16), "shard", scatter_dimension=0, tiled=True
        ).astype(jnp.float32),
        lax.psum_scatter(
            totals[1].astype(jnp.bfloat16), "shard", scatter_dimension=0, tiled=True
        ).astype(jnp.float32),
        lax.psum_scatter(
            totals[2].astype(jnp.bfloat16), "shard", scatter_dimension=0, tiled=True
        ).astype(jnp.float32),
        lax.psum_scatter(
            totals[3].astype(jnp.bfloat16), "shard", scatter_dimension=0, tiled=True
        ).astype(jnp.float32),
        lax.psum_scatter(
            totals[4].astype(jnp.bfloat16), "shard", scatter_dimension=0, tiled=True
        ).astype(jnp.float32),
        lax.psum_scatter(
            totals[5].astype(jnp.bfloat16), "shard", scatter_dimension=0, tiled=True
        ).astype(jnp.float32),
        lax.psum_scatter(
            totals[6].astype(jnp.bfloat16), "shard", scatter_dimension=0, tiled=True
        ).astype(jnp.float32),
        lax.psum_scatter(
            totals[7].astype(jnp.bfloat16), "shard", scatter_dimension=0, tiled=True
        ).astype(jnp.float32),
        lax.psum_scatter(
            totals[8].astype(jnp.bfloat16), "shard", scatter_dimension=0, tiled=True
        ).astype(jnp.float32),
        lax.psum_scatter(
            totals[9].astype(jnp.bfloat16), "shard", scatter_dimension=0, tiled=True
        ).astype(jnp.float32),
        lax.psum_scatter(
            totals[10].astype(jnp.bfloat16), "shard", scatter_dimension=0, tiled=True
        ).astype(jnp.float32),
        lax.psum_scatter(
            totals[11].astype(jnp.bfloat16), "shard", scatter_dimension=0, tiled=True
        ).astype(jnp.float32),
        lax.psum_scatter(
            totals[12].astype(jnp.bfloat16), "shard", scatter_dimension=0, tiled=True
        ).astype(jnp.float32),
    )
    grad_total = (
        lax.psum(grad_local[0].astype(jnp.bfloat16), "grp").astype(jnp.float32),
        lax.psum(grad_local[1].astype(jnp.bfloat16), "grp").astype(jnp.float32),
        lax.psum(grad_local[2].astype(jnp.bfloat16), "grp").astype(jnp.float32),
        lax.psum(grad_local[3].astype(jnp.bfloat16), "grp").astype(jnp.float32),
        lax.psum(grad_local[4].astype(jnp.bfloat16), "grp").astype(jnp.float32),
        lax.psum(grad_local[5].astype(jnp.bfloat16), "grp").astype(jnp.float32),
        lax.psum(grad_local[6].astype(jnp.bfloat16), "grp").astype(jnp.float32),
        lax.psum(grad_local[7].astype(jnp.bfloat16), "grp").astype(jnp.float32),
        lax.psum(grad_local[8].astype(jnp.bfloat16), "grp").astype(jnp.float32),
        lax.psum(grad_local[9].astype(jnp.bfloat16), "grp").astype(jnp.float32),
        lax.psum(grad_local[10].astype(jnp.bfloat16), "grp").astype(jnp.float32),
        lax.psum(grad_local[11].astype(jnp.bfloat16), "grp").astype(jnp.float32),
        lax.psum(grad_local[12].astype(jnp.bfloat16), "grp").astype(jnp.float32),
    )
    return (
        jnp.stack(layer_rows),
        jnp.stack(grad_rows),
        grad_total[0],
        grad_total[1],
        grad_total[2],
        grad_total[3],
        grad_total[4],
        grad_total[5],
        grad_total[6],
        grad_total[7],
        grad_total[8],
        grad_total[9],
        grad_total[10],
        grad_total[11],
        grad_total[12],
    )


BF = jnp.bfloat16
GRANT = 60 << 20
COST = pl.CostEstimate(flops=1024, bytes_accessed=1024, transcendentals=0)
F32 = jnp.float32


def swap_core(value):
    return lax.ppermute(value, "grp", [(i, i ^ 1) for i in range(8)])


def swap_x(value):
    return lax.ppermute(value, "grp", [(i, i ^ 2) for i in range(8)])


def swap_y(value):
    return lax.ppermute(value, "grp", [(i, i ^ 4) for i in range(8)])


def swap_z(value, flip):
    return lax.ppermute(value, "shard", [(i, i ^ flip) for i in range(4)])


def swap_xy(value):
    return lax.ppermute(value, "grp", [(i, i ^ 6) for i in range(8)])


def dot32(left_mat, right_mat):
    return jnp.dot(left_mat, right_mat, preferred_element_type=F32)


def after(values, *others):
    return lax.optimization_barrier((values, others))[0]


def sequence_perm(flip):
    pairs = []
    for grp in range(8):
        for line in range(4):
            dst_grp = (grp & 6) | (line // 2)
            dst_line = 2 * (grp & 1) + ((line % 2) ^ flip)
            pairs.append((grp * 4 + line, dst_grp * 4 + dst_line))
    return pairs


def send_first(block):
    return lax.ppermute(block, ("grp", "shard"), sequence_perm(0))


def send_second(block):
    return lax.ppermute(block, ("grp", "shard"), sequence_perm(1))


def send_rows(first, second):
    return send_first(first), send_second(second)


def return_block(block, flip):
    return lax.ppermute(block, ("grp", "shard"), [(dst, src) for src, dst in sequence_perm(flip)])


def return_rows(first, second):
    return return_block(first, 0), return_block(second, 1)


def join_rows(first, second, parity):
    return jnp.where(parity == 0, jnp.stack([first, second]), jnp.stack([second, first]))


CORE, PLANE, LINE, PARITY = range(4)


def start_moves(moves, where_ref, sources, targets, sems):
    where = [where_ref[idx] for idx in range(4)]
    place = lambda at, unit: at if isinstance(at, int) else pl.multiple_of(at(*where), unit)
    copies = []
    for idx, (src, src_row, src_col, rows, cols, dst, dst_row, dst_col) in enumerate(moves):
        copies.append(
            pltpu.make_async_copy(
                sources[src].at[pl.ds(place(src_row, 8), rows), pl.ds(place(src_col, 128), cols)],
                targets[dst].at[pl.ds(place(dst_row, 8), rows), pl.ds(place(dst_col, 128), cols)],
                sems.at[idx],
            )
        )
    for copy in copies:
        copy.start()
    return copies


def move_kernel(count, moves, where_ref, *refs):
    for copy in start_moves(moves, where_ref, refs[:count], refs[count:-1], refs[-1]):
        copy.wait()


def move_blocks(where, sources, moves, shapes, grant=16 << 20):
    moved = sum(move[3] * move[4] for move in moves) * 2
    return pl.pallas_call(
        functools.partial(move_kernel, len(sources), moves),
        out_shape=[jax.ShapeDtypeStruct(shape, sources[0].dtype) for shape in shapes],
        in_specs=[pl.BlockSpec(memory_space=pltpu.SMEM)]
        + [pl.BlockSpec(memory_space=pl.ANY)] * len(sources),
        out_specs=[pl.BlockSpec(memory_space=pltpu.VMEM)] * len(shapes),
        scratch_shapes=[pltpu.SemaphoreType.DMA((len(moves),))],
        cost_estimate=COST,
        compiler_params=pltpu.CompilerParams(vmem_limit_bytes=grant),
    )(where, *sources)


def join_blocks(where, parts):
    moves, at = [], 0
    for idx, part in enumerate(parts):
        moves.append((idx, 0, 0, part.shape[0], part.shape[1], 0, at, 0))
        at += part.shape[0]
    return move_blocks(where, list(parts), moves, [(at, parts[0].shape[1])])[0]


def along_line(piece):
    return [swap_z(piece, flip) for flip in (1, 2, 3)]


def across_plane(came):
    return [swap_x(came), swap_y(came), swap_xy(came)]


def placed_moves(first_src, height, piece_rows, col, cols, dst):
    moves = []
    for flip in range(4):
        for step in range(1, 4):
            at = lambda core, plane, line, parity, flip=flip, step=step: (
                (line ^ step) * (4 * piece_rows) + (plane ^ flip) * piece_rows
            )
            moves.append((first_src + flip, (step - 1) * height, col, piece_rows, cols, dst, at, 0))
    return moves


def pick(arr, idx, axis):
    return lax.dynamic_index_in_dim(arr, idx, axis, keepdims=False)


def add_low(left, right):
    return (left.astype(F32) + right.astype(F32)).astype(BF)


def reduce_first(grads, cut, col, row):
    join = lambda arrs: arrs[0] if len(arrs) == 1 else jnp.concatenate(arrs, axis=-1)
    low_part = lambda idx: join([pick(grad[:, :, :, :cut], idx, 2) for grad in grads])
    high_part = lambda idx: join([pick(grad[:, :, :, cut:], idx, 1) for grad in grads])
    sent = (low_part(1 - col), high_part(1 - row))
    return (low_part(col), high_part(row), swap_x(sent[0]), swap_y(sent[1])), sent


def reduce_second(state, col, row):
    low, high, low_got, high_got = state
    low, high = add_low(low, low_got), add_low(high, high_got)
    sent = (pick(low, 1 - row, 1), pick(high, 1 - col, 1))
    return (pick(low, row, 1), pick(high, col, 1), swap_y(sent[0]), swap_x(sent[1])), sent


def reduce_near(states, line):
    mine = [
        jnp.concatenate([add_low(low, low_got), add_low(high, high_got)], axis=1)
        for low, high, low_got, high_got in states
    ]
    mine = mine[0] if len(mine) == 1 else jnp.concatenate(mine, axis=-1)
    pairs = mine.reshape((2, 2) + mine.shape[1:])
    sent = pick(pairs, 1 - line % 2, 1)
    return (pick(pairs, line % 2, 1), swap_z(sent, 1)), sent


def reduce_far(state, line):
    mine = add_low(*state)
    sent = pick(mine, 1 - line // 2, 0)
    return (pick(mine, line // 2, 0), swap_z(sent, 2)), sent


def direct_spread(state):
    piece = sum(part.astype(F32) for part in state).astype(BF)
    return [piece] + across_plane(piece), piece


def final_kernel(layout, rows, extra, flips, where_ref, mine_ref, other_ref, *outs):
    plane = where_ref[PLANE]
    height = mine_ref.shape[0] // 4

    low = where_ref[CORE] == 0
    for half in range(2):
        for at in range(4):
            part = plane ^ flips[at]
            for src_col, cols, dst, row_of, dst_col in layout(half):
                row = pl.multiple_of(row_of(part), 16)
                here = (pl.ds(at * height, rows), pl.ds(src_col, cols))
                mine, other = mine_ref[here], other_ref[here]
                value = jnp.where(low, mine, other) if half == 0 else jnp.where(low, other, mine)
                outs[dst][pl.ds(row, rows), pl.ds(dst_col, cols)] = value.astype(F32)
    if extra is not None:
        vecs = outs[-9:]
        slab = vecs[0].shape[0]
        for at in range(4):

            @pl.when(plane == flips[at])
            def _(at=at):
                begin, end = [
                    mine_ref[here, pl.ds(extra, 128)].astype(F32) + other_ref[here, pl.ds(extra, 128)].astype(F32)
                    for here in (pl.ds(at * height, 16), pl.ds(at * height + 16, 16))
                ]
                both = jnp.concatenate([begin, end], axis=1)
                for idx in range(8):
                    vecs[idx][...] = both[idx : idx + 1, :slab].reshape(slab)
                spread = jnp.concatenate([both, jnp.zeros((16, 4 * slab - 256), F32)], axis=1)
                lane = lax.broadcasted_iota(jnp.int32, spread.shape, 1)
                spread = jnp.where(lane < slab, spread, 0.0)
                wide = spread[8:9]
                for part in range(1, 4):
                    wide += pltpu.roll(spread[8 + part : 9 + part], part * slab, 1)
                vecs[8][...] = wide.reshape(4 * slab)


def spread_first(state, through_x):
    piece = add_low(*state)
    return piece, (swap_x if through_x else swap_y)(piece)


def spread_second(state, through_x):
    both = jnp.concatenate(state, axis=0)
    return both, (swap_y if through_x else swap_x)(both)


def spread_core(state):
    mine = jnp.concatenate(state, axis=0)
    return mine, swap_core(mine)


def finish_grad(where, state, through_x, layout, rows, shapes, extra=None):
    mine, other = state
    mine_flips = (0, 1, 2, 3) if through_x else (0, 2, 1, 3)
    shapes = list(shapes) + ([] if extra is None else [(shapes[0][0],)] * 8 + [(4 * shapes[0][0],)])
    vmem = pl.BlockSpec(memory_space=pltpu.VMEM)
    return pl.pallas_call(
        functools.partial(final_kernel, layout, rows, extra, mine_flips),
        out_shape=[jax.ShapeDtypeStruct(shape, F32) for shape in shapes],
        in_specs=[pl.BlockSpec(memory_space=pltpu.SMEM), vmem, vmem],
        out_specs=[vmem] * len(shapes),
        cost_estimate=COST,
        compiler_params=pltpu.CompilerParams(vmem_limit_bytes=16 << 20),
    )(where, mine, other)


ROWS = 256


def row_spec(width, shift=0, steps=1, block=ROWS):
    if shift:
        return pl.BlockSpec((block, width), lambda blk: ((blk + shift) % steps, 0))
    return pl.BlockSpec((block, width), lambda blk: (blk, 0))


def whole_spec(rows, width):
    return pl.BlockSpec((rows, width), lambda blk: (0, 0))


def mean_last(values):
    return jnp.mean(values, axis=-1, keepdims=True)


def norm_parts(values):
    centered = values - mean_last(values)
    scale = lax.rsqrt(mean_last(centered * centered) + eps)
    return centered * scale, scale


def norm_back(grad_normed, normed, scale):
    return scale * (grad_normed - mean_last(grad_normed) - normed * mean_last(grad_normed * normed))


def up_kernel(part_ref, got_ref, tok_ref, vec_ref, bias_ref, w_ref, low_ref, n_ref, r_ref, act_ref, slope_ref):
    vec = vec_ref[...]
    attn_out = part_ref[...].astype(F32) + got_ref[...].astype(F32) + vec[0:1]
    normed, scale = norm_parts(tok_ref[...].astype(F32) + attn_out)
    hidden = (normed * vec[1:2] + vec[2:3]).astype(BF)
    n_ref[...] = normed
    r_ref[...] = jnp.broadcast_to(scale, r_ref.shape)
    low_ref[...] = hidden
    for at in range(0, w_ref.shape[1], 384):
        cols = pl.ds(at, 384)
        up = dot32(hidden, w_ref[:, cols]) + bias_ref[:, cols]
        cdf = 0.5 + 0.5 * lax.erf(up * 0.5**0.5)
        act_ref[:, cols] = (up * cdf).astype(BF)
        slope = cdf + up * (jnp.exp(up * up * -0.5) * (2 * math.pi) ** -0.5)
        slope_ref[:, cols] = slope.astype(BF)


def ffn_up(part, got, tokens, vectors, up_bias, weight):
    rows, width = part.shape
    units = weight.shape[1]
    block = ROWS // 2
    steps = rows // block
    return pl.pallas_call(
        up_kernel,
        grid=(steps,),
        out_shape=[
            jax.ShapeDtypeStruct((rows, width), BF),
            jax.ShapeDtypeStruct((rows, width), F32),
            jax.ShapeDtypeStruct((rows, 128), F32),
            jax.ShapeDtypeStruct((rows, units), BF),
            jax.ShapeDtypeStruct((rows, units), BF),
        ],
        in_specs=[
            row_spec(width, block=block),
            row_spec(width, steps // 2, steps, block=block),
            row_spec(width, block=block),
            whole_spec(8, width),
            whole_spec(1, units),
            whole_spec(width, units),
        ],
        out_specs=[row_spec(width, block=block), row_spec(width, block=block), row_spec(128, block=block), row_spec(units, block=block), row_spec(units, block=block)],
        cost_estimate=COST,
        compiler_params=pltpu.CompilerParams(vmem_limit_bytes=20 << 20),
    )(part, got, tokens, vectors, up_bias, weight)


def turn_kernel(
    half_steps, part_ref, got_ref, n_ref, cot_ref, bias_ref, vec_ref, first_ref, second_ref, dr_ref, low_ref, sum_ref
):
    blk = pl.program_id(0)
    vec = vec_ref[...]
    hidden = n_ref[...] * vec[1:2] + vec[2:3]
    ffn_out = part_ref[...].astype(F32) + got_ref[...].astype(F32) + vec[3:4]
    normed, scale = norm_parts(hidden + ffn_out)
    mask = jnp.where(bias_ref[:, 0:1] < 0.0, 0.0, 1.0)
    result = ((normed * vec[4:5] + vec[5:6]) * mask).astype(BF)
    dy = cot_ref[...].astype(F32) * mask
    dr = norm_back(dy * vec[4:5], normed, scale)
    dr_low = dr.astype(BF)
    dr_ref[...] = dr
    low_ref[...] = dr_low

    @pl.when(blk == 0)
    def _():
        sum_ref[...] = jnp.zeros_like(sum_ref)
        first_ref[...] = result

    @pl.when(blk == 1)
    def _():
        second_ref[...] = result

    @pl.when(blk < half_steps)
    def _():
        sum_ref[0:1] += jnp.sum(dy * normed, axis=0, keepdims=True)
        sum_ref[1:2] += jnp.sum(dy, axis=0, keepdims=True)
        sum_ref[2:3] += jnp.sum(dr_low.astype(F32), axis=0, keepdims=True)


def norm_turn(part, got, n_one, cot, bias, vectors):
    rows, width = part.shape
    steps = rows // ROWS
    return pl.pallas_call(
        functools.partial(turn_kernel, steps // 2),
        grid=(steps,),
        out_shape=[jax.ShapeDtypeStruct((ROWS, width), BF)] * 2
        + [
            jax.ShapeDtypeStruct((rows, width), F32),
            jax.ShapeDtypeStruct((rows, width), BF),
            jax.ShapeDtypeStruct((8, width), F32),
        ],
        in_specs=[
            row_spec(width),
            row_spec(width, steps // 2, steps),
            row_spec(width),
            row_spec(width),
            row_spec(128),
            whole_spec(8, width),
        ],
        out_specs=[whole_spec(ROWS, width)] * 2 + [row_spec(width), row_spec(width), whole_spec(8, width)],
        cost_estimate=COST,
        compiler_params=pltpu.CompilerParams(vmem_limit_bytes=28 << 20),
    )(part, got, n_one, cot, bias, vectors)


def ffn_back_kernel(dffn_ref, down_ref, slope_ref, up_ref, dup_ref, part_ref, sum_ref):
    @pl.when(pl.program_id(0) == 0)
    def _():
        sum_ref[...] = jnp.zeros_like(sum_ref)

    total = jnp.zeros(part_ref.shape, F32)
    dffn = dffn_ref[...]
    for at in range(0, dup_ref.shape[1], 512):
        here = pl.ds(at, 512)
        dup = (contract_cols(dffn, down_ref[here, :]) * slope_ref[:, here].astype(F32)).astype(BF)
        dup_ref[:, here] = dup
        sum_ref[:, here] += jnp.sum(dup.astype(F32), axis=0, keepdims=True)
        total += contract_cols(dup, up_ref[:, here])
    part_ref[...] = total.astype(BF)


def ffn_back(dffn, down_weight, slope, up_weight):
    rows, width = dffn.shape
    units = slope.shape[1]
    return pl.pallas_call(
        ffn_back_kernel,
        grid=(rows // ROWS,),
        out_shape=[
            jax.ShapeDtypeStruct((rows, units), BF),
            jax.ShapeDtypeStruct((rows, width), BF),
            jax.ShapeDtypeStruct((1, units), F32),
        ],
        in_specs=[row_spec(width), whole_spec(units, width), row_spec(units), whole_spec(width, units)],
        out_specs=[row_spec(units), row_spec(width), whole_spec(1, units)],
        cost_estimate=COST,
        compiler_params=pltpu.CompilerParams(vmem_limit_bytes=20 << 20),
    )(dffn, down_weight, slope, up_weight)


def back_kernel(
    half_steps, where_ref, dr_ref, part_ref, got_ref, n_ref, r_ref, vec_ref, own_ref, low_ref, part_low_ref, sum_ref
):
    blk = pl.program_id(0)
    vec = vec_ref[...]
    normed = n_ref[...]
    dhidden = dr_ref[...] + (part_ref[...].astype(F32) + got_ref[...].astype(F32))
    dr = norm_back(dhidden * vec[1:2], normed, r_ref[:, 0:1])
    dr_low = dr.astype(BF)
    low_ref[...] = dr_low
    half = dr.shape[1] // 2
    part_low_ref[...] = jnp.where(where_ref[CORE] == 0, dr_low[:, :half], dr_low[:, half:])

    @pl.when(blk == 0)
    def _():
        sum_ref[...] = jnp.zeros_like(sum_ref)

    @pl.when(blk < half_steps)
    def _():
        own_ref[...] = dr
        sum_ref[0:1] += jnp.sum(dhidden * normed, axis=0, keepdims=True)
        sum_ref[1:2] += jnp.sum(dhidden, axis=0, keepdims=True)
        sum_ref[2:3] += jnp.sum(dr_low.astype(F32), axis=0, keepdims=True)


def norm_one_back(where, dr_two, part, got, n_one, r_one, vectors):
    rows, width = part.shape
    steps = rows // ROWS
    return pl.pallas_call(
        functools.partial(back_kernel, steps // 2),
        grid=(steps,),
        out_shape=[
            jax.ShapeDtypeStruct((rows // 2, width), F32),
            jax.ShapeDtypeStruct((rows, width), BF),
            jax.ShapeDtypeStruct((rows, width // 2), BF),
            jax.ShapeDtypeStruct((8, width), F32),
        ],
        in_specs=[
            pl.BlockSpec(memory_space=pltpu.SMEM),
            row_spec(width),
            row_spec(width),
            row_spec(width, steps // 2, steps),
            row_spec(width),
            row_spec(128),
            whole_spec(8, width),
        ],
        out_specs=[
            pl.BlockSpec((ROWS, width), lambda blk: (jnp.minimum(blk, steps // 2 - 1), 0)),
            row_spec(width),
            row_spec(width // 2),
            whole_spec(8, width),
        ],
        cost_estimate=COST,
        compiler_params=pltpu.CompilerParams(vmem_limit_bytes=28 << 20),
    )(where, dr_two, part, got, n_one, r_one, vectors)


Q_BLOCK = 512
PAIR = 128


def contract_last(left_mat, right_mat):
    return lax.dot_general(
        left_mat, right_mat, (((1,), (1,)), ((), ())), preferred_element_type=F32
    )


def head_lanes(block, head):
    lane = lax.broadcasted_iota(jnp.int32, block.shape, 1)
    return jnp.where((lane // HD) == head, block, jnp.zeros_like(block))


def attend_fwd_kernel(q_ref, k_ref, v_ref, bias_ref, ctx_ref, lse_ref, vt_ref, out_ref):
    vt_ref[...] = v_ref[...].T

    @pl.loop(0, q_ref.shape[0] // Q_BLOCK)
    def _(blk):
        at = pl.multiple_of(blk * Q_BLOCK, Q_BLOCK)

        @pl.loop(0, 2)
        def _(head):
            q_blk = q_ref[pl.ds(at, Q_BLOCK), :] * jnp.asarray(HD ** (-0.5), BF)
            here = pl.ds(pl.multiple_of(head * HD, HD), HD)
            scores = contract_last(k_ref[...], head_lanes(q_blk, head))
            scores = scores + jnp.concatenate([bias_ref[...]] * (Q_BLOCK // 128), axis=1)
            top = jnp.max(scores, axis=0, keepdims=True)
            exps = jnp.exp(scores - top)
            total = jnp.sum(exps, axis=0, keepdims=True)
            out_ref[here, :] = dot32(vt_ref[here, :], exps.astype(BF)) * (1.0 / total)
            lse_ref[0, pl.ds(head, 1), pl.ds(at, Q_BLOCK)] = top + jnp.log(total)

        ctx_ref[pl.ds(at, Q_BLOCK), :] = out_ref[...].T.astype(BF)


def attend_bwd_kernel(
    q_ref, k_ref, v_ref, bias_ref, lse_ref, grad_ref, dq_ref, dk_ref, dv_ref, kt_ref, dk_acc, dv_acc, out_ref
):
    kt_ref[...] = k_ref[...].T
    dk_acc[...] = jnp.zeros_like(dk_acc)
    dv_acc[...] = jnp.zeros_like(dv_acc)

    @pl.loop(0, q_ref.shape[0] // Q_BLOCK)
    def _(blk):
        at = pl.multiple_of(blk * Q_BLOCK, Q_BLOCK)

        @pl.loop(0, 2)
        def _(head):
            q_head = head_lanes(q_ref[pl.ds(at, Q_BLOCK), :] * jnp.asarray(HD ** (-0.5), BF), head)
            grad_head = head_lanes(grad_ref[pl.ds(at, Q_BLOCK), :], head)
            here = pl.ds(pl.multiple_of(head * HD, HD), HD)
            scores = contract_last(k_ref[...], q_head)
            scores = scores + jnp.concatenate([bias_ref[...]] * (Q_BLOCK // 128), axis=1)
            probs = jnp.exp(scores - lse_ref[0, pl.ds(head, 1), pl.ds(at, Q_BLOCK)])
            weighed = probs * contract_last(v_ref[...], grad_head)
            delta = jnp.sum(weighed, axis=0, keepdims=True)
            grad_scores = (weighed - probs * delta).astype(BF)
            dk_acc[...] += dot32(grad_scores, q_head)
            dv_acc[...] += dot32(probs.astype(BF), grad_head)
            out_ref[here, :] = dot32(kt_ref[here, :], grad_scores)

        dq_ref[pl.ds(at, Q_BLOCK), :] = (out_ref[...].T * (HD ** (-0.5))).astype(BF)

    dk_ref[...] = dk_acc[...].astype(BF)
    dv_ref[...] = dv_acc[...].astype(BF)


def column_spec(rows, first):
    return pl.BlockSpec((rows, PAIR), lambda pair: (0, first + pair))


def attend_chip_forward(qkv, bias, pair):
    rows, half = qkv.shape[0], qkv.shape[1] // 3
    pairs = half // PAIR
    return pl.pallas_call(
        attend_fwd_kernel,
        grid=(1,),
        out_shape=[
            jax.ShapeDtypeStruct((rows, PAIR), BF),
            jax.ShapeDtypeStruct((1, 2, rows), F32),
        ],
        in_specs=[column_spec(rows, idx * pairs + pair) for idx in range(3)]
        + [pl.BlockSpec((rows, 128), lambda step: (0, 0))],
        out_specs=[column_spec(rows, 0), pl.BlockSpec((1, 2, rows), lambda step: (0, 0, 0))],
        scratch_shapes=[pltpu.VMEM((PAIR, rows), BF), pltpu.VMEM((PAIR, Q_BLOCK), F32)],
        cost_estimate=COST,
        compiler_params=pltpu.CompilerParams(vmem_limit_bytes=28 << 20),
    )(qkv, qkv, qkv, bias)


def attend_chip_backward(qkv, bias, lse, grad_ctx, pair):
    rows, half = qkv.shape[0], qkv.shape[1] // 3
    pairs = half // PAIR
    return pl.pallas_call(
        attend_bwd_kernel,
        grid=(1,),
        out_shape=[jax.ShapeDtypeStruct((rows, PAIR), BF)] * 3,
        in_specs=[column_spec(rows, idx * pairs + pair) for idx in range(3)]
        + [
            pl.BlockSpec((rows, 128), lambda step: (0, 0)),
            pl.BlockSpec((1, 2, rows), lambda step: (0, 0, 0)),
            column_spec(rows, pair),
        ],
        out_specs=[column_spec(rows, 0)] * 3,
        scratch_shapes=[
            pltpu.VMEM((PAIR, rows), BF),
            pltpu.VMEM((rows, PAIR), F32),
            pltpu.VMEM((rows, PAIR), F32),
            pltpu.VMEM((PAIR, Q_BLOCK), F32),
        ],
        cost_estimate=COST,
        compiler_params=pltpu.CompilerParams(vmem_limit_bytes=32 << 20),
    )(qkv, qkv, qkv, bias, lse, grad_ctx)


def pack_kernel(count, moves, vec_at, slab, where_ref, *refs):
    sources, vecs = refs[:count], refs[count : count + 9]
    targets, sems = refs[count + 9 : -1], refs[-1]
    copies = start_moves(moves, where_ref, sources, targets, sems)
    dst, row = vec_at
    width = targets[dst].shape[1]
    rows = [vec[...].reshape(1, slab).astype(F32) for vec in vecs[:8]]
    wide = vecs[8][...].reshape(1, -1).astype(F32)
    count_wide = wide.shape[1] // slab
    rows += [wide[:, :slab]]
    rows += [pltpu.roll(wide, wide.shape[1] - idx * slab, 1)[:, :slab] for idx in range(1, count_wide)]
    rows += [jnp.zeros((4, slab), F32)]
    block = jnp.concatenate(rows, axis=0)
    targets[dst][pl.ds(row, 16), :] = jnp.concatenate(
        [block, jnp.zeros((16, width - slab), F32)], axis=1
    ).astype(BF)
    for copy in copies:
        copy.wait()


def pack_blocks(where, sources, vecs, moves, shapes, vec_at, slab):
    return pl.pallas_call(
        functools.partial(pack_kernel, len(sources), moves, vec_at, slab),
        out_shape=[jax.ShapeDtypeStruct(shape, BF) for shape in shapes],
        in_specs=[pl.BlockSpec(memory_space=pltpu.SMEM)]
        + [pl.BlockSpec(memory_space=pl.ANY)] * len(sources)
        + [pl.BlockSpec(memory_space=pltpu.VMEM)] * len(vecs),
        out_specs=[pl.BlockSpec(memory_space=pltpu.VMEM)] * len(shapes),
        scratch_shapes=[pltpu.SemaphoreType.DMA((len(moves),))],
        cost_estimate=COST,
        compiler_params=pltpu.CompilerParams(vmem_limit_bytes=60 << 20),
    )(where, *sources, *vecs)


def vector_kernel(height, at, slab, where_ref, own_ref, came_ref, block_ref, qkv_ref, up_ref, buf, sems):
    line = where_ref[LINE]
    copies = [pltpu.make_async_copy(own_ref.at[pl.ds(at, 16)], buf.at[line], sems.at[0])]
    for step in range(1, 4):
        copies.append(
            pltpu.make_async_copy(
                came_ref.at[pl.ds((step - 1) * height + at, 16)], buf.at[line ^ step], sems.at[step]
            )
        )
    for copy in copies:
        copy.start()
    for copy in copies:
        copy.wait()
    width = block_ref.shape[1]
    half = width // 2
    joined = jnp.zeros((16, width), F32)
    lane = lax.broadcasted_iota(jnp.int32, (16, width), 1)
    wide = []
    for idx in range(4):
        rows = jnp.where(lane < slab, buf[idx, :, :width].astype(F32), 0.0)
        joined += rows if idx == 0 else pltpu.roll(rows, idx * slab, 1)
        row = rows[8:9]
        for part in range(1, 4):
            row += pltpu.roll(rows[8 + part : 9 + part], part * slab, 1)
        wide.append(row)
    low = where_ref[CORE] == 0
    pick_half = lambda row: jnp.where(low, row[:, :half], row[:, half:])
    block_ref[...] = jnp.concatenate([joined[2:8], jnp.zeros((2, width), F32)], axis=0)
    qkv_ref[...] = jnp.concatenate(
        [pick_half(joined[0:1]), jnp.zeros((1, half), F32), pick_half(joined[1:2])], axis=1
    )
    up_ref[...] = jnp.concatenate([pick_half(row) for row in wide], axis=1)


def join_vectors(where, own, came, at, slab, width):
    height = came.shape[0] // 3
    return pl.pallas_call(
        functools.partial(vector_kernel, height, at, slab),
        out_shape=[
            jax.ShapeDtypeStruct((8, width), F32),
            jax.ShapeDtypeStruct((1, 3 * width // 2), F32),
            jax.ShapeDtypeStruct((1, 2 * width), F32),
        ],
        in_specs=[pl.BlockSpec(memory_space=pltpu.SMEM)] + [pl.BlockSpec(memory_space=pl.ANY)] * 2,
        out_specs=[pl.BlockSpec(memory_space=pltpu.VMEM)] * 3,
        scratch_shapes=[pltpu.VMEM((4, 16, own.shape[1]), BF), pltpu.SemaphoreType.DMA((4,))],
        cost_estimate=COST,
        compiler_params=pltpu.CompilerParams(vmem_limit_bytes=4 << 20),
    )(where, own, came)


def small_kernel(slab, where_ref, one_ref, two_ref, up_ref, qkv_ref, out_ref):
    width = one_ref.shape[1]
    half = width // 2
    low = where_ref[CORE] == 0
    zero = jnp.zeros((1, half), F32)
    on_core = lambda row: jnp.where(
        low, jnp.concatenate([row, zero], axis=1), jnp.concatenate([zero, row], axis=1)
    )
    one, two = one_ref[...], two_ref[...]
    rows = jnp.concatenate(
        [
            on_core(qkv_ref[:, :half]),
            on_core(qkv_ref[:, 2 * half :]),
            one[2:3],
            one[0:1],
            one[1:2],
            two[2:3],
            two[0:1],
            two[1:2],
        ],
        axis=0,
    )
    out_ref[...] = jnp.zeros_like(out_ref)
    for idx in range(4):
        wide = on_core(up_ref[:, idx * half : (idx + 1) * half])
        at = lambda row, part: row if part == 0 else pltpu.roll(row, width - part * slab, 1)
        parts = [at(wide, part)[:, :256] for part in range(4)]
        block = jnp.concatenate([at(rows, idx)[:, :256]] + parts + [jnp.zeros((4, 256), F32)], axis=0)
        lane = lax.broadcasted_iota(jnp.int32, block.shape, 1)
        block = jnp.where(lane < slab, block, 0.0).astype(BF)
        out_ref[idx, 0:16, :] = block[:, :128]
        out_ref[idx, 16:32, :] = block[:, 128:]


def small_grads(where, sums_one, sums_two, up_sums, qkv_sums, slab):
    vmem = pl.BlockSpec(memory_space=pltpu.VMEM)
    return pl.pallas_call(
        functools.partial(small_kernel, slab),
        out_shape=jax.ShapeDtypeStruct((4, slab // 4, 128), BF),
        in_specs=[pl.BlockSpec(memory_space=pltpu.SMEM)] + [vmem] * 4,
        out_specs=vmem,
        compiler_params=pltpu.CompilerParams(vmem_limit_bytes=4 << 20),
    )(where, sums_one, sums_two, up_sums, qkv_sums)


def per_device_chip(
    tokens,
    cotangent,
    lengths,
    w_qkv,
    bias_q,
    bias_v,
    w_out,
    bias_out,
    gain_attn,
    shift_attn,
    w_up,
    bias_up,
    w_down,
    bias_down,
    gain_ffn,
    shift_ffn,
):
    quarter, width = tokens.shape[1:]
    half_rows = 2 * quarter
    units = w_up.shape[1] // 2
    slab = w_qkv.shape[0]
    wide = w_down.shape[0]
    half = width // 2
    slab_part, wide_part = slab // 4, wide // 8
    vec_rows = 16
    group = lax.axis_index("grp")
    line = lax.axis_index("shard")
    core = group % 2
    plane = group // 2
    col, row = plane % 2, plane // 2
    parity = line % 2
    where = jnp.stack([core, plane, line, parity]).astype(jnp.int32)

    vecs = [bias_q, bias_v, bias_out, gain_attn, shift_attn, bias_down, gain_ffn, shift_ffn, bias_up]
    moves = []
    slab_at = lambda c, p, z, e: p * slab_part
    for idx in range(3):
        at = lambda c, p, z, e, idx=idx: idx * width + c * half
        moves.append((0, slab_at, at, slab_part, half, 0, 0, idx * half))
    (qkv_piece,) = pack_blocks(
        where, [w_qkv], vecs, moves, [(slab_part + vec_rows, 3 * half)], (0, slab_part), slab
    )
    qkv_parts = along_line(qkv_piece)
    moves = []
    for idx in range(2):
        moves.append((idx, lambda c, p, z, e: e * quarter, 0, quarter, width, 2 * idx, 0, 0))
        moves.append((idx, lambda c, p, z, e: (1 - e) * quarter, 0, quarter, width, 2 * idx + 1, 0, 0))
    for idx in range(4):
        at = lambda c, p, z, e, idx=idx: idx * wide + c * (wide // 2)
        moves.append((2, slab_at, at, slab_part, wide // 2, 4, 0, idx * (wide // 2)))
    moves.append((3, slab_at, lambda c, p, z, e: c * half, slab_part, half, 4, 0, units))
    moves.append((4, lambda c, p, z, e: c * (wide // 2) + p * wide_part, 0, wide_part, width, 5, 0, 0))
    tok_first, tok_second, cot_first, cot_second, up_piece, down_piece = move_blocks(
        where,
        [after(tokens.reshape(half_rows, width), qkv_parts[0]), cotangent.reshape(half_rows, width), w_up, w_out, w_down],
        moves,
        [(quarter, width)] * 4 + [(slab_part, units + half), (wide_part, width)],
        grant=GRANT,
    )
    slab_start = lambda c, p, z, e: z * slab

    stack = lambda parts: join_blocks(where, parts)
    len_other = swap_core(lengths)
    len_all = jnp.where(core == 0, jnp.concatenate([lengths, len_other]), jnp.concatenate([len_other, lengths]))
    seq_len = len_all[line]
    place = lax.broadcasted_iota(jnp.int32, (4 * quarter, 128), 0)
    place = ((place // quarter) ^ (2 * core + parity)) * quarter + place % quarter
    bias = jnp.where(place < seq_len, 0.0, masked_score).astype(F32)
    tok_first, tok_second = send_rows(tok_first, tok_second)
    qkv_came = stack(after(qkv_parts, bias, down_piece))
    qkv_plane = across_plane(qkv_came)
    vec_block, qkv_bias, up_bias = join_vectors(where, qkv_piece, qkv_came, slab_part, slab, width)
    tok_own = stack(after([tok_first, tok_second], vec_block, *qkv_plane))
    up_parts = along_line(after(up_piece, tok_own))
    tok_all = stack([tok_own, swap_core(tok_own)])

    moves = []
    for idx in range(3):
        at = lambda c, p, z, e, idx=idx: idx * width + c * half
        moves.append((0, 0, at, slab, half, 0, slab_start, idx * half))
    moves += placed_moves(1, slab_part + vec_rows, slab_part, 0, 3 * half, 0)
    (qkv_weight,) = move_blocks(
        where, [w_qkv, after(qkv_came, vec_block)] + qkv_plane, moves, [(width, 3 * half)]
    )

    qkv = (dot32(tok_all, qkv_weight) + qkv_bias).astype(BF)
    pairs = half // PAIR
    contexts, lses = [], []
    for pair in range(pairs):
        qkv_in = after(qkv, contexts[-1]) if contexts else qkv
        if pair == 1:
            up_came = stack(after(up_parts, contexts[0]))
            up_plane = across_plane(up_came)
            down_far = swap_z(after(down_piece, up_came), 2)
            cot_first = send_first(after(cot_first, up_came))
            qkv_in = after(qkv, up_came)
        elif pair == 2:
            down_two = stack(after([down_piece, down_far], contexts[1]))
            down_near = swap_z(down_two, 1)
            cot_second = send_second(after(cot_second, down_two))
            qkv_in = after(qkv, down_two)
        got = attend_chip_forward(qkv_in, bias, pair)
        contexts.append(got[0])
        lses.append(got[1])
    context = jnp.concatenate(contexts, axis=1)
    down_near = after(down_near, context)
    down_came = stack([down_near[:wide_part], down_far, down_near[wide_part:]])
    cot_own = stack(after([cot_first, cot_second], down_came))

    moves = []
    for idx in range(4):
        at = lambda c, p, z, e, idx=idx: idx * wide + c * (wide // 2)
        moves.append((0, 0, at, slab, wide // 2, 0, slab_start, idx * (wide // 2)))
    moves.append((1, 0, lambda c, p, z, e: c * half, slab, half, 1, slab_start, 0))
    moves += placed_moves(2, slab_part, slab_part, 0, units, 0)
    moves += placed_moves(2, slab_part, slab_part, units, half, 1)
    up_weight, out_half = move_blocks(
        where,
        [w_up, w_out, after(up_came, down_came, cot_own)] + up_plane,
        moves,
        [(width, units), (width, half)],
    )
    out_got = swap_core(out_half)
    down_plane = across_plane(after(down_came, out_half))
    moves = [
        (0, lambda c, p, z, e: c * half, 0, half, half, 0, 0, lambda c, p, z, e: c * half),
        (1, lambda c, p, z, e: c * half, 0, half, half, 0, 0, lambda c, p, z, e: (1 - c) * half),
    ]
    (out_weight,) = move_blocks(where, [out_half, out_got], moves, [(half, width)])
    part = dot32(context, out_weight).astype(BF)
    got = swap_core(part)
    hidden_low, n_one, r_one, act, slope = ffn_up(part, got, tok_all, vec_block, up_bias, up_weight)

    cot_all = stack([cot_own, swap_core(cot_own)])
    moves = [
        (0, 0, 0, 4 * quarter, half, 0, 0, lambda c, p, z, e: c * half),
        (1, 0, 0, half_rows, half, 0, half_rows, lambda c, p, z, e: (1 - c) * half),
        (1, half_rows, 0, half_rows, half, 0, 0, lambda c, p, z, e: (1 - c) * half),
    ]
    (context_all,) = move_blocks(
        where, [context, swap_core(after(context, cot_own))], moves, [(4 * quarter, width)]
    )
    moves = [(0, lambda c, p, z, e: c * (wide // 2), 0, wide // 2, width, 0, lambda c, p, z, e: z * (wide // 2), 0)]
    moves += placed_moves(1, wide_part, wide_part, 0, width, 0)
    (down_weight,) = move_blocks(where, [w_down, after(down_came, act, cot_all, context_all)] + down_plane, moves, [(units, width)])
    part = dot32(act, down_weight).astype(BF)
    out_first, out_second, dr_two, dffn, sums_two = norm_turn(
        part, swap_core(part), n_one, cot_all, bias, vec_block
    )

    blocks = lambda grad: grad.reshape(4, 2, 2, grad.shape[0] // 16, grad.shape[1])
    g_down = contract_rows(act, dffn).astype(BF)
    down_state, sent = reduce_first([blocks(g_down)], wide_part // 2, col, row)
    dffn = after(dffn, sent)
    dup, part, up_sums = ffn_back(dffn, down_weight, slope, up_weight)
    got = swap_core(part)
    dup_late = after(dup, part)
    g_up = contract_rows(hidden_low, dup_late).astype(BF)
    up_state, sent_up = reduce_first([blocks(g_up)], slab_part // 2, col, row)
    dr_one, dattn, dattn_part, sums_one = norm_one_back(
        where, dr_two, part, after(got, sent_up), n_one, r_one, vec_block
    )
    grad_ctx = contract_cols(dattn, out_weight).astype(BF)
    g_out = contract_rows(context_all, after(dattn_part, grad_ctx)).astype(BF)
    down_state, sent = reduce_second(after(down_state, g_out), col, row)
    layer_first = return_block(after(out_first, g_down), 0)
    layer_second = return_block(after(out_second, layer_first, g_out), 1)

    dqkv = []
    side = lambda parts: jnp.concatenate(parts, axis=1)
    qkv_in = after(qkv, sent)
    dqkv.append(attend_chip_backward(qkv_in, bias, lses[0], grad_ctx, 0))
    layer_out = join_rows(*after((layer_first, layer_second), dqkv[-1]), parity)
    down_state, sent = reduce_near([after(down_state, layer_out)], line)
    up_state, sent_up = reduce_second(after(up_state, sent), col, row)
    qkv_in = after(qkv, sent_up)
    for pair in range(1, pairs - 1):
        dqkv.append(attend_chip_backward(qkv_in, bias, lses[pair], grad_ctx, pair))
    most = side([part[idx] for idx in range(3) for part in dqkv])
    g_most = contract_rows(tok_all, most).astype(BF)
    most_state, sent = reduce_first([blocks(g_most), blocks(g_out)], slab_part // 2, col, row)
    down_state, sent = reduce_far(after(down_state, sent), line)
    up_state, sent_up = reduce_near([after(up_state, sent)], line)
    qkv_in = after(qkv, sent_up)
    dqkv.append(attend_chip_backward(qkv_in, bias, lses[-1], grad_ctx, pairs - 1))
    most_state, sent = reduce_second(after(most_state, dqkv[-1]), col, row)
    last = side(dqkv[-1])
    g_last = contract_rows(tok_all, after(last, sent)).astype(BF)
    dqkv = side([part[idx] for idx in range(3) for part in dqkv])
    qkv_sums = jnp.sum(dqkv.astype(F32), axis=0, keepdims=True)
    small = small_grads(where, sums_one, sums_two, up_sums, qkv_sums, slab)
    small = jnp.pad(small[:, None, None], ((0, 0), (0, 1), (0, 1), (0, 0), (0, 0)))
    last_state, sent = reduce_first([blocks(g_last), small], slab_part // 2, col, row)
    down_state = spread_first(after(down_state, sent), True)
    up_state, sent_up = reduce_far(after(up_state, down_state[0]), line)
    dqkv = after(dqkv, sent_up)
    dtok_low = contract_cols(dqkv[half_rows:], qkv_weight).astype(BF)
    dtok_got = swap_core(dtok_low)
    grad_tok = contract_cols(after(dqkv[:half_rows], dtok_low), qkv_weight) + dr_one
    last_state, sent = reduce_second(after(last_state, grad_tok), col, row)
    down_state = spread_second(after(down_state, sent), True)
    grad_tok = (after(grad_tok, down_state[0]) + dtok_got.astype(F32)).astype(BF)
    back_first = return_block(grad_tok[:quarter], 0)
    up_state = spread_first(after(up_state, grad_tok), False)
    attn_state, sent = reduce_near([most_state, after(last_state, up_state[0])], line)
    down_state = spread_core(after(down_state, sent))
    up_state = spread_second(after(up_state, down_state[0]), False)
    attn_state, sent = reduce_far(after(attn_state, up_state[0], back_first), line)
    back_second = return_block(after(grad_tok[quarter:], sent), 1)
    up_state = spread_core(after(up_state, sent))
    down_layout = lambda half_at: [(0, width, 0, lambda part: half_at * (wide // 2) + part * wide_part, 0)]
    (grad_down,) = finish_grad(where, after(down_state, up_state[0]), True, down_layout, wide_part, [(wide, width)])
    slab_row = lambda part: part * slab_part
    up_layout = lambda half_at: [
        (idx * (wide // 2), wide // 2, 0, slab_row, idx * wide + half_at * (wide // 2)) for idx in range(4)
    ]
    (grad_up,) = finish_grad(
        where, after(up_state, grad_down), False, up_layout, slab_part, [(slab, 2 * units)]
    )
    attn_state, sent = direct_spread(after(attn_state, grad_up))
    attn_state = spread_core(attn_state)
    span = half - PAIR
    attn_layout = lambda half_at: (
        [(idx * span, span, 0, slab_row, idx * width + half_at * half) for idx in range(3)]
        + [(3 * span, half, 1, slab_row, half_at * half)]
        + [
            (3 * span + half + idx * PAIR, PAIR, 0, slab_row, idx * width + half_at * half + span)
            for idx in range(3)
        ]
    )
    grad_qkv, grad_out, *vec_grads = finish_grad(
        where, after(attn_state, grad_up), True, attn_layout, slab_part, [(slab, 3 * width), (slab, width)], 4 * half
    )
    grad_tokens = join_rows(*after((back_first, back_second), grad_qkv), parity)
    vec_of = lambda idx: vec_grads[idx]
    return (
        layer_out,
        grad_tokens,
        grad_qkv,
        vec_of(0),
        vec_of(1),
        grad_out,
        vec_of(2),
        vec_of(3),
        vec_of(4),
        grad_up,
        vec_of(8),
        grad_down,
        vec_of(5),
        vec_of(6),
        vec_of(7),
    )


def solution(mesh):
    placed = (
        P("grp", "shard", None),
        P("grp", "shard", None),
        P("grp"),
        P("shard", None),
        P("shard"),
        P("shard"),
        P("shard", None),
        P("shard"),
        P("shard"),
        P("shard"),
        P("shard", None),
        P("shard"),
        P("shard", None),
        P("shard"),
        P("shard"),
        P("shard"),
    )
    plan = per_device_chip if dict(mesh.shape) == {"grp": 8, "shard": 4} else per_device
    return jax.shard_map(
        plan,
        mesh=mesh,
        in_specs=placed,
        out_specs=(
            P("grp", "shard", None),
            P("grp", "shard", None),
            P("shard", None),
            P("shard"),
            P("shard"),
            P("shard", None),
            P("shard"),
            P("shard"),
            P("shard"),
            P("shard", None),
            P("shard"),
            P("shard", None),
            P("shard"),
            P("shard"),
            P("shard"),
        ),
        check_vma=False,
    )
```

```python
import functools
import math

import jax
import jax.numpy as jnp
from jax import lax
from jax.experimental import pallas as pl
from jax.experimental.pallas import tpu as pltpu
from jax.sharding import PartitionSpec as P


H = 12
HD = 64


eps = 1e-12
masked_score = -1000000000.0


def layer_norm(values_in, gain_vec, shift_vec):
    row_mean = jnp.mean(values_in, axis=-1, keepdims=True)
    centered = values_in - row_mean
    variance = jnp.mean(centered * centered, axis=-1, keepdims=True)
    return centered * lax.rsqrt(variance + eps) * gain_vec + shift_vec


def gelu_exact(values_in):
    return jax.nn.gelu(values_in, approximate=False)


def contract_cols(left_mat, right_mat):
    return lax.dot_general(
        left_mat, right_mat, (((1,), (1,)), ((), ())), preferred_element_type=jnp.float32
    )


def contract_rows(left_mat, right_mat):
    return lax.dot_general(
        left_mat, right_mat, (((0,), (0,)), ((), ())), preferred_element_type=jnp.float32
    )


def column_sums(matrix):
    return jnp.sum(matrix.astype(jnp.float32), axis=0)


def unpack(weights_full):
    (
        qkv_weight,
        query_bias,
        value_bias,
        out_weight,
        out_bias,
        gain_one,
        shift_one,
        up_weight,
        up_bias,
        down_weight,
        down_bias,
        gain_two,
        shift_two,
    ) = weights_full
    as_float = lambda vector: vector.astype(jnp.float32)
    return (
        qkv_weight,
        as_float(query_bias),
        as_float(value_bias),
        out_weight,
        as_float(out_bias),
        as_float(gain_one),
        as_float(shift_one),
        up_weight,
        as_float(up_bias),
        down_weight,
        as_float(down_bias),
        as_float(gain_two),
        as_float(shift_two),
    )


def head_scores(queries, keys, key_mask, head_idx):
    col_start = head_idx * HD
    q_head = lax.dynamic_slice_in_dim(queries, col_start, HD, 1)
    k_head = lax.dynamic_slice_in_dim(keys, col_start, HD, 1)
    scores = contract_cols(q_head, k_head) * HD ** (-0.5)
    return (q_head, k_head, jnp.where(key_mask[None, :], scores, masked_score))


def attend_forward(queries, keys, values, key_mask):
    row_count, width = queries.shape

    def one_head(head_idx, carry):
        context, lse_rows = carry
        q_head, k_head, scores = head_scores(queries, keys, key_mask, head_idx)
        v_head = lax.dynamic_slice_in_dim(values, head_idx * HD, HD, 1)
        row_max = jnp.max(scores, axis=1, keepdims=True)
        exp_scores = jnp.exp(scores - row_max)
        row_total = jnp.sum(exp_scores, axis=1, keepdims=True)
        prob_low = (exp_scores / row_total).astype(jnp.bfloat16)
        head_out = jnp.dot(prob_low, v_head, preferred_element_type=jnp.float32)
        context = lax.dynamic_update_slice_in_dim(context, head_out, head_idx * HD, 1)
        lse_rows = lax.dynamic_update_slice_in_dim(
            lse_rows, row_max + jnp.log(row_total), head_idx, 1
        )
        return (context, lse_rows)

    start_state = (
        jnp.zeros((row_count, width), jnp.float32),
        jnp.zeros((row_count, H), jnp.float32),
    )
    return lax.fori_loop(0, H, one_head, start_state)


def attend_backward(queries, keys, values, key_mask, lse_rows, grad_context):
    row_count, width = queries.shape
    slot_count = keys.shape[0]

    def one_head(head_idx, carry):
        grad_q, grad_k, grad_v = carry
        col_start = head_idx * HD
        q_head, k_head, scores = head_scores(queries, keys, key_mask, head_idx)
        v_head = lax.dynamic_slice_in_dim(values, col_start, HD, 1)
        grad_head = lax.dynamic_slice_in_dim(grad_context, col_start, HD, 1)
        probs = jnp.exp(scores - lax.dynamic_slice_in_dim(lse_rows, head_idx, 1, 1))
        grad_probs = contract_cols(grad_head, v_head)
        delta = jnp.sum(probs * grad_probs, axis=1, keepdims=True)
        grad_scores = (probs * (grad_probs - delta)).astype(jnp.bfloat16)
        head_gq = jnp.dot(grad_scores, k_head, preferred_element_type=jnp.float32) * HD ** (-0.5)
        head_gk = contract_rows(grad_scores, q_head) * HD ** (-0.5)
        head_gv = contract_rows(probs.astype(jnp.bfloat16), grad_head)
        grad_q = lax.dynamic_update_slice_in_dim(grad_q, head_gq, col_start, 1)
        grad_k = lax.dynamic_update_slice_in_dim(grad_k, head_gk, col_start, 1)
        grad_v = lax.dynamic_update_slice_in_dim(grad_v, head_gv, col_start, 1)
        return (grad_q, grad_k, grad_v)

    start_state = (
        jnp.zeros((row_count, width), jnp.float32),
        jnp.zeros((slot_count, width), jnp.float32),
        jnp.zeros((slot_count, width), jnp.float32),
    )
    return lax.fori_loop(0, H, one_head, start_state)


def per_device(
    tokens,
    cotangent,
    lengths,
    w_qkv,
    bias_q,
    bias_v,
    w_out,
    bias_out,
    gain_attn,
    shift_attn,
    w_up,
    bias_up,
    w_down,
    bias_down,
    gain_ffn,
    shift_ffn,
):
    batch_count, row_count, width = tokens.shape
    dev_count = lax.axis_size("shard")
    slot_count = row_count * dev_count
    first_row = lax.axis_index("shard") * row_count
    key_place = jnp.arange(slot_count, dtype=jnp.int32)
    row_place = first_row + jnp.arange(row_count, dtype=jnp.int32)
    sharded = (
        w_qkv,
        bias_q,
        bias_v,
        w_out,
        bias_out,
        gain_attn,
        shift_attn,
        w_up,
        bias_up,
        w_down,
        bias_down,
        gain_ffn,
        shift_ffn,
    )
    totals = [
        jnp.zeros((piece.shape[0] * dev_count,) + piece.shape[1:], jnp.float32) for piece in sharded
    ]
    layer_rows = []
    grad_rows = []
    for batch_idx in range(batch_count):
        weights_full = unpack(
            (
                lax.all_gather(w_qkv, "shard", axis=0, tiled=True),
                lax.all_gather(bias_q, "shard", axis=0, tiled=True),
                lax.all_gather(bias_v, "shard", axis=0, tiled=True),
                lax.all_gather(w_out, "shard", axis=0, tiled=True),
                lax.all_gather(bias_out, "shard", axis=0, tiled=True),
                lax.all_gather(gain_attn, "shard", axis=0, tiled=True),
                lax.all_gather(shift_attn, "shard", axis=0, tiled=True),
                lax.all_gather(w_up, "shard", axis=0, tiled=True),
                lax.all_gather(bias_up, "shard", axis=0, tiled=True),
                lax.all_gather(w_down, "shard", axis=0, tiled=True),
                lax.all_gather(bias_down, "shard", axis=0, tiled=True),
                lax.all_gather(gain_ffn, "shard", axis=0, tiled=True),
                lax.all_gather(shift_ffn, "shard", axis=0, tiled=True),
            )
        )
        (
            qkv_weight,
            query_bias,
            value_bias,
            out_weight,
            out_bias,
            gain_one,
            shift_one,
            up_weight,
            up_bias,
            down_weight,
            down_bias,
            gain_two,
            shift_two,
        ) = weights_full
        seq_in = tokens[batch_idx]
        seq_len = lengths[batch_idx]
        key_mask = key_place < seq_len
        own_valid = row_place < seq_len
        row_mask = own_valid.astype(jnp.float32)[:, None]
        qkv_bias = jnp.concatenate([query_bias, jnp.zeros_like(query_bias), value_bias])
        qkv_low = (
            jnp.dot(seq_in, qkv_weight, preferred_element_type=jnp.float32) + qkv_bias
        ).astype(jnp.bfloat16)
        queries = qkv_low[:, :width]
        key_part = qkv_low[:, width : 2 * width]
        value_part = qkv_low[:, 2 * width :]
        keys_all, values_all = (
            lax.all_gather(key_part, "shard", axis=0, tiled=True),
            lax.all_gather(value_part, "shard", axis=0, tiled=True),
        )
        context, lse_rows = attend_forward(queries, keys_all, values_all, key_mask)
        context_low = context.astype(jnp.bfloat16)
        attn_out = jnp.dot(context_low, out_weight, preferred_element_type=jnp.float32) + out_bias
        hidden, norm_one_back = jax.vjp(
            layer_norm, seq_in.astype(jnp.float32) + attn_out, gain_one, shift_one
        )
        hidden_low = hidden.astype(jnp.bfloat16)
        up_proj = jnp.dot(hidden_low, up_weight, preferred_element_type=jnp.float32) + up_bias
        activation, gelu_back = jax.vjp(gelu_exact, up_proj)
        act_low = activation.astype(jnp.bfloat16)
        ffn_out = jnp.dot(act_low, down_weight, preferred_element_type=jnp.float32) + down_bias
        normed, norm_two_back = jax.vjp(layer_norm, hidden + ffn_out, gain_two, shift_two)
        layer_rows.append((normed * row_mask).astype(jnp.bfloat16))
        weights_full = unpack(
            (
                lax.all_gather(w_qkv, "shard", axis=0, tiled=True),
                lax.all_gather(bias_q, "shard", axis=0, tiled=True),
                lax.all_gather(bias_v, "shard", axis=0, tiled=True),
                lax.all_gather(w_out, "shard", axis=0, tiled=True),
                lax.all_gather(bias_out, "shard", axis=0, tiled=True),
                lax.all_gather(gain_attn, "shard", axis=0, tiled=True),
                lax.all_gather(shift_attn, "shard", axis=0, tiled=True),
                lax.all_gather(w_up, "shard", axis=0, tiled=True),
                lax.all_gather(bias_up, "shard", axis=0, tiled=True),
                lax.all_gather(w_down, "shard", axis=0, tiled=True),
                lax.all_gather(bias_down, "shard", axis=0, tiled=True),
                lax.all_gather(gain_ffn, "shard", axis=0, tiled=True),
                lax.all_gather(shift_ffn, "shard", axis=0, tiled=True),
            )
        )
        (
            qkv_weight,
            query_bias,
            value_bias,
            out_weight,
            out_bias,
            gain_one,
            shift_one,
            up_weight,
            up_bias,
            down_weight,
            down_bias,
            gain_two,
            shift_two,
        ) = weights_full
        grad_out = cotangent[batch_idx].astype(jnp.float32) * row_mask
        grad_res_two, grad_gain_two, grad_shift_two = norm_two_back(grad_out)
        grad_ffn_low = grad_res_two.astype(jnp.bfloat16)
        grad_act = contract_cols(grad_ffn_low, down_weight)
        (grad_up,) = gelu_back(grad_act)
        grad_up_low = grad_up.astype(jnp.bfloat16)
        grad_hidden = grad_res_two + contract_cols(grad_up_low, up_weight)
        grad_res_one, grad_gain_one, grad_shift_one = norm_one_back(grad_hidden)
        grad_attn_low = grad_res_one.astype(jnp.bfloat16)
        grad_ctx_low = contract_cols(grad_attn_low, out_weight).astype(jnp.bfloat16)
        keys_all, values_all = (
            lax.all_gather(key_part, "shard", axis=0, tiled=True),
            lax.all_gather(value_part, "shard", axis=0, tiled=True),
        )
        grad_q, grad_keys_all, grad_values_all = attend_backward(
            queries, keys_all, values_all, key_mask, lse_rows, grad_ctx_low
        )
        grad_keys, grad_values = (
            lax.psum_scatter(
                grad_keys_all.astype(jnp.bfloat16), "shard", scatter_dimension=0, tiled=True
            ).astype(jnp.float32),
            lax.psum_scatter(
                grad_values_all.astype(jnp.bfloat16), "shard", scatter_dimension=0, tiled=True
            ).astype(jnp.float32),
        )
        grad_qkv_low = jnp.concatenate([grad_q, grad_keys, grad_values], axis=1).astype(
            jnp.bfloat16
        )
        grad_input = grad_res_one + contract_cols(grad_qkv_low, qkv_weight)
        grad_rows.append(grad_input.astype(jnp.bfloat16))
        terms = (
            contract_rows(seq_in, grad_qkv_low),
            column_sums(grad_qkv_low[:, :width]),
            column_sums(grad_qkv_low[:, 2 * width :]),
            contract_rows(context_low, grad_attn_low),
            column_sums(grad_attn_low),
            grad_gain_one,
            grad_shift_one,
            contract_rows(hidden_low, grad_up_low),
            column_sums(grad_up_low),
            contract_rows(act_low, grad_ffn_low),
            column_sums(grad_ffn_low),
            grad_gain_two,
            grad_shift_two,
        )
        totals = [running + fresh for running, fresh in zip(totals, terms)]
    grad_local = (
        lax.psum_scatter(
            totals[0].astype(jnp.bfloat16), "shard", scatter_dimension=0, tiled=True
        ).astype(jnp.float32),
        lax.psum_scatter(
            totals[1].astype(jnp.bfloat16), "shard", scatter_dimension=0, tiled=True
        ).astype(jnp.float32),
        lax.psum_scatter(
            totals[2].astype(jnp.bfloat16), "shard", scatter_dimension=0, tiled=True
        ).astype(jnp.float32),
        lax.psum_scatter(
            totals[3].astype(jnp.bfloat16), "shard", scatter_dimension=0, tiled=True
        ).astype(jnp.float32),
        lax.psum_scatter(
            totals[4].astype(jnp.bfloat16), "shard", scatter_dimension=0, tiled=True
        ).astype(jnp.float32),
        lax.psum_scatter(
            totals[5].astype(jnp.bfloat16), "shard", scatter_dimension=0, tiled=True
        ).astype(jnp.float32),
        lax.psum_scatter(
            totals[6].astype(jnp.bfloat16), "shard", scatter_dimension=0, tiled=True
        ).astype(jnp.float32),
        lax.psum_scatter(
            totals[7].astype(jnp.bfloat16), "shard", scatter_dimension=0, tiled=True
        ).astype(jnp.float32),
        lax.psum_scatter(
            totals[8].astype(jnp.bfloat16), "shard", scatter_dimension=0, tiled=True
        ).astype(jnp.float32),
        lax.psum_scatter(
            totals[9].astype(jnp.bfloat16), "shard", scatter_dimension=0, tiled=True
        ).astype(jnp.float32),
        lax.psum_scatter(
            totals[10].astype(jnp.bfloat16), "shard", scatter_dimension=0, tiled=True
        ).astype(jnp.float32),
        lax.psum_scatter(
            totals[11].astype(jnp.bfloat16), "shard", scatter_dimension=0, tiled=True
        ).astype(jnp.float32),
        lax.psum_scatter(
            totals[12].astype(jnp.bfloat16), "shard", scatter_dimension=0, tiled=True
        ).astype(jnp.float32),
    )
    grad_total = (
        lax.psum(grad_local[0].astype(jnp.bfloat16), "grp").astype(jnp.float32),
        lax.psum(grad_local[1].astype(jnp.bfloat16), "grp").astype(jnp.float32),
        lax.psum(grad_local[2].astype(jnp.bfloat16), "grp").astype(jnp.float32),
        lax.psum(grad_local[3].astype(jnp.bfloat16), "grp").astype(jnp.float32),
        lax.psum(grad_local[4].astype(jnp.bfloat16), "grp").astype(jnp.float32),
        lax.psum(grad_local[5].astype(jnp.bfloat16), "grp").astype(jnp.float32),
        lax.psum(grad_local[6].astype(jnp.bfloat16), "grp").astype(jnp.float32),
        lax.psum(grad_local[7].astype(jnp.bfloat16), "grp").astype(jnp.float32),
        lax.psum(grad_local[8].astype(jnp.bfloat16), "grp").astype(jnp.float32),
        lax.psum(grad_local[9].astype(jnp.bfloat16), "grp").astype(jnp.float32),
        lax.psum(grad_local[10].astype(jnp.bfloat16), "grp").astype(jnp.float32),
        lax.psum(grad_local[11].astype(jnp.bfloat16), "grp").astype(jnp.float32),
        lax.psum(grad_local[12].astype(jnp.bfloat16), "grp").astype(jnp.float32),
    )
    return (
        jnp.stack(layer_rows),
        jnp.stack(grad_rows),
        grad_total[0],
        grad_total[1],
        grad_total[2],
        grad_total[3],
        grad_total[4],
        grad_total[5],
        grad_total[6],
        grad_total[7],
        grad_total[8],
        grad_total[9],
        grad_total[10],
        grad_total[11],
        grad_total[12],
    )


BF = jnp.bfloat16
GRANT = 60 << 20
COST = pl.CostEstimate(flops=1024, bytes_accessed=1024, transcendentals=0)
F32 = jnp.float32


def swap_core(value):
    return lax.ppermute(value, "grp", [(i, i ^ 1) for i in range(8)])


def swap_x(value):
    return lax.ppermute(value, "grp", [(i, i ^ 2) for i in range(8)])


def swap_y(value):
    return lax.ppermute(value, "grp", [(i, i ^ 4) for i in range(8)])


def swap_z(value, flip):
    return lax.ppermute(value, "shard", [(i, i ^ flip) for i in range(4)])


def swap_xy(value):
    return lax.ppermute(value, "grp", [(i, i ^ 6) for i in range(8)])


def dot32(left_mat, right_mat):
    return jnp.dot(left_mat, right_mat, preferred_element_type=F32)


def after(values, *others):
    return lax.optimization_barrier((values, others))[0]


def sequence_perm(flip):
    pairs = []
    for grp in range(8):
        for line in range(4):
            dst_grp = (grp & 6) | (line // 2)
            dst_line = 2 * (grp & 1) + ((line % 2) ^ flip)
            pairs.append((grp * 4 + line, dst_grp * 4 + dst_line))
    return pairs


def send_first(block):
    return lax.ppermute(block, ("grp", "shard"), sequence_perm(0))


def send_second(block):
    return lax.ppermute(block, ("grp", "shard"), sequence_perm(1))


def send_rows(first, second):
    return send_first(first), send_second(second)


def return_block(block, flip):
    return lax.ppermute(block, ("grp", "shard"), [(dst, src) for src, dst in sequence_perm(flip)])


def return_rows(first, second):
    return return_block(first, 0), return_block(second, 1)


def join_rows(first, second, parity):
    return jnp.where(parity == 0, jnp.stack([first, second]), jnp.stack([second, first]))


CORE, PLANE, LINE, PARITY = range(4)


def start_moves(moves, where_ref, sources, targets, sems):
    where = [where_ref[idx] for idx in range(4)]
    place = lambda at, unit: at if isinstance(at, int) else pl.multiple_of(at(*where), unit)
    copies = []
    for idx, (src, src_row, src_col, rows, cols, dst, dst_row, dst_col) in enumerate(moves):
        copies.append(
            pltpu.make_async_copy(
                sources[src].at[pl.ds(place(src_row, 8), rows), pl.ds(place(src_col, 128), cols)],
                targets[dst].at[pl.ds(place(dst_row, 8), rows), pl.ds(place(dst_col, 128), cols)],
                sems.at[idx],
            )
        )
    for copy in copies:
        copy.start()
    return copies


def move_kernel(count, moves, where_ref, *refs):
    for copy in start_moves(moves, where_ref, refs[:count], refs[count:-1], refs[-1]):
        copy.wait()


def move_blocks(where, sources, moves, shapes, grant=16 << 20):
    moved = sum(move[3] * move[4] for move in moves) * 2
    return pl.pallas_call(
        functools.partial(move_kernel, len(sources), moves),
        out_shape=[jax.ShapeDtypeStruct(shape, sources[0].dtype) for shape in shapes],
        in_specs=[pl.BlockSpec(memory_space=pltpu.SMEM)]
        + [pl.BlockSpec(memory_space=pl.ANY)] * len(sources),
        out_specs=[pl.BlockSpec(memory_space=pltpu.VMEM)] * len(shapes),
        scratch_shapes=[pltpu.SemaphoreType.DMA((len(moves),))],
        cost_estimate=COST,
        compiler_params=pltpu.CompilerParams(vmem_limit_bytes=grant),
    )(where, *sources)


def join_blocks(where, parts):
    moves, at = [], 0
    for idx, part in enumerate(parts):
        moves.append((idx, 0, 0, part.shape[0], part.shape[1], 0, at, 0))
        at += part.shape[0]
    return move_blocks(where, list(parts), moves, [(at, parts[0].shape[1])])[0]


def along_line(piece):
    return [swap_z(piece, flip) for flip in (1, 2, 3)]


def across_plane(came):
    return [swap_x(came), swap_y(came), swap_xy(came)]


def placed_moves(first_src, height, piece_rows, col, cols, dst):
    moves = []
    for flip in range(4):
        for step in range(1, 4):
            at = lambda core, plane, line, parity, flip=flip, step=step: (
                (line ^ step) * (4 * piece_rows) + (plane ^ flip) * piece_rows
            )
            moves.append((first_src + flip, (step - 1) * height, col, piece_rows, cols, dst, at, 0))
    return moves


def pick(arr, idx, axis):
    return lax.dynamic_index_in_dim(arr, idx, axis, keepdims=False)


def add_low(left, right):
    return (left.astype(F32) + right.astype(F32)).astype(BF)


def reduce_first(grads, cut, col, row):
    join = lambda arrs: arrs[0] if len(arrs) == 1 else jnp.concatenate(arrs, axis=-1)
    low_part = lambda idx: join([pick(grad[:, :, :, :cut], idx, 2) for grad in grads])
    high_part = lambda idx: join([pick(grad[:, :, :, cut:], idx, 1) for grad in grads])
    sent = (low_part(1 - col), high_part(1 - row))
    return (low_part(col), high_part(row), swap_x(sent[0]), swap_y(sent[1])), sent


def reduce_second(state, col, row):
    low, high, low_got, high_got = state
    low, high = add_low(low, low_got), add_low(high, high_got)
    sent = (pick(low, 1 - row, 1), pick(high, 1 - col, 1))
    return (pick(low, row, 1), pick(high, col, 1), swap_y(sent[0]), swap_x(sent[1])), sent


def reduce_near(states, line):
    mine = [
        jnp.concatenate([add_low(low, low_got), add_low(high, high_got)], axis=1)
        for low, high, low_got, high_got in states
    ]
    mine = mine[0] if len(mine) == 1 else jnp.concatenate(mine, axis=-1)
    pairs = mine.reshape((2, 2) + mine.shape[1:])
    sent = pick(pairs, 1 - line % 2, 1)
    return (pick(pairs, line % 2, 1), swap_z(sent, 1)), sent


def reduce_far(state, line):
    mine = add_low(*state)
    sent = pick(mine, 1 - line // 2, 0)
    return (pick(mine, line // 2, 0), swap_z(sent, 2)), sent


def direct_spread(state):
    piece = sum(part.astype(F32) for part in state).astype(BF)
    return [piece] + across_plane(piece), piece


def final_kernel(layout, rows, extra, flips, where_ref, mine_ref, other_ref, *outs):
    plane = where_ref[PLANE]
    height = mine_ref.shape[0] // 4

    low = where_ref[CORE] == 0
    for half in range(2):
        for at in range(4):
            part = plane ^ flips[at]
            for src_col, cols, dst, row_of, dst_col in layout(half):
                row = pl.multiple_of(row_of(part), 16)
                here = (pl.ds(at * height, rows), pl.ds(src_col, cols))
                mine, other = mine_ref[here], other_ref[here]
                value = jnp.where(low, mine, other) if half == 0 else jnp.where(low, other, mine)
                outs[dst][pl.ds(row, rows), pl.ds(dst_col, cols)] = value.astype(F32)
    if extra is not None:
        vecs = outs[-9:]
        slab = vecs[0].shape[0]
        for at in range(4):

            @pl.when(plane == flips[at])
            def _(at=at):
                begin, end = [
                    mine_ref[here, pl.ds(extra, 128)].astype(F32) + other_ref[here, pl.ds(extra, 128)].astype(F32)
                    for here in (pl.ds(at * height, 16), pl.ds(at * height + 16, 16))
                ]
                both = jnp.concatenate([begin, end], axis=1)
                for idx in range(8):
                    vecs[idx][...] = both[idx : idx + 1, :slab].reshape(slab)
                spread = jnp.concatenate([both, jnp.zeros((16, 4 * slab - 256), F32)], axis=1)
                lane = lax.broadcasted_iota(jnp.int32, spread.shape, 1)
                spread = jnp.where(lane < slab, spread, 0.0)
                wide = spread[8:9]
                for part in range(1, 4):
                    wide += pltpu.roll(spread[8 + part : 9 + part], part * slab, 1)
                vecs[8][...] = wide.reshape(4 * slab)


def spread_first(state, through_x):
    piece = add_low(*state)
    return piece, (swap_x if through_x else swap_y)(piece)


def spread_second(state, through_x):
    both = jnp.concatenate(state, axis=0)
    return both, (swap_y if through_x else swap_x)(both)


def spread_core(state):
    mine = jnp.concatenate(state, axis=0)
    return mine, swap_core(mine)


def finish_grad(where, state, through_x, layout, rows, shapes, extra=None):
    mine, other = state
    mine_flips = (0, 1, 2, 3) if through_x else (0, 2, 1, 3)
    shapes = list(shapes) + ([] if extra is None else [(shapes[0][0],)] * 8 + [(4 * shapes[0][0],)])
    vmem = pl.BlockSpec(memory_space=pltpu.VMEM)
    return pl.pallas_call(
        functools.partial(final_kernel, layout, rows, extra, mine_flips),
        out_shape=[jax.ShapeDtypeStruct(shape, F32) for shape in shapes],
        in_specs=[pl.BlockSpec(memory_space=pltpu.SMEM), vmem, vmem],
        out_specs=[vmem] * len(shapes),
        cost_estimate=COST,
        compiler_params=pltpu.CompilerParams(vmem_limit_bytes=16 << 20),
    )(where, mine, other)


ROWS = 256


def row_spec(width, shift=0, steps=1, block=ROWS):
    if shift:
        return pl.BlockSpec((block, width), lambda blk: ((blk + shift) % steps, 0))
    return pl.BlockSpec((block, width), lambda blk: (blk, 0))


def whole_spec(rows, width):
    return pl.BlockSpec((rows, width), lambda blk: (0, 0))


def mean_last(values):
    return jnp.mean(values, axis=-1, keepdims=True)


def norm_parts(values):
    centered = values - mean_last(values)
    scale = lax.rsqrt(mean_last(centered * centered) + eps)
    return centered * scale, scale


def norm_back(grad_normed, normed, scale):
    return scale * (grad_normed - mean_last(grad_normed) - normed * mean_last(grad_normed * normed))


def up_kernel(part_ref, got_ref, tok_ref, vec_ref, bias_ref, w_ref, low_ref, n_ref, r_ref, act_ref, slope_ref):
    vec = vec_ref[...]
    attn_out = part_ref[...].astype(F32) + got_ref[...].astype(F32) + vec[0:1]
    normed, scale = norm_parts(tok_ref[...].astype(F32) + attn_out)
    hidden = (normed * vec[1:2] + vec[2:3]).astype(BF)
    n_ref[...] = normed
    r_ref[...] = jnp.broadcast_to(scale, r_ref.shape)
    low_ref[...] = hidden
    for at in range(0, w_ref.shape[1], 384):
        cols = pl.ds(at, 384)
        up = dot32(hidden, w_ref[:, cols]) + bias_ref[:, cols]
        cdf = 0.5 + 0.5 * lax.erf(up * 0.5**0.5)
        act_ref[:, cols] = (up * cdf).astype(BF)
        slope = cdf + up * (jnp.exp(up * up * -0.5) * (2 * math.pi) ** -0.5)
        slope_ref[:, cols] = slope.astype(BF)


def ffn_up(part, got, tokens, vectors, up_bias, weight):
    rows, width = part.shape
    units = weight.shape[1]
    block = ROWS // 2
    steps = rows // block
    return pl.pallas_call(
        up_kernel,
        grid=(steps,),
        out_shape=[
            jax.ShapeDtypeStruct((rows, width), BF),
            jax.ShapeDtypeStruct((rows, width), F32),
            jax.ShapeDtypeStruct((rows, 128), F32),
            jax.ShapeDtypeStruct((rows, units), BF),
            jax.ShapeDtypeStruct((rows, units), BF),
        ],
        in_specs=[
            row_spec(width, block=block),
            row_spec(width, steps // 2, steps, block=block),
            row_spec(width, block=block),
            whole_spec(8, width),
            whole_spec(1, units),
            whole_spec(width, units),
        ],
        out_specs=[row_spec(width, block=block), row_spec(width, block=block), row_spec(128, block=block), row_spec(units, block=block), row_spec(units, block=block)],
        cost_estimate=COST,
        compiler_params=pltpu.CompilerParams(vmem_limit_bytes=20 << 20),
    )(part, got, tokens, vectors, up_bias, weight)


def turn_kernel(
    half_steps, part_ref, got_ref, n_ref, cot_ref, bias_ref, vec_ref, first_ref, second_ref, dr_ref, low_ref, sum_ref
):
    blk = pl.program_id(0)
    vec = vec_ref[...]
    hidden = n_ref[...] * vec[1:2] + vec[2:3]
    ffn_out = part_ref[...].astype(F32) + got_ref[...].astype(F32) + vec[3:4]
    normed, scale = norm_parts(hidden + ffn_out)
    mask = jnp.where(bias_ref[:, 0:1] < 0.0, 0.0, 1.0)
    result = ((normed * vec[4:5] + vec[5:6]) * mask).astype(BF)
    dy = cot_ref[...].astype(F32) * mask
    dr = norm_back(dy * vec[4:5], normed, scale)
    dr_low = dr.astype(BF)
    dr_ref[...] = dr
    low_ref[...] = dr_low

    @pl.when(blk == 0)
    def _():
        sum_ref[...] = jnp.zeros_like(sum_ref)
        first_ref[...] = result

    @pl.when(blk == 1)
    def _():
        second_ref[...] = result

    @pl.when(blk < half_steps)
    def _():
        sum_ref[0:1] += jnp.sum(dy * normed, axis=0, keepdims=True)
        sum_ref[1:2] += jnp.sum(dy, axis=0, keepdims=True)
        sum_ref[2:3] += jnp.sum(dr_low.astype(F32), axis=0, keepdims=True)


def norm_turn(part, got, n_one, cot, bias, vectors):
    rows, width = part.shape
    steps = rows // ROWS
    return pl.pallas_call(
        functools.partial(turn_kernel, steps // 2),
        grid=(steps,),
        out_shape=[jax.ShapeDtypeStruct((ROWS, width), BF)] * 2
        + [
            jax.ShapeDtypeStruct((rows, width), F32),
            jax.ShapeDtypeStruct((rows, width), BF),
            jax.ShapeDtypeStruct((8, width), F32),
        ],
        in_specs=[
            row_spec(width),
            row_spec(width, steps // 2, steps),
            row_spec(width),
            row_spec(width),
            row_spec(128),
            whole_spec(8, width),
        ],
        out_specs=[whole_spec(ROWS, width)] * 2 + [row_spec(width), row_spec(width), whole_spec(8, width)],
        cost_estimate=COST,
        compiler_params=pltpu.CompilerParams(vmem_limit_bytes=28 << 20),
    )(part, got, n_one, cot, bias, vectors)


def ffn_back_kernel(dffn_ref, down_ref, slope_ref, up_ref, dup_ref, part_ref, sum_ref):
    @pl.when(pl.program_id(0) == 0)
    def _():
        sum_ref[...] = jnp.zeros_like(sum_ref)

    total = jnp.zeros(part_ref.shape, F32)
    dffn = dffn_ref[...]
    for at in range(0, dup_ref.shape[1], 512):
        here = pl.ds(at, 512)
        dup = (contract_cols(dffn, down_ref[here, :]) * slope_ref[:, here].astype(F32)).astype(BF)
        dup_ref[:, here] = dup
        sum_ref[:, here] += jnp.sum(dup.astype(F32), axis=0, keepdims=True)
        total += contract_cols(dup, up_ref[:, here])
    part_ref[...] = total.astype(BF)


def ffn_back(dffn, down_weight, slope, up_weight):
    rows, width = dffn.shape
    units = slope.shape[1]
    return pl.pallas_call(
        ffn_back_kernel,
        grid=(rows // ROWS,),
        out_shape=[
            jax.ShapeDtypeStruct((rows, units), BF),
            jax.ShapeDtypeStruct((rows, width), BF),
            jax.ShapeDtypeStruct((1, units), F32),
        ],
        in_specs=[row_spec(width), whole_spec(units, width), row_spec(units), whole_spec(width, units)],
        out_specs=[row_spec(units), row_spec(width), whole_spec(1, units)],
        cost_estimate=COST,
        compiler_params=pltpu.CompilerParams(vmem_limit_bytes=20 << 20),
    )(dffn, down_weight, slope, up_weight)


def back_kernel(
    half_steps, where_ref, dr_ref, part_ref, got_ref, n_ref, r_ref, vec_ref, own_ref, low_ref, part_low_ref, sum_ref
):
    blk = pl.program_id(0)
    vec = vec_ref[...]
    normed = n_ref[...]
    dhidden = dr_ref[...] + (part_ref[...].astype(F32) + got_ref[...].astype(F32))
    dr = norm_back(dhidden * vec[1:2], normed, r_ref[:, 0:1])
    dr_low = dr.astype(BF)
    low_ref[...] = dr_low
    half = dr.shape[1] // 2
    part_low_ref[...] = jnp.where(where_ref[CORE] == 0, dr_low[:, :half], dr_low[:, half:])

    @pl.when(blk == 0)
    def _():
        sum_ref[...] = jnp.zeros_like(sum_ref)

    @pl.when(blk < half_steps)
    def _():
        own_ref[...] = dr
        sum_ref[0:1] += jnp.sum(dhidden * normed, axis=0, keepdims=True)
        sum_ref[1:2] += jnp.sum(dhidden, axis=0, keepdims=True)
        sum_ref[2:3] += jnp.sum(dr_low.astype(F32), axis=0, keepdims=True)


def norm_one_back(where, dr_two, part, got, n_one, r_one, vectors):
    rows, width = part.shape
    steps = rows // ROWS
    return pl.pallas_call(
        functools.partial(back_kernel, steps // 2),
        grid=(steps,),
        out_shape=[
            jax.ShapeDtypeStruct((rows // 2, width), F32),
            jax.ShapeDtypeStruct((rows, width), BF),
            jax.ShapeDtypeStruct((rows, width // 2), BF),
            jax.ShapeDtypeStruct((8, width), F32),
        ],
        in_specs=[
            pl.BlockSpec(memory_space=pltpu.SMEM),
            row_spec(width),
            row_spec(width),
            row_spec(width, steps // 2, steps),
            row_spec(width),
            row_spec(128),
            whole_spec(8, width),
        ],
        out_specs=[
            pl.BlockSpec((ROWS, width), lambda blk: (jnp.minimum(blk, steps // 2 - 1), 0)),
            row_spec(width),
            row_spec(width // 2),
            whole_spec(8, width),
        ],
        cost_estimate=COST,
        compiler_params=pltpu.CompilerParams(vmem_limit_bytes=28 << 20),
    )(where, dr_two, part, got, n_one, r_one, vectors)


Q_BLOCK = 512
PAIR = 128


def contract_last(left_mat, right_mat):
    return lax.dot_general(
        left_mat, right_mat, (((1,), (1,)), ((), ())), preferred_element_type=F32
    )


def head_lanes(block, head):
    lane = lax.broadcasted_iota(jnp.int32, block.shape, 1)
    return jnp.where((lane // HD) == head, block, jnp.zeros_like(block))


def attend_fwd_kernel(q_ref, k_ref, v_ref, bias_ref, ctx_ref, lse_ref, vt_ref, out_ref):
    vt_ref[...] = v_ref[...].T

    @pl.loop(0, q_ref.shape[0] // Q_BLOCK)
    def _(blk):
        at = pl.multiple_of(blk * Q_BLOCK, Q_BLOCK)

        @pl.loop(0, 2)
        def _(head):
            q_blk = q_ref[pl.ds(at, Q_BLOCK), :] * jnp.asarray(HD ** (-0.5), BF)
            here = pl.ds(pl.multiple_of(head * HD, HD), HD)
            scores = contract_last(k_ref[...], head_lanes(q_blk, head))
            scores = scores + jnp.concatenate([bias_ref[...]] * (Q_BLOCK // 128), axis=1)
            top = jnp.max(scores, axis=0, keepdims=True)
            exps = jnp.exp(scores - top)
            total = jnp.sum(exps, axis=0, keepdims=True)
            out_ref[here, :] = dot32(vt_ref[here, :], exps.astype(BF)) * (1.0 / total)
            lse_ref[0, pl.ds(head, 1), pl.ds(at, Q_BLOCK)] = top + jnp.log(total)

        ctx_ref[pl.ds(at, Q_BLOCK), :] = out_ref[...].T.astype(BF)


def attend_bwd_kernel(
    q_ref, k_ref, v_ref, bias_ref, lse_ref, grad_ref, dq_ref, dk_ref, dv_ref, kt_ref, dk_acc, dv_acc, out_ref
):
    kt_ref[...] = k_ref[...].T
    dk_acc[...] = jnp.zeros_like(dk_acc)
    dv_acc[...] = jnp.zeros_like(dv_acc)

    @pl.loop(0, q_ref.shape[0] // Q_BLOCK)
    def _(blk):
        at = pl.multiple_of(blk * Q_BLOCK, Q_BLOCK)

        @pl.loop(0, 2)
        def _(head):
            q_head = head_lanes(q_ref[pl.ds(at, Q_BLOCK), :] * jnp.asarray(HD ** (-0.5), BF), head)
            grad_head = head_lanes(grad_ref[pl.ds(at, Q_BLOCK), :], head)
            here = pl.ds(pl.multiple_of(head * HD, HD), HD)
            scores = contract_last(k_ref[...], q_head)
            scores = scores + jnp.concatenate([bias_ref[...]] * (Q_BLOCK // 128), axis=1)
            probs = jnp.exp(scores - lse_ref[0, pl.ds(head, 1), pl.ds(at, Q_BLOCK)])
            weighed = probs * contract_last(v_ref[...], grad_head)
            delta = jnp.sum(weighed, axis=0, keepdims=True)
            grad_scores = (weighed - probs * delta).astype(BF)
            dk_acc[...] += dot32(grad_scores, q_head)
            dv_acc[...] += dot32(probs.astype(BF), grad_head)
            out_ref[here, :] = dot32(kt_ref[here, :], grad_scores)

        dq_ref[pl.ds(at, Q_BLOCK), :] = (out_ref[...].T * (HD ** (-0.5))).astype(BF)

    dk_ref[...] = dk_acc[...].astype(BF)
    dv_ref[...] = dv_acc[...].astype(BF)


def column_spec(rows, first):
    return pl.BlockSpec((rows, PAIR), lambda pair: (0, first + pair))


def attend_chip_forward(qkv, bias, pair):
    rows, half = qkv.shape[0], qkv.shape[1] // 3
    pairs = half // PAIR
    return pl.pallas_call(
        attend_fwd_kernel,
        grid=(1,),
        out_shape=[
            jax.ShapeDtypeStruct((rows, PAIR), BF),
            jax.ShapeDtypeStruct((1, 2, rows), F32),
        ],
        in_specs=[column_spec(rows, idx * pairs + pair) for idx in range(3)]
        + [pl.BlockSpec((rows, 128), lambda step: (0, 0))],
        out_specs=[column_spec(rows, 0), pl.BlockSpec((1, 2, rows), lambda step: (0, 0, 0))],
        scratch_shapes=[pltpu.VMEM((PAIR, rows), BF), pltpu.VMEM((PAIR, Q_BLOCK), F32)],
        cost_estimate=COST,
        compiler_params=pltpu.CompilerParams(vmem_limit_bytes=28 << 20),
    )(qkv, qkv, qkv, bias)


def attend_chip_backward(qkv, bias, lse, grad_ctx, pair):
    rows, half = qkv.shape[0], qkv.shape[1] // 3
    pairs = half // PAIR
    return pl.pallas_call(
        attend_bwd_kernel,
        grid=(1,),
        out_shape=[jax.ShapeDtypeStruct((rows, PAIR), BF)] * 3,
        in_specs=[column_spec(rows, idx * pairs + pair) for idx in range(3)]
        + [
            pl.BlockSpec((rows, 128), lambda step: (0, 0)),
            pl.BlockSpec((1, 2, rows), lambda step: (0, 0, 0)),
            column_spec(rows, pair),
        ],
        out_specs=[column_spec(rows, 0)] * 3,
        scratch_shapes=[
            pltpu.VMEM((PAIR, rows), BF),
            pltpu.VMEM((rows, PAIR), F32),
            pltpu.VMEM((rows, PAIR), F32),
            pltpu.VMEM((PAIR, Q_BLOCK), F32),
        ],
        cost_estimate=COST,
        compiler_params=pltpu.CompilerParams(vmem_limit_bytes=32 << 20),
    )(qkv, qkv, qkv, bias, lse, grad_ctx)


def pack_kernel(count, moves, vec_at, slab, where_ref, *refs):
    sources, vecs = refs[:count], refs[count : count + 9]
    targets, sems = refs[count + 9 : -1], refs[-1]
    copies = start_moves(moves, where_ref, sources, targets, sems)
    dst, row = vec_at
    width = targets[dst].shape[1]
    rows = [vec[...].reshape(1, slab).astype(F32) for vec in vecs[:8]]
    wide = vecs[8][...].reshape(1, -1).astype(F32)
    count_wide = wide.shape[1] // slab
    rows += [wide[:, :slab]]
    rows += [pltpu.roll(wide, wide.shape[1] - idx * slab, 1)[:, :slab] for idx in range(1, count_wide)]
    rows += [jnp.zeros((4, slab), F32)]
    block = jnp.concatenate(rows, axis=0)
    targets[dst][pl.ds(row, 16), :] = jnp.concatenate(
        [block, jnp.zeros((16, width - slab), F32)], axis=1
    ).astype(BF)
    for copy in copies:
        copy.wait()


def pack_blocks(where, sources, vecs, moves, shapes, vec_at, slab):
    return pl.pallas_call(
        functools.partial(pack_kernel, len(sources), moves, vec_at, slab),
        out_shape=[jax.ShapeDtypeStruct(shape, BF) for shape in shapes],
        in_specs=[pl.BlockSpec(memory_space=pltpu.SMEM)]
        + [pl.BlockSpec(memory_space=pl.ANY)] * len(sources)
        + [pl.BlockSpec(memory_space=pltpu.VMEM)] * len(vecs),
        out_specs=[pl.BlockSpec(memory_space=pltpu.VMEM)] * len(shapes),
        scratch_shapes=[pltpu.SemaphoreType.DMA((len(moves),))],
        cost_estimate=COST,
        compiler_params=pltpu.CompilerParams(vmem_limit_bytes=60 << 20),
    )(where, *sources, *vecs)


def vector_kernel(height, at, slab, where_ref, own_ref, came_ref, block_ref, qkv_ref, up_ref, buf, sems):
    line = where_ref[LINE]
    copies = [pltpu.make_async_copy(own_ref.at[pl.ds(at, 16)], buf.at[line], sems.at[0])]
    for step in range(1, 4):
        copies.append(
            pltpu.make_async_copy(
                came_ref.at[pl.ds((step - 1) * height + at, 16)], buf.at[line ^ step], sems.at[step]
            )
        )
    for copy in copies:
        copy.start()
    for copy in copies:
        copy.wait()
    width = block_ref.shape[1]
    half = width // 2
    joined = jnp.zeros((16, width), F32)
    lane = lax.broadcasted_iota(jnp.int32, (16, width), 1)
    wide = []
    for idx in range(4):
        rows = jnp.where(lane < slab, buf[idx, :, :width].astype(F32), 0.0)
        joined += rows if idx == 0 else pltpu.roll(rows, idx * slab, 1)
        row = rows[8:9]
        for part in range(1, 4):
            row += pltpu.roll(rows[8 + part : 9 + part], part * slab, 1)
        wide.append(row)
    low = where_ref[CORE] == 0
    pick_half = lambda row: jnp.where(low, row[:, :half], row[:, half:])
    block_ref[...] = jnp.concatenate([joined[2:8], jnp.zeros((2, width), F32)], axis=0)
    qkv_ref[...] = jnp.concatenate(
        [pick_half(joined[0:1]), jnp.zeros((1, half), F32), pick_half(joined[1:2])], axis=1
    )
    up_ref[...] = jnp.concatenate([pick_half(row) for row in wide], axis=1)


def join_vectors(where, own, came, at, slab, width):
    height = came.shape[0] // 3
    return pl.pallas_call(
        functools.partial(vector_kernel, height, at, slab),
        out_shape=[
            jax.ShapeDtypeStruct((8, width), F32),
            jax.ShapeDtypeStruct((1, 3 * width // 2), F32),
            jax.ShapeDtypeStruct((1, 2 * width), F32),
        ],
        in_specs=[pl.BlockSpec(memory_space=pltpu.SMEM)] + [pl.BlockSpec(memory_space=pl.ANY)] * 2,
        out_specs=[pl.BlockSpec(memory_space=pltpu.VMEM)] * 3,
        scratch_shapes=[pltpu.VMEM((4, 16, own.shape[1]), BF), pltpu.SemaphoreType.DMA((4,))],
        cost_estimate=COST,
        compiler_params=pltpu.CompilerParams(vmem_limit_bytes=4 << 20),
    )(where, own, came)


def small_kernel(slab, where_ref, one_ref, two_ref, up_ref, qkv_ref, out_ref):
    width = one_ref.shape[1]
    half = width // 2
    low = where_ref[CORE] == 0
    zero = jnp.zeros((1, half), F32)
    on_core = lambda row: jnp.where(
        low, jnp.concatenate([row, zero], axis=1), jnp.concatenate([zero, row], axis=1)
    )
    one, two = one_ref[...], two_ref[...]
    rows = jnp.concatenate(
        [
            on_core(qkv_ref[:, :half]),
            on_core(qkv_ref[:, 2 * half :]),
            one[2:3],
            one[0:1],
            one[1:2],
            two[2:3],
            two[0:1],
            two[1:2],
        ],
        axis=0,
    )
    out_ref[...] = jnp.zeros_like(out_ref)
    for idx in range(4):
        wide = on_core(up_ref[:, idx * half : (idx + 1) * half])
        at = lambda row, part: row if part == 0 else pltpu.roll(row, width - part * slab, 1)
        parts = [at(wide, part)[:, :256] for part in range(4)]
        block = jnp.concatenate([at(rows, idx)[:, :256]] + parts + [jnp.zeros((4, 256), F32)], axis=0)
        lane = lax.broadcasted_iota(jnp.int32, block.shape, 1)
        block = jnp.where(lane < slab, block, 0.0).astype(BF)
        out_ref[idx, 0:16, :] = block[:, :128]
        out_ref[idx, 16:32, :] = block[:, 128:]


def small_grads(where, sums_one, sums_two, up_sums, qkv_sums, slab):
    vmem = pl.BlockSpec(memory_space=pltpu.VMEM)
    return pl.pallas_call(
        functools.partial(small_kernel, slab),
        out_shape=jax.ShapeDtypeStruct((4, slab // 4, 128), BF),
        in_specs=[pl.BlockSpec(memory_space=pltpu.SMEM)] + [vmem] * 4,
        out_specs=vmem,
        compiler_params=pltpu.CompilerParams(vmem_limit_bytes=4 << 20),
    )(where, sums_one, sums_two, up_sums, qkv_sums)


def per_device_chip(
    tokens,
    cotangent,
    lengths,
    w_qkv,
    bias_q,
    bias_v,
    w_out,
    bias_out,
    gain_attn,
    shift_attn,
    w_up,
    bias_up,
    w_down,
    bias_down,
    gain_ffn,
    shift_ffn,
):
    quarter, width = tokens.shape[1:]
    half_rows = 2 * quarter
    units = w_up.shape[1] // 2
    slab = w_qkv.shape[0]
    wide = w_down.shape[0]
    half = width // 2
    slab_part, wide_part = slab // 4, wide // 8
    vec_rows = 16
    group = lax.axis_index("grp")
    line = lax.axis_index("shard")
    core = group % 2
    plane = group // 2
    col, row = plane % 2, plane // 2
    parity = line % 2
    where = jnp.stack([core, plane, line, parity]).astype(jnp.int32)

    vecs = [bias_q, bias_v, bias_out, gain_attn, shift_attn, bias_down, gain_ffn, shift_ffn, bias_up]
    moves = []
    slab_at = lambda c, p, z, e: p * slab_part
    for idx in range(3):
        at = lambda c, p, z, e, idx=idx: idx * width + c * half
        moves.append((0, slab_at, at, slab_part, half, 0, 0, idx * half))
    (qkv_piece,) = pack_blocks(
        where, [w_qkv], vecs, moves, [(slab_part + vec_rows, 3 * half)], (0, slab_part), slab
    )
    qkv_parts = along_line(qkv_piece)
    moves = []
    for idx in range(2):
        moves.append((idx, lambda c, p, z, e: e * quarter, 0, quarter, width, 2 * idx, 0, 0))
        moves.append((idx, lambda c, p, z, e: (1 - e) * quarter, 0, quarter, width, 2 * idx + 1, 0, 0))
    for idx in range(4):
        at = lambda c, p, z, e, idx=idx: idx * wide + c * (wide // 2)
        moves.append((2, slab_at, at, slab_part, wide // 2, 4, 0, idx * (wide // 2)))
    moves.append((3, slab_at, lambda c, p, z, e: c * half, slab_part, half, 4, 0, units))
    moves.append((4, lambda c, p, z, e: c * (wide // 2) + p * wide_part, 0, wide_part, width, 5, 0, 0))
    tok_first, tok_second, cot_first, cot_second, up_piece, down_piece = move_blocks(
        where,
        [after(tokens.reshape(half_rows, width), qkv_parts[0]), cotangent.reshape(half_rows, width), w_up, w_out, w_down],
        moves,
        [(quarter, width)] * 4 + [(slab_part, units + half), (wide_part, width)],
        grant=GRANT,
    )
    slab_start = lambda c, p, z, e: z * slab

    stack = lambda parts: join_blocks(where, parts)
    len_other = swap_core(lengths)
    len_all = jnp.where(core == 0, jnp.concatenate([lengths, len_other]), jnp.concatenate([len_other, lengths]))
    seq_len = len_all[line]
    place = lax.broadcasted_iota(jnp.int32, (4 * quarter, 128), 0)
    place = ((place // quarter) ^ (2 * core + parity)) * quarter + place % quarter
    bias = jnp.where(place < seq_len, 0.0, masked_score).astype(F32)
    tok_first, tok_second = send_rows(tok_first, tok_second)
    qkv_came = stack(after(qkv_parts, bias, down_piece))
    qkv_plane = across_plane(qkv_came)
    vec_block, qkv_bias, up_bias = join_vectors(where, qkv_piece, qkv_came, slab_part, slab, width)
    tok_own = stack(after([tok_first, tok_second], vec_block, *qkv_plane))
    up_parts = along_line(after(up_piece, tok_own))
    tok_all = stack([tok_own, swap_core(tok_own)])

    moves = []
    for idx in range(3):
        at = lambda c, p, z, e, idx=idx: idx * width + c * half
        moves.append((0, 0, at, slab, half, 0, slab_start, idx * half))
    moves += placed_moves(1, slab_part + vec_rows, slab_part, 0, 3 * half, 0)
    (qkv_weight,) = move_blocks(
        where, [w_qkv, after(qkv_came, vec_block)] + qkv_plane, moves, [(width, 3 * half)]
    )

    qkv = (dot32(tok_all, qkv_weight) + qkv_bias).astype(BF)
    pairs = half // PAIR
    contexts, lses = [], []
    for pair in range(pairs):
        qkv_in = after(qkv, contexts[-1]) if contexts else qkv
        if pair == 1:
            up_came = stack(after(up_parts, contexts[0]))
            up_plane = across_plane(up_came)
            down_far = swap_z(after(down_piece, up_came), 2)
            cot_first = send_first(after(cot_first, up_came))
            qkv_in = after(qkv, up_came)
        elif pair == 2:
            down_two = stack(after([down_piece, down_far], contexts[1]))
            down_near = swap_z(down_two, 1)
            cot_second = send_second(after(cot_second, down_two))
            qkv_in = after(qkv, down_two)
        got = attend_chip_forward(qkv_in, bias, pair)
        contexts.append(got[0])
        lses.append(got[1])
    context = jnp.concatenate(contexts, axis=1)
    down_near = after(down_near, context)
    down_came = stack([down_near[:wide_part], down_far, down_near[wide_part:]])
    cot_own = stack(after([cot_first, cot_second], down_came))

    moves = []
    for idx in range(4):
        at = lambda c, p, z, e, idx=idx: idx * wide + c * (wide // 2)
        moves.append((0, 0, at, slab, wide // 2, 0, slab_start, idx * (wide // 2)))
    moves.append((1, 0, lambda c, p, z, e: c * half, slab, half, 1, slab_start, 0))
    moves += placed_moves(2, slab_part, slab_part, 0, units, 0)
    moves += placed_moves(2, slab_part, slab_part, units, half, 1)
    up_weight, out_half = move_blocks(
        where,
        [w_up, w_out, after(up_came, down_came, cot_own)] + up_plane,
        moves,
        [(width, units), (width, half)],
    )
    out_got = swap_core(out_half)
    down_plane = across_plane(after(down_came, out_half))
    moves = [
        (0, lambda c, p, z, e: c * half, 0, half, half, 0, 0, lambda c, p, z, e: c * half),
        (1, lambda c, p, z, e: c * half, 0, half, half, 0, 0, lambda c, p, z, e: (1 - c) * half),
    ]
    (out_weight,) = move_blocks(where, [out_half, out_got], moves, [(half, width)])
    part = dot32(context, out_weight).astype(BF)
    got = swap_core(part)
    hidden_low, n_one, r_one, act, slope = ffn_up(part, got, tok_all, vec_block, up_bias, up_weight)

    cot_all = stack([cot_own, swap_core(cot_own)])
    moves = [
        (0, 0, 0, 4 * quarter, half, 0, 0, lambda c, p, z, e: c * half),
        (1, 0, 0, half_rows, half, 0, half_rows, lambda c, p, z, e: (1 - c) * half),
        (1, half_rows, 0, half_rows, half, 0, 0, lambda c, p, z, e: (1 - c) * half),
    ]
    (context_all,) = move_blocks(
        where, [context, swap_core(after(context, cot_own))], moves, [(4 * quarter, width)]
    )
    moves = [(0, lambda c, p, z, e: c * (wide // 2), 0, wide // 2, width, 0, lambda c, p, z, e: z * (wide // 2), 0)]
    moves += placed_moves(1, wide_part, wide_part, 0, width, 0)
    (down_weight,) = move_blocks(where, [w_down, after(down_came, act, cot_all, context_all)] + down_plane, moves, [(units, width)])
    part = dot32(act, down_weight).astype(BF)
    out_first, out_second, dr_two, dffn, sums_two = norm_turn(
        part, swap_core(part), n_one, cot_all, bias, vec_block
    )

    blocks = lambda grad: grad.reshape(4, 2, 2, grad.shape[0] // 16, grad.shape[1])
    g_down = contract_rows(act, dffn).astype(BF)
    down_state, sent = reduce_first([blocks(g_down)], wide_part // 2, col, row)
    dffn = after(dffn, sent)
    dup, part, up_sums = ffn_back(dffn, down_weight, slope, up_weight)
    got = swap_core(part)
    dup_late = after(dup, part)
    g_up = contract_rows(hidden_low, dup_late).astype(BF)
    up_state, sent_up = reduce_first([blocks(g_up)], slab_part // 2, col, row)
    dr_one, dattn, dattn_part, sums_one = norm_one_back(
        where, dr_two, part, after(got, sent_up), n_one, r_one, vec_block
    )
    grad_ctx = contract_cols(dattn, out_weight).astype(BF)
    g_out = contract_rows(context_all, after(dattn_part, grad_ctx)).astype(BF)
    down_state, sent = reduce_second(after(down_state, g_out), col, row)
    layer_first = return_block(after(out_first, g_down), 0)
    layer_second = return_block(after(out_second, layer_first, g_out), 1)

    dqkv = []
    side = lambda parts: jnp.concatenate(parts, axis=1)
    qkv_in = after(qkv, sent)
    dqkv.append(attend_chip_backward(qkv_in, bias, lses[0], grad_ctx, 0))
    layer_out = join_rows(*after((layer_first, layer_second), dqkv[-1]), parity)
    down_state, sent = reduce_near([after(down_state, layer_out)], line)
    up_state, sent_up = reduce_second(after(up_state, sent), col, row)
    qkv_in = after(qkv, sent_up)
    for pair in range(1, pairs - 1):
        dqkv.append(attend_chip_backward(qkv_in, bias, lses[pair], grad_ctx, pair))
    most = side([part[idx] for idx in range(3) for part in dqkv])
    g_most = contract_rows(tok_all, most).astype(BF)
    most_state, sent = reduce_first([blocks(g_most), blocks(g_out)], slab_part // 2, col, row)
    down_state, sent = reduce_far(after(down_state, sent), line)
    up_state, sent_up = reduce_near([after(up_state, sent)], line)
    qkv_in = after(qkv, sent_up)
    dqkv.append(attend_chip_backward(qkv_in, bias, lses[-1], grad_ctx, pairs - 1))
    most_state, sent = reduce_second(after(most_state, dqkv[-1]), col, row)
    last = side(dqkv[-1])
    g_last = contract_rows(tok_all, after(last, sent)).astype(BF)
    dqkv = side([part[idx] for idx in range(3) for part in dqkv])
    qkv_sums = jnp.sum(dqkv.astype(F32), axis=0, keepdims=True)
    small = small_grads(where, sums_one, sums_two, up_sums, qkv_sums, slab)
    small = jnp.pad(small[:, None, None], ((0, 0), (0, 1), (0, 1), (0, 0), (0, 0)))
    last_state, sent = reduce_first([blocks(g_last), small], slab_part // 2, col, row)
    down_state = spread_first(after(down_state, sent), True)
    up_state, sent_up = reduce_far(after(up_state, down_state[0]), line)
    dqkv = after(dqkv, sent_up)
    dtok_low = contract_cols(dqkv[half_rows:], qkv_weight).astype(BF)
    dtok_got = swap_core(dtok_low)
    grad_tok = contract_cols(after(dqkv[:half_rows], dtok_low), qkv_weight) + dr_one
    last_state, sent = reduce_second(after(last_state, grad_tok), col, row)
    down_state = spread_second(after(down_state, sent), True)
    grad_tok = (after(grad_tok, down_state[0]) + dtok_got.astype(F32)).astype(BF)
    back_first = return_block(grad_tok[:quarter], 0)
    up_state = spread_first(after(up_state, grad_tok), False)
    attn_state, sent = reduce_near([most_state, after(last_state, up_state[0])], line)
    down_state = spread_core(after(down_state, sent))
    up_state = spread_second(after(up_state, down_state[0]), False)
    attn_state, sent = reduce_far(after(attn_state, up_state[0], back_first), line)
    back_second = return_block(after(grad_tok[quarter:], sent), 1)
    up_state = spread_core(after(up_state, sent))
    down_layout = lambda half_at: [(0, width, 0, lambda part: half_at * (wide // 2) + part * wide_part, 0)]
    (grad_down,) = finish_grad(where, after(down_state, up_state[0]), True, down_layout, wide_part, [(wide, width)])
    slab_row = lambda part: part * slab_part
    up_layout = lambda half_at: [
        (idx * (wide // 2), wide // 2, 0, slab_row, idx * wide + half_at * (wide // 2)) for idx in range(4)
    ]
    (grad_up,) = finish_grad(
        where, after(up_state, grad_down), False, up_layout, slab_part, [(slab, 2 * units)]
    )
    attn_state, sent = direct_spread(after(attn_state, grad_up))
    grad_tokens = join_rows(*after((back_first, back_second), attn_state[1]), parity)
    attn_state = spread_core(after(attn_state, grad_tokens))
    span = half - PAIR
    attn_layout = lambda half_at: (
        [(idx * span, span, 0, slab_row, idx * width + half_at * half) for idx in range(3)]
        + [(3 * span, half, 1, slab_row, half_at * half)]
        + [
            (3 * span + half + idx * PAIR, PAIR, 0, slab_row, idx * width + half_at * half + span)
            for idx in range(3)
        ]
    )
    grad_qkv, grad_out, *vec_grads = finish_grad(
        where, after(attn_state, grad_up), True, attn_layout, slab_part, [(slab, 3 * width), (slab, width)], 4 * half
    )
    vec_of = lambda idx: vec_grads[idx]
    return (
        layer_out,
        grad_tokens,
        grad_qkv,
        vec_of(0),
        vec_of(1),
        grad_out,
        vec_of(2),
        vec_of(3),
        vec_of(4),
        grad_up,
        vec_of(8),
        grad_down,
        vec_of(5),
        vec_of(6),
        vec_of(7),
    )


def solution(mesh):
    placed = (
        P("grp", "shard", None),
        P("grp", "shard", None),
        P("grp"),
        P("shard", None),
        P("shard"),
        P("shard"),
        P("shard", None),
        P("shard"),
        P("shard"),
        P("shard"),
        P("shard", None),
        P("shard"),
        P("shard", None),
        P("shard"),
        P("shard"),
        P("shard"),
    )
    plan = per_device_chip if dict(mesh.shape) == {"grp": 8, "shard": 4} else per_device
    return jax.shard_map(
        plan,
        mesh=mesh,
        in_specs=placed,
        out_specs=(
            P("grp", "shard", None),
            P("grp", "shard", None),
            P("shard", None),
            P("shard"),
            P("shard"),
            P("shard", None),
            P("shard"),
            P("shard"),
            P("shard"),
            P("shard", None),
            P("shard"),
            P("shard", None),
            P("shard"),
            P("shard"),
            P("shard"),
        ),
        check_vma=False,
    )
```

```python
import functools
import math

import jax
import jax.numpy as jnp
from jax import lax
from jax.experimental import pallas as pl
from jax.experimental.pallas import tpu as pltpu
from jax.sharding import PartitionSpec as P


H = 12
HD = 64


eps = 1e-12
masked_score = -1000000000.0


def layer_norm(values_in, gain_vec, shift_vec):
    row_mean = jnp.mean(values_in, axis=-1, keepdims=True)
    centered = values_in - row_mean
    variance = jnp.mean(centered * centered, axis=-1, keepdims=True)
    return centered * lax.rsqrt(variance + eps) * gain_vec + shift_vec


def gelu_exact(values_in):
    return jax.nn.gelu(values_in, approximate=False)


def contract_cols(left_mat, right_mat):
    return lax.dot_general(
        left_mat, right_mat, (((1,), (1,)), ((), ())), preferred_element_type=jnp.float32
    )


def contract_rows(left_mat, right_mat):
    return lax.dot_general(
        left_mat, right_mat, (((0,), (0,)), ((), ())), preferred_element_type=jnp.float32
    )


def column_sums(matrix):
    return jnp.sum(matrix.astype(jnp.float32), axis=0)


def unpack(weights_full):
    (
        qkv_weight,
        query_bias,
        value_bias,
        out_weight,
        out_bias,
        gain_one,
        shift_one,
        up_weight,
        up_bias,
        down_weight,
        down_bias,
        gain_two,
        shift_two,
    ) = weights_full
    as_float = lambda vector: vector.astype(jnp.float32)
    return (
        qkv_weight,
        as_float(query_bias),
        as_float(value_bias),
        out_weight,
        as_float(out_bias),
        as_float(gain_one),
        as_float(shift_one),
        up_weight,
        as_float(up_bias),
        down_weight,
        as_float(down_bias),
        as_float(gain_two),
        as_float(shift_two),
    )


def head_scores(queries, keys, key_mask, head_idx):
    col_start = head_idx * HD
    q_head = lax.dynamic_slice_in_dim(queries, col_start, HD, 1)
    k_head = lax.dynamic_slice_in_dim(keys, col_start, HD, 1)
    scores = contract_cols(q_head, k_head) * HD ** (-0.5)
    return (q_head, k_head, jnp.where(key_mask[None, :], scores, masked_score))


def attend_forward(queries, keys, values, key_mask):
    row_count, width = queries.shape

    def one_head(head_idx, carry):
        context, lse_rows = carry
        q_head, k_head, scores = head_scores(queries, keys, key_mask, head_idx)
        v_head = lax.dynamic_slice_in_dim(values, head_idx * HD, HD, 1)
        row_max = jnp.max(scores, axis=1, keepdims=True)
        exp_scores = jnp.exp(scores - row_max)
        row_total = jnp.sum(exp_scores, axis=1, keepdims=True)
        prob_low = (exp_scores / row_total).astype(jnp.bfloat16)
        head_out = jnp.dot(prob_low, v_head, preferred_element_type=jnp.float32)
        context = lax.dynamic_update_slice_in_dim(context, head_out, head_idx * HD, 1)
        lse_rows = lax.dynamic_update_slice_in_dim(
            lse_rows, row_max + jnp.log(row_total), head_idx, 1
        )
        return (context, lse_rows)

    start_state = (
        jnp.zeros((row_count, width), jnp.float32),
        jnp.zeros((row_count, H), jnp.float32),
    )
    return lax.fori_loop(0, H, one_head, start_state)


def attend_backward(queries, keys, values, key_mask, lse_rows, grad_context):
    row_count, width = queries.shape
    slot_count = keys.shape[0]

    def one_head(head_idx, carry):
        grad_q, grad_k, grad_v = carry
        col_start = head_idx * HD
        q_head, k_head, scores = head_scores(queries, keys, key_mask, head_idx)
        v_head = lax.dynamic_slice_in_dim(values, col_start, HD, 1)
        grad_head = lax.dynamic_slice_in_dim(grad_context, col_start, HD, 1)
        probs = jnp.exp(scores - lax.dynamic_slice_in_dim(lse_rows, head_idx, 1, 1))
        grad_probs = contract_cols(grad_head, v_head)
        delta = jnp.sum(probs * grad_probs, axis=1, keepdims=True)
        grad_scores = (probs * (grad_probs - delta)).astype(jnp.bfloat16)
        head_gq = jnp.dot(grad_scores, k_head, preferred_element_type=jnp.float32) * HD ** (-0.5)
        head_gk = contract_rows(grad_scores, q_head) * HD ** (-0.5)
        head_gv = contract_rows(probs.astype(jnp.bfloat16), grad_head)
        grad_q = lax.dynamic_update_slice_in_dim(grad_q, head_gq, col_start, 1)
        grad_k = lax.dynamic_update_slice_in_dim(grad_k, head_gk, col_start, 1)
        grad_v = lax.dynamic_update_slice_in_dim(grad_v, head_gv, col_start, 1)
        return (grad_q, grad_k, grad_v)

    start_state = (
        jnp.zeros((row_count, width), jnp.float32),
        jnp.zeros((slot_count, width), jnp.float32),
        jnp.zeros((slot_count, width), jnp.float32),
    )
    return lax.fori_loop(0, H, one_head, start_state)


def per_device(
    tokens,
    cotangent,
    lengths,
    w_qkv,
    bias_q,
    bias_v,
    w_out,
    bias_out,
    gain_attn,
    shift_attn,
    w_up,
    bias_up,
    w_down,
    bias_down,
    gain_ffn,
    shift_ffn,
):
    batch_count, row_count, width = tokens.shape
    dev_count = lax.axis_size("shard")
    slot_count = row_count * dev_count
    first_row = lax.axis_index("shard") * row_count
    key_place = jnp.arange(slot_count, dtype=jnp.int32)
    row_place = first_row + jnp.arange(row_count, dtype=jnp.int32)
    sharded = (
        w_qkv,
        bias_q,
        bias_v,
        w_out,
        bias_out,
        gain_attn,
        shift_attn,
        w_up,
        bias_up,
        w_down,
        bias_down,
        gain_ffn,
        shift_ffn,
    )
    totals = [
        jnp.zeros((piece.shape[0] * dev_count,) + piece.shape[1:], jnp.float32) for piece in sharded
    ]
    layer_rows = []
    grad_rows = []
    for batch_idx in range(batch_count):
        weights_full = unpack(
            (
                lax.all_gather(w_qkv, "shard", axis=0, tiled=True),
                lax.all_gather(bias_q, "shard", axis=0, tiled=True),
                lax.all_gather(bias_v, "shard", axis=0, tiled=True),
                lax.all_gather(w_out, "shard", axis=0, tiled=True),
                lax.all_gather(bias_out, "shard", axis=0, tiled=True),
                lax.all_gather(gain_attn, "shard", axis=0, tiled=True),
                lax.all_gather(shift_attn, "shard", axis=0, tiled=True),
                lax.all_gather(w_up, "shard", axis=0, tiled=True),
                lax.all_gather(bias_up, "shard", axis=0, tiled=True),
                lax.all_gather(w_down, "shard", axis=0, tiled=True),
                lax.all_gather(bias_down, "shard", axis=0, tiled=True),
                lax.all_gather(gain_ffn, "shard", axis=0, tiled=True),
                lax.all_gather(shift_ffn, "shard", axis=0, tiled=True),
            )
        )
        (
            qkv_weight,
            query_bias,
            value_bias,
            out_weight,
            out_bias,
            gain_one,
            shift_one,
            up_weight,
            up_bias,
            down_weight,
            down_bias,
            gain_two,
            shift_two,
        ) = weights_full
        seq_in = tokens[batch_idx]
        seq_len = lengths[batch_idx]
        key_mask = key_place < seq_len
        own_valid = row_place < seq_len
        row_mask = own_valid.astype(jnp.float32)[:, None]
        qkv_bias = jnp.concatenate([query_bias, jnp.zeros_like(query_bias), value_bias])
        qkv_low = (
            jnp.dot(seq_in, qkv_weight, preferred_element_type=jnp.float32) + qkv_bias
        ).astype(jnp.bfloat16)
        queries = qkv_low[:, :width]
        key_part = qkv_low[:, width : 2 * width]
        value_part = qkv_low[:, 2 * width :]
        keys_all, values_all = (
            lax.all_gather(key_part, "shard", axis=0, tiled=True),
            lax.all_gather(value_part, "shard", axis=0, tiled=True),
        )
        context, lse_rows = attend_forward(queries, keys_all, values_all, key_mask)
        context_low = context.astype(jnp.bfloat16)
        attn_out = jnp.dot(context_low, out_weight, preferred_element_type=jnp.float32) + out_bias
        hidden, norm_one_back = jax.vjp(
            layer_norm, seq_in.astype(jnp.float32) + attn_out, gain_one, shift_one
        )
        hidden_low = hidden.astype(jnp.bfloat16)
        up_proj = jnp.dot(hidden_low, up_weight, preferred_element_type=jnp.float32) + up_bias
        activation, gelu_back = jax.vjp(gelu_exact, up_proj)
        act_low = activation.astype(jnp.bfloat16)
        ffn_out = jnp.dot(act_low, down_weight, preferred_element_type=jnp.float32) + down_bias
        normed, norm_two_back = jax.vjp(layer_norm, hidden + ffn_out, gain_two, shift_two)
        layer_rows.append((normed * row_mask).astype(jnp.bfloat16))
        weights_full = unpack(
            (
                lax.all_gather(w_qkv, "shard", axis=0, tiled=True),
                lax.all_gather(bias_q, "shard", axis=0, tiled=True),
                lax.all_gather(bias_v, "shard", axis=0, tiled=True),
                lax.all_gather(w_out, "shard", axis=0, tiled=True),
                lax.all_gather(bias_out, "shard", axis=0, tiled=True),
                lax.all_gather(gain_attn, "shard", axis=0, tiled=True),
                lax.all_gather(shift_attn, "shard", axis=0, tiled=True),
                lax.all_gather(w_up, "shard", axis=0, tiled=True),
                lax.all_gather(bias_up, "shard", axis=0, tiled=True),
                lax.all_gather(w_down, "shard", axis=0, tiled=True),
                lax.all_gather(bias_down, "shard", axis=0, tiled=True),
                lax.all_gather(gain_ffn, "shard", axis=0, tiled=True),
                lax.all_gather(shift_ffn, "shard", axis=0, tiled=True),
            )
        )
        (
            qkv_weight,
            query_bias,
            value_bias,
            out_weight,
            out_bias,
            gain_one,
            shift_one,
            up_weight,
            up_bias,
            down_weight,
            down_bias,
            gain_two,
            shift_two,
        ) = weights_full
        grad_out = cotangent[batch_idx].astype(jnp.float32) * row_mask
        grad_res_two, grad_gain_two, grad_shift_two = norm_two_back(grad_out)
        grad_ffn_low = grad_res_two.astype(jnp.bfloat16)
        grad_act = contract_cols(grad_ffn_low, down_weight)
        (grad_up,) = gelu_back(grad_act)
        grad_up_low = grad_up.astype(jnp.bfloat16)
        grad_hidden = grad_res_two + contract_cols(grad_up_low, up_weight)
        grad_res_one, grad_gain_one, grad_shift_one = norm_one_back(grad_hidden)
        grad_attn_low = grad_res_one.astype(jnp.bfloat16)
        grad_ctx_low = contract_cols(grad_attn_low, out_weight).astype(jnp.bfloat16)
        keys_all, values_all = (
            lax.all_gather(key_part, "shard", axis=0, tiled=True),
            lax.all_gather(value_part, "shard", axis=0, tiled=True),
        )
        grad_q, grad_keys_all, grad_values_all = attend_backward(
            queries, keys_all, values_all, key_mask, lse_rows, grad_ctx_low
        )
        grad_keys, grad_values = (
            lax.psum_scatter(
                grad_keys_all.astype(jnp.bfloat16), "shard", scatter_dimension=0, tiled=True
            ).astype(jnp.float32),
            lax.psum_scatter(
                grad_values_all.astype(jnp.bfloat16), "shard", scatter_dimension=0, tiled=True
            ).astype(jnp.float32),
        )
        grad_qkv_low = jnp.concatenate([grad_q, grad_keys, grad_values], axis=1).astype(
            jnp.bfloat16
        )
        grad_input = grad_res_one + contract_cols(grad_qkv_low, qkv_weight)
        grad_rows.append(grad_input.astype(jnp.bfloat16))
        terms = (
            contract_rows(seq_in, grad_qkv_low),
            column_sums(grad_qkv_low[:, :width]),
            column_sums(grad_qkv_low[:, 2 * width :]),
            contract_rows(context_low, grad_attn_low),
            column_sums(grad_attn_low),
            grad_gain_one,
            grad_shift_one,
            contract_rows(hidden_low, grad_up_low),
            column_sums(grad_up_low),
            contract_rows(act_low, grad_ffn_low),
            column_sums(grad_ffn_low),
            grad_gain_two,
            grad_shift_two,
        )
        totals = [running + fresh for running, fresh in zip(totals, terms)]
    grad_local = (
        lax.psum_scatter(
            totals[0].astype(jnp.bfloat16), "shard", scatter_dimension=0, tiled=True
        ).astype(jnp.float32),
        lax.psum_scatter(
            totals[1].astype(jnp.bfloat16), "shard", scatter_dimension=0, tiled=True
        ).astype(jnp.float32),
        lax.psum_scatter(
            totals[2].astype(jnp.bfloat16), "shard", scatter_dimension=0, tiled=True
        ).astype(jnp.float32),
        lax.psum_scatter(
            totals[3].astype(jnp.bfloat16), "shard", scatter_dimension=0, tiled=True
        ).astype(jnp.float32),
        lax.psum_scatter(
            totals[4].astype(jnp.bfloat16), "shard", scatter_dimension=0, tiled=True
        ).astype(jnp.float32),
        lax.psum_scatter(
            totals[5].astype(jnp.bfloat16), "shard", scatter_dimension=0, tiled=True
        ).astype(jnp.float32),
        lax.psum_scatter(
            totals[6].astype(jnp.bfloat16), "shard", scatter_dimension=0, tiled=True
        ).astype(jnp.float32),
        lax.psum_scatter(
            totals[7].astype(jnp.bfloat16), "shard", scatter_dimension=0, tiled=True
        ).astype(jnp.float32),
        lax.psum_scatter(
            totals[8].astype(jnp.bfloat16), "shard", scatter_dimension=0, tiled=True
        ).astype(jnp.float32),
        lax.psum_scatter(
            totals[9].astype(jnp.bfloat16), "shard", scatter_dimension=0, tiled=True
        ).astype(jnp.float32),
        lax.psum_scatter(
            totals[10].astype(jnp.bfloat16), "shard", scatter_dimension=0, tiled=True
        ).astype(jnp.float32),
        lax.psum_scatter(
            totals[11].astype(jnp.bfloat16), "shard", scatter_dimension=0, tiled=True
        ).astype(jnp.float32),
        lax.psum_scatter(
            totals[12].astype(jnp.bfloat16), "shard", scatter_dimension=0, tiled=True
        ).astype(jnp.float32),
    )
    grad_total = (
        lax.psum(grad_local[0].astype(jnp.bfloat16), "grp").astype(jnp.float32),
        lax.psum(grad_local[1].astype(jnp.bfloat16), "grp").astype(jnp.float32),
        lax.psum(grad_local[2].astype(jnp.bfloat16), "grp").astype(jnp.float32),
        lax.psum(grad_local[3].astype(jnp.bfloat16), "grp").astype(jnp.float32),
        lax.psum(grad_local[4].astype(jnp.bfloat16), "grp").astype(jnp.float32),
        lax.psum(grad_local[5].astype(jnp.bfloat16), "grp").astype(jnp.float32),
        lax.psum(grad_local[6].astype(jnp.bfloat16), "grp").astype(jnp.float32),
        lax.psum(grad_local[7].astype(jnp.bfloat16), "grp").astype(jnp.float32),
        lax.psum(grad_local[8].astype(jnp.bfloat16), "grp").astype(jnp.float32),
        lax.psum(grad_local[9].astype(jnp.bfloat16), "grp").astype(jnp.float32),
        lax.psum(grad_local[10].astype(jnp.bfloat16), "grp").astype(jnp.float32),
        lax.psum(grad_local[11].astype(jnp.bfloat16), "grp").astype(jnp.float32),
        lax.psum(grad_local[12].astype(jnp.bfloat16), "grp").astype(jnp.float32),
    )
    return (
        jnp.stack(layer_rows),
        jnp.stack(grad_rows),
        grad_total[0],
        grad_total[1],
        grad_total[2],
        grad_total[3],
        grad_total[4],
        grad_total[5],
        grad_total[6],
        grad_total[7],
        grad_total[8],
        grad_total[9],
        grad_total[10],
        grad_total[11],
        grad_total[12],
    )


BF = jnp.bfloat16
GRANT = 60 << 20
COST = pl.CostEstimate(flops=1024, bytes_accessed=1024, transcendentals=0)
F32 = jnp.float32


def swap_core(value):
    return lax.ppermute(value, "grp", [(i, i ^ 1) for i in range(8)])


def swap_x(value):
    return lax.ppermute(value, "grp", [(i, i ^ 2) for i in range(8)])


def swap_y(value):
    return lax.ppermute(value, "grp", [(i, i ^ 4) for i in range(8)])


def swap_z(value, flip):
    return lax.ppermute(value, "shard", [(i, i ^ flip) for i in range(4)])


def swap_xy(value):
    return lax.ppermute(value, "grp", [(i, i ^ 6) for i in range(8)])


def dot32(left_mat, right_mat):
    return jnp.dot(left_mat, right_mat, preferred_element_type=F32)


def after(values, *others):
    return lax.optimization_barrier((values, others))[0]


def sequence_perm(flip):
    pairs = []
    for grp in range(8):
        for line in range(4):
            dst_grp = (grp & 6) | (line // 2)
            dst_line = 2 * (grp & 1) + ((line % 2) ^ flip)
            pairs.append((grp * 4 + line, dst_grp * 4 + dst_line))
    return pairs


def send_first(block):
    return lax.ppermute(block, ("grp", "shard"), sequence_perm(0))


def send_second(block):
    return lax.ppermute(block, ("grp", "shard"), sequence_perm(1))


def send_rows(first, second):
    return send_first(first), send_second(second)


def return_block(block, flip):
    return lax.ppermute(block, ("grp", "shard"), [(dst, src) for src, dst in sequence_perm(flip)])


def return_rows(first, second):
    return return_block(first, 0), return_block(second, 1)


def join_rows(first, second, parity):
    return jnp.where(parity == 0, jnp.stack([first, second]), jnp.stack([second, first]))


CORE, PLANE, LINE, PARITY = range(4)


def start_moves(moves, where_ref, sources, targets, sems):
    where = [where_ref[idx] for idx in range(4)]
    place = lambda at, unit: at if isinstance(at, int) else pl.multiple_of(at(*where), unit)
    copies = []
    for idx, (src, src_row, src_col, rows, cols, dst, dst_row, dst_col) in enumerate(moves):
        copies.append(
            pltpu.make_async_copy(
                sources[src].at[pl.ds(place(src_row, 8), rows), pl.ds(place(src_col, 128), cols)],
                targets[dst].at[pl.ds(place(dst_row, 8), rows), pl.ds(place(dst_col, 128), cols)],
                sems.at[idx],
            )
        )
    for copy in copies:
        copy.start()
    return copies


def move_kernel(count, moves, where_ref, *refs):
    for copy in start_moves(moves, where_ref, refs[:count], refs[count:-1], refs[-1]):
        copy.wait()


def move_blocks(where, sources, moves, shapes, grant=16 << 20):
    moved = sum(move[3] * move[4] for move in moves) * 2
    return pl.pallas_call(
        functools.partial(move_kernel, len(sources), moves),
        out_shape=[jax.ShapeDtypeStruct(shape, sources[0].dtype) for shape in shapes],
        in_specs=[pl.BlockSpec(memory_space=pltpu.SMEM)]
        + [pl.BlockSpec(memory_space=pl.ANY)] * len(sources),
        out_specs=[pl.BlockSpec(memory_space=pltpu.VMEM)] * len(shapes),
        scratch_shapes=[pltpu.SemaphoreType.DMA((len(moves),))],
        cost_estimate=COST,
        compiler_params=pltpu.CompilerParams(vmem_limit_bytes=grant),
    )(where, *sources)


def join_blocks(where, parts):
    moves, at = [], 0
    for idx, part in enumerate(parts):
        moves.append((idx, 0, 0, part.shape[0], part.shape[1], 0, at, 0))
        at += part.shape[0]
    return move_blocks(where, list(parts), moves, [(at, parts[0].shape[1])])[0]


def along_line(piece):
    return [swap_z(piece, flip) for flip in (1, 2, 3)]


def across_plane(came):
    return [swap_x(came), swap_y(came), swap_xy(came)]


def placed_moves(first_src, height, piece_rows, col, cols, dst):
    moves = []
    for flip in range(4):
        for step in range(1, 4):
            at = lambda core, plane, line, parity, flip=flip, step=step: (
                (line ^ step) * (4 * piece_rows) + (plane ^ flip) * piece_rows
            )
            moves.append((first_src + flip, (step - 1) * height, col, piece_rows, cols, dst, at, 0))
    return moves


def pick(arr, idx, axis):
    return lax.dynamic_index_in_dim(arr, idx, axis, keepdims=False)


def add_low(left, right):
    return (left.astype(F32) + right.astype(F32)).astype(BF)


def reduce_first(grads, cut, col, row):
    join = lambda arrs: arrs[0] if len(arrs) == 1 else jnp.concatenate(arrs, axis=-1)
    low_part = lambda idx: join([pick(grad[:, :, :, :cut], idx, 2) for grad in grads])
    high_part = lambda idx: join([pick(grad[:, :, :, cut:], idx, 1) for grad in grads])
    sent = (low_part(1 - col), high_part(1 - row))
    return (low_part(col), high_part(row), swap_x(sent[0]), swap_y(sent[1])), sent


def reduce_second(state, col, row):
    low, high, low_got, high_got = state
    low, high = add_low(low, low_got), add_low(high, high_got)
    sent = (pick(low, 1 - row, 1), pick(high, 1 - col, 1))
    return (pick(low, row, 1), pick(high, col, 1), swap_y(sent[0]), swap_x(sent[1])), sent


def reduce_near(states, line):
    mine = [
        jnp.concatenate([add_low(low, low_got), add_low(high, high_got)], axis=1)
        for low, high, low_got, high_got in states
    ]
    mine = mine[0] if len(mine) == 1 else jnp.concatenate(mine, axis=-1)
    pairs = mine.reshape((2, 2) + mine.shape[1:])
    sent = pick(pairs, 1 - line % 2, 1)
    return (pick(pairs, line % 2, 1), swap_z(sent, 1)), sent


def reduce_far(state, line):
    mine = add_low(*state)
    sent = pick(mine, 1 - line // 2, 0)
    return (pick(mine, line // 2, 0), swap_z(sent, 2)), sent


def direct_spread(state):
    piece = sum(part.astype(F32) for part in state).astype(BF)
    return [piece] + across_plane(piece), piece


def final_kernel(layout, rows, extra, flips, where_ref, mine_ref, other_ref, *outs):
    plane = where_ref[PLANE]
    height = mine_ref.shape[0] // 4

    low = where_ref[CORE] == 0
    for half in range(2):
        for at in range(4):
            part = plane ^ flips[at]
            for src_col, cols, dst, row_of, dst_col in layout(half):
                row = pl.multiple_of(row_of(part), 16)
                here = (pl.ds(at * height, rows), pl.ds(src_col, cols))
                mine, other = mine_ref[here], other_ref[here]
                value = jnp.where(low, mine, other) if half == 0 else jnp.where(low, other, mine)
                outs[dst][pl.ds(row, rows), pl.ds(dst_col, cols)] = value.astype(F32)
    if extra is not None:
        vecs = outs[-9:]
        slab = vecs[0].shape[0]
        for at in range(4):

            @pl.when(plane == flips[at])
            def _(at=at):
                begin, end = [
                    mine_ref[here, pl.ds(extra, 128)].astype(F32) + other_ref[here, pl.ds(extra, 128)].astype(F32)
                    for here in (pl.ds(at * height, 16), pl.ds(at * height + 16, 16))
                ]
                both = jnp.concatenate([begin, end], axis=1)
                for idx in range(8):
                    vecs[idx][...] = both[idx : idx + 1, :slab].reshape(slab)
                spread = jnp.concatenate([both, jnp.zeros((16, 4 * slab - 256), F32)], axis=1)
                lane = lax.broadcasted_iota(jnp.int32, spread.shape, 1)
                spread = jnp.where(lane < slab, spread, 0.0)
                wide = spread[8:9]
                for part in range(1, 4):
                    wide += pltpu.roll(spread[8 + part : 9 + part], part * slab, 1)
                vecs[8][...] = wide.reshape(4 * slab)


def spread_first(state, through_x):
    piece = add_low(*state)
    return piece, (swap_x if through_x else swap_y)(piece)


def spread_second(state, through_x):
    both = jnp.concatenate(state, axis=0)
    return both, (swap_y if through_x else swap_x)(both)


def spread_core(state):
    mine = jnp.concatenate(state, axis=0)
    return mine, swap_core(mine)


def finish_grad(where, state, through_x, layout, rows, shapes, extra=None):
    mine, other = state
    mine_flips = (0, 1, 2, 3) if through_x else (0, 2, 1, 3)
    shapes = list(shapes) + ([] if extra is None else [(shapes[0][0],)] * 8 + [(4 * shapes[0][0],)])
    vmem = pl.BlockSpec(memory_space=pltpu.VMEM)
    return pl.pallas_call(
        functools.partial(final_kernel, layout, rows, extra, mine_flips),
        out_shape=[jax.ShapeDtypeStruct(shape, F32) for shape in shapes],
        in_specs=[pl.BlockSpec(memory_space=pltpu.SMEM), vmem, vmem],
        out_specs=[vmem] * len(shapes),
        cost_estimate=COST,
        compiler_params=pltpu.CompilerParams(vmem_limit_bytes=16 << 20),
    )(where, mine, other)


ROWS = 256


def row_spec(width, shift=0, steps=1, block=ROWS):
    if shift:
        return pl.BlockSpec((block, width), lambda blk: ((blk + shift) % steps, 0))
    return pl.BlockSpec((block, width), lambda blk: (blk, 0))


def whole_spec(rows, width):
    return pl.BlockSpec((rows, width), lambda blk: (0, 0))


def mean_last(values):
    return jnp.mean(values, axis=-1, keepdims=True)


def norm_parts(values):
    centered = values - mean_last(values)
    scale = lax.rsqrt(mean_last(centered * centered) + eps)
    return centered * scale, scale


def norm_back(grad_normed, normed, scale):
    return scale * (grad_normed - mean_last(grad_normed) - normed * mean_last(grad_normed * normed))


def up_kernel(part_ref, got_ref, tok_ref, vec_ref, bias_ref, w_ref, low_ref, n_ref, r_ref, act_ref, slope_ref):
    vec = vec_ref[...]
    attn_out = part_ref[...].astype(F32) + got_ref[...].astype(F32) + vec[0:1]
    normed, scale = norm_parts(tok_ref[...].astype(F32) + attn_out)
    hidden = (normed * vec[1:2] + vec[2:3]).astype(BF)
    n_ref[...] = normed
    r_ref[...] = jnp.broadcast_to(scale, r_ref.shape)
    low_ref[...] = hidden
    for at in range(0, w_ref.shape[1], 384):
        cols = pl.ds(at, 384)
        up = dot32(hidden, w_ref[:, cols]) + bias_ref[:, cols]
        cdf = 0.5 + 0.5 * lax.erf(up * 0.5**0.5)
        act_ref[:, cols] = (up * cdf).astype(BF)
        slope = cdf + up * (jnp.exp(up * up * -0.5) * (2 * math.pi) ** -0.5)
        slope_ref[:, cols] = slope.astype(BF)


def ffn_up(part, got, tokens, vectors, up_bias, weight):
    rows, width = part.shape
    units = weight.shape[1]
    block = ROWS // 2
    steps = rows // block
    return pl.pallas_call(
        up_kernel,
        grid=(steps,),
        out_shape=[
            jax.ShapeDtypeStruct((rows, width), BF),
            jax.ShapeDtypeStruct((rows, width), F32),
            jax.ShapeDtypeStruct((rows, 128), F32),
            jax.ShapeDtypeStruct((rows, units), BF),
            jax.ShapeDtypeStruct((rows, units), BF),
        ],
        in_specs=[
            row_spec(width, block=block),
            row_spec(width, steps // 2, steps, block=block),
            row_spec(width, block=block),
            whole_spec(8, width),
            whole_spec(1, units),
            whole_spec(width, units),
        ],
        out_specs=[row_spec(width, block=block), row_spec(width, block=block), row_spec(128, block=block), row_spec(units, block=block), row_spec(units, block=block)],
        cost_estimate=COST,
        compiler_params=pltpu.CompilerParams(vmem_limit_bytes=20 << 20),
    )(part, got, tokens, vectors, up_bias, weight)


def turn_kernel(
    half_steps, part_ref, got_ref, n_ref, cot_ref, bias_ref, vec_ref, first_ref, second_ref, dr_ref, low_ref, sum_ref
):
    blk = pl.program_id(0)
    vec = vec_ref[...]
    hidden = n_ref[...] * vec[1:2] + vec[2:3]
    ffn_out = part_ref[...].astype(F32) + got_ref[...].astype(F32) + vec[3:4]
    normed, scale = norm_parts(hidden + ffn_out)
    mask = jnp.where(bias_ref[:, 0:1] < 0.0, 0.0, 1.0)
    result = ((normed * vec[4:5] + vec[5:6]) * mask).astype(BF)
    dy = cot_ref[...].astype(F32) * mask
    dr = norm_back(dy * vec[4:5], normed, scale)
    dr_low = dr.astype(BF)
    dr_ref[...] = dr
    low_ref[...] = dr_low

    @pl.when(blk == 0)
    def _():
        sum_ref[...] = jnp.zeros_like(sum_ref)
        first_ref[...] = result

    @pl.when(blk == 1)
    def _():
        second_ref[...] = result

    @pl.when(blk < half_steps)
    def _():
        sum_ref[0:1] += jnp.sum(dy * normed, axis=0, keepdims=True)
        sum_ref[1:2] += jnp.sum(dy, axis=0, keepdims=True)
        sum_ref[2:3] += jnp.sum(dr_low.astype(F32), axis=0, keepdims=True)


def norm_turn(part, got, n_one, cot, bias, vectors):
    rows, width = part.shape
    steps = rows // ROWS
    return pl.pallas_call(
        functools.partial(turn_kernel, steps // 2),
        grid=(steps,),
        out_shape=[jax.ShapeDtypeStruct((ROWS, width), BF)] * 2
        + [
            jax.ShapeDtypeStruct((rows, width), F32),
            jax.ShapeDtypeStruct((rows, width), BF),
            jax.ShapeDtypeStruct((8, width), F32),
        ],
        in_specs=[
            row_spec(width),
            row_spec(width, steps // 2, steps),
            row_spec(width),
            row_spec(width),
            row_spec(128),
            whole_spec(8, width),
        ],
        out_specs=[whole_spec(ROWS, width)] * 2 + [row_spec(width), row_spec(width), whole_spec(8, width)],
        cost_estimate=COST,
        compiler_params=pltpu.CompilerParams(vmem_limit_bytes=28 << 20),
    )(part, got, n_one, cot, bias, vectors)


def ffn_back_kernel(dffn_ref, down_ref, slope_ref, up_ref, dup_ref, part_ref, sum_ref):
    @pl.when(pl.program_id(0) == 0)
    def _():
        sum_ref[...] = jnp.zeros_like(sum_ref)

    total = jnp.zeros(part_ref.shape, F32)
    dffn = dffn_ref[...]
    for at in range(0, dup_ref.shape[1], 512):
        here = pl.ds(at, 512)
        dup = (contract_cols(dffn, down_ref[here, :]) * slope_ref[:, here].astype(F32)).astype(BF)
        dup_ref[:, here] = dup
        sum_ref[:, here] += jnp.sum(dup.astype(F32), axis=0, keepdims=True)
        total += contract_cols(dup, up_ref[:, here])
    part_ref[...] = total.astype(BF)


def ffn_back(dffn, down_weight, slope, up_weight):
    rows, width = dffn.shape
    units = slope.shape[1]
    return pl.pallas_call(
        ffn_back_kernel,
        grid=(rows // ROWS,),
        out_shape=[
            jax.ShapeDtypeStruct((rows, units), BF),
            jax.ShapeDtypeStruct((rows, width), BF),
            jax.ShapeDtypeStruct((1, units), F32),
        ],
        in_specs=[row_spec(width), whole_spec(units, width), row_spec(units), whole_spec(width, units)],
        out_specs=[row_spec(units), row_spec(width), whole_spec(1, units)],
        cost_estimate=COST,
        compiler_params=pltpu.CompilerParams(vmem_limit_bytes=20 << 20),
    )(dffn, down_weight, slope, up_weight)


def back_kernel(
    half_steps, where_ref, dr_ref, part_ref, got_ref, n_ref, r_ref, vec_ref, own_ref, low_ref, part_low_ref, sum_ref
):
    blk = pl.program_id(0)
    vec = vec_ref[...]
    normed = n_ref[...]
    dhidden = dr_ref[...] + (part_ref[...].astype(F32) + got_ref[...].astype(F32))
    dr = norm_back(dhidden * vec[1:2], normed, r_ref[:, 0:1])
    dr_low = dr.astype(BF)
    low_ref[...] = dr_low
    half = dr.shape[1] // 2
    part_low_ref[...] = jnp.where(where_ref[CORE] == 0, dr_low[:, :half], dr_low[:, half:])

    @pl.when(blk == 0)
    def _():
        sum_ref[...] = jnp.zeros_like(sum_ref)

    @pl.when(blk < half_steps)
    def _():
        own_ref[...] = dr
        sum_ref[0:1] += jnp.sum(dhidden * normed, axis=0, keepdims=True)
        sum_ref[1:2] += jnp.sum(dhidden, axis=0, keepdims=True)
        sum_ref[2:3] += jnp.sum(dr_low.astype(F32), axis=0, keepdims=True)


def norm_one_back(where, dr_two, part, got, n_one, r_one, vectors):
    rows, width = part.shape
    steps = rows // ROWS
    return pl.pallas_call(
        functools.partial(back_kernel, steps // 2),
        grid=(steps,),
        out_shape=[
            jax.ShapeDtypeStruct((rows // 2, width), F32),
            jax.ShapeDtypeStruct((rows, width), BF),
            jax.ShapeDtypeStruct((rows, width // 2), BF),
            jax.ShapeDtypeStruct((8, width), F32),
        ],
        in_specs=[
            pl.BlockSpec(memory_space=pltpu.SMEM),
            row_spec(width),
            row_spec(width),
            row_spec(width, steps // 2, steps),
            row_spec(width),
            row_spec(128),
            whole_spec(8, width),
        ],
        out_specs=[
            pl.BlockSpec((ROWS, width), lambda blk: (jnp.minimum(blk, steps // 2 - 1), 0)),
            row_spec(width),
            row_spec(width // 2),
            whole_spec(8, width),
        ],
        cost_estimate=COST,
        compiler_params=pltpu.CompilerParams(vmem_limit_bytes=28 << 20),
    )(where, dr_two, part, got, n_one, r_one, vectors)


Q_BLOCK = 512
PAIR = 128


def contract_last(left_mat, right_mat):
    return lax.dot_general(
        left_mat, right_mat, (((1,), (1,)), ((), ())), preferred_element_type=F32
    )


def head_lanes(block, head):
    lane = lax.broadcasted_iota(jnp.int32, block.shape, 1)
    return jnp.where((lane // HD) == head, block, jnp.zeros_like(block))


def attend_fwd_kernel(q_ref, k_ref, v_ref, bias_ref, ctx_ref, lse_ref, vt_ref, out_ref):
    vt_ref[...] = v_ref[...].T

    @pl.loop(0, q_ref.shape[0] // Q_BLOCK)
    def _(blk):
        at = pl.multiple_of(blk * Q_BLOCK, Q_BLOCK)

        @pl.loop(0, 2)
        def _(head):
            q_blk = q_ref[pl.ds(at, Q_BLOCK), :] * jnp.asarray(HD ** (-0.5), BF)
            here = pl.ds(pl.multiple_of(head * HD, HD), HD)
            scores = contract_last(k_ref[...], head_lanes(q_blk, head))
            scores = scores + jnp.concatenate([bias_ref[...]] * (Q_BLOCK // 128), axis=1)
            top = jnp.max(scores, axis=0, keepdims=True)
            exps = jnp.exp(scores - top)
            total = jnp.sum(exps, axis=0, keepdims=True)
            out_ref[here, :] = dot32(vt_ref[here, :], exps.astype(BF)) * (1.0 / total)
            lse_ref[0, pl.ds(head, 1), pl.ds(at, Q_BLOCK)] = top + jnp.log(total)

        ctx_ref[pl.ds(at, Q_BLOCK), :] = out_ref[...].T.astype(BF)


def attend_bwd_kernel(
    q_ref, k_ref, v_ref, bias_ref, lse_ref, grad_ref, dq_ref, dk_ref, dv_ref, kt_ref, dk_acc, dv_acc, out_ref
):
    kt_ref[...] = k_ref[...].T
    dk_acc[...] = jnp.zeros_like(dk_acc)
    dv_acc[...] = jnp.zeros_like(dv_acc)

    @pl.loop(0, q_ref.shape[0] // Q_BLOCK)
    def _(blk):
        at = pl.multiple_of(blk * Q_BLOCK, Q_BLOCK)

        @pl.loop(0, 2)
        def _(head):
            q_head = head_lanes(q_ref[pl.ds(at, Q_BLOCK), :] * jnp.asarray(HD ** (-0.5), BF), head)
            grad_head = head_lanes(grad_ref[pl.ds(at, Q_BLOCK), :], head)
            here = pl.ds(pl.multiple_of(head * HD, HD), HD)
            scores = contract_last(k_ref[...], q_head)
            scores = scores + jnp.concatenate([bias_ref[...]] * (Q_BLOCK // 128), axis=1)
            probs = jnp.exp(scores - lse_ref[0, pl.ds(head, 1), pl.ds(at, Q_BLOCK)])
            weighed = probs * contract_last(v_ref[...], grad_head)
            delta = jnp.sum(weighed, axis=0, keepdims=True)
            grad_scores = (weighed - probs * delta).astype(BF)
            dk_acc[...] += dot32(grad_scores, q_head)
            dv_acc[...] += dot32(probs.astype(BF), grad_head)
            out_ref[here, :] = dot32(kt_ref[here, :], grad_scores)

        dq_ref[pl.ds(at, Q_BLOCK), :] = (out_ref[...].T * (HD ** (-0.5))).astype(BF)

    dk_ref[...] = dk_acc[...].astype(BF)
    dv_ref[...] = dv_acc[...].astype(BF)


def column_spec(rows, first):
    return pl.BlockSpec((rows, PAIR), lambda pair: (0, first + pair))


def attend_chip_forward(qkv, bias, pair):
    rows, half = qkv.shape[0], qkv.shape[1] // 3
    pairs = half // PAIR
    return pl.pallas_call(
        attend_fwd_kernel,
        grid=(1,),
        out_shape=[
            jax.ShapeDtypeStruct((rows, PAIR), BF),
            jax.ShapeDtypeStruct((1, 2, rows), F32),
        ],
        in_specs=[column_spec(rows, idx * pairs + pair) for idx in range(3)]
        + [pl.BlockSpec((rows, 128), lambda step: (0, 0))],
        out_specs=[column_spec(rows, 0), pl.BlockSpec((1, 2, rows), lambda step: (0, 0, 0))],
        scratch_shapes=[pltpu.VMEM((PAIR, rows), BF), pltpu.VMEM((PAIR, Q_BLOCK), F32)],
        cost_estimate=COST,
        compiler_params=pltpu.CompilerParams(vmem_limit_bytes=28 << 20),
    )(qkv, qkv, qkv, bias)


def attend_chip_backward(qkv, bias, lse, grad_ctx, pair):
    rows, half = qkv.shape[0], qkv.shape[1] // 3
    pairs = half // PAIR
    return pl.pallas_call(
        attend_bwd_kernel,
        grid=(1,),
        out_shape=[jax.ShapeDtypeStruct((rows, PAIR), BF)] * 3,
        in_specs=[column_spec(rows, idx * pairs + pair) for idx in range(3)]
        + [
            pl.BlockSpec((rows, 128), lambda step: (0, 0)),
            pl.BlockSpec((1, 2, rows), lambda step: (0, 0, 0)),
            column_spec(rows, pair),
        ],
        out_specs=[column_spec(rows, 0)] * 3,
        scratch_shapes=[
            pltpu.VMEM((PAIR, rows), BF),
            pltpu.VMEM((rows, PAIR), F32),
            pltpu.VMEM((rows, PAIR), F32),
            pltpu.VMEM((PAIR, Q_BLOCK), F32),
        ],
        cost_estimate=COST,
        compiler_params=pltpu.CompilerParams(vmem_limit_bytes=32 << 20),
    )(qkv, qkv, qkv, bias, lse, grad_ctx)


def pack_kernel(count, moves, vec_at, slab, where_ref, *refs):
    sources, vecs = refs[:count], refs[count : count + 9]
    targets, sems = refs[count + 9 : -1], refs[-1]
    copies = start_moves(moves, where_ref, sources, targets, sems)
    dst, row = vec_at
    width = targets[dst].shape[1]
    rows = [vec[...].reshape(1, slab).astype(F32) for vec in vecs[:8]]
    wide = vecs[8][...].reshape(1, -1).astype(F32)
    count_wide = wide.shape[1] // slab
    rows += [wide[:, :slab]]
    rows += [pltpu.roll(wide, wide.shape[1] - idx * slab, 1)[:, :slab] for idx in range(1, count_wide)]
    rows += [jnp.zeros((4, slab), F32)]
    block = jnp.concatenate(rows, axis=0)
    targets[dst][pl.ds(row, 16), :] = jnp.concatenate(
        [block, jnp.zeros((16, width - slab), F32)], axis=1
    ).astype(BF)
    for copy in copies:
        copy.wait()


def pack_blocks(where, sources, vecs, moves, shapes, vec_at, slab):
    return pl.pallas_call(
        functools.partial(pack_kernel, len(sources), moves, vec_at, slab),
        out_shape=[jax.ShapeDtypeStruct(shape, BF) for shape in shapes],
        in_specs=[pl.BlockSpec(memory_space=pltpu.SMEM)]
        + [pl.BlockSpec(memory_space=pl.ANY)] * len(sources)
        + [pl.BlockSpec(memory_space=pltpu.VMEM)] * len(vecs),
        out_specs=[pl.BlockSpec(memory_space=pltpu.VMEM)] * len(shapes),
        scratch_shapes=[pltpu.SemaphoreType.DMA((len(moves),))],
        cost_estimate=COST,
        compiler_params=pltpu.CompilerParams(vmem_limit_bytes=60 << 20),
    )(where, *sources, *vecs)


def vector_kernel(height, at, slab, where_ref, own_ref, came_ref, block_ref, qkv_ref, up_ref, buf, sems):
    line = where_ref[LINE]
    copies = [pltpu.make_async_copy(own_ref.at[pl.ds(at, 16)], buf.at[line], sems.at[0])]
    for step in range(1, 4):
        copies.append(
            pltpu.make_async_copy(
                came_ref.at[pl.ds((step - 1) * height + at, 16)], buf.at[line ^ step], sems.at[step]
            )
        )
    for copy in copies:
        copy.start()
    for copy in copies:
        copy.wait()
    width = block_ref.shape[1]
    half = width // 2
    joined = jnp.zeros((16, width), F32)
    lane = lax.broadcasted_iota(jnp.int32, (16, width), 1)
    wide = []
    for idx in range(4):
        rows = jnp.where(lane < slab, buf[idx, :, :width].astype(F32), 0.0)
        joined += rows if idx == 0 else pltpu.roll(rows, idx * slab, 1)
        row = rows[8:9]
        for part in range(1, 4):
            row += pltpu.roll(rows[8 + part : 9 + part], part * slab, 1)
        wide.append(row)
    low = where_ref[CORE] == 0
    pick_half = lambda row: jnp.where(low, row[:, :half], row[:, half:])
    block_ref[...] = jnp.concatenate([joined[2:8], jnp.zeros((2, width), F32)], axis=0)
    qkv_ref[...] = jnp.concatenate(
        [pick_half(joined[0:1]), jnp.zeros((1, half), F32), pick_half(joined[1:2])], axis=1
    )
    up_ref[...] = jnp.concatenate([pick_half(row) for row in wide], axis=1)


def join_vectors(where, own, came, at, slab, width):
    height = came.shape[0] // 3
    return pl.pallas_call(
        functools.partial(vector_kernel, height, at, slab),
        out_shape=[
            jax.ShapeDtypeStruct((8, width), F32),
            jax.ShapeDtypeStruct((1, 3 * width // 2), F32),
            jax.ShapeDtypeStruct((1, 2 * width), F32),
        ],
        in_specs=[pl.BlockSpec(memory_space=pltpu.SMEM)] + [pl.BlockSpec(memory_space=pl.ANY)] * 2,
        out_specs=[pl.BlockSpec(memory_space=pltpu.VMEM)] * 3,
        scratch_shapes=[pltpu.VMEM((4, 16, own.shape[1]), BF), pltpu.SemaphoreType.DMA((4,))],
        cost_estimate=COST,
        compiler_params=pltpu.CompilerParams(vmem_limit_bytes=4 << 20),
    )(where, own, came)


def small_kernel(slab, where_ref, one_ref, two_ref, up_ref, qkv_ref, out_ref):
    width = one_ref.shape[1]
    half = width // 2
    low = where_ref[CORE] == 0
    zero = jnp.zeros((1, half), F32)
    on_core = lambda row: jnp.where(
        low, jnp.concatenate([row, zero], axis=1), jnp.concatenate([zero, row], axis=1)
    )
    one, two = one_ref[...], two_ref[...]
    rows = jnp.concatenate(
        [
            on_core(qkv_ref[:, :half]),
            on_core(qkv_ref[:, 2 * half :]),
            one[2:3],
            one[0:1],
            one[1:2],
            two[2:3],
            two[0:1],
            two[1:2],
        ],
        axis=0,
    )
    out_ref[...] = jnp.zeros_like(out_ref)
    for idx in range(4):
        wide = on_core(up_ref[:, idx * half : (idx + 1) * half])
        at = lambda row, part: row if part == 0 else pltpu.roll(row, width - part * slab, 1)
        parts = [at(wide, part)[:, :256] for part in range(4)]
        block = jnp.concatenate([at(rows, idx)[:, :256]] + parts + [jnp.zeros((4, 256), F32)], axis=0)
        lane = lax.broadcasted_iota(jnp.int32, block.shape, 1)
        block = jnp.where(lane < slab, block, 0.0).astype(BF)
        out_ref[idx, 0:16, :] = block[:, :128]
        out_ref[idx, 16:32, :] = block[:, 128:]


def small_grads(where, sums_one, sums_two, up_sums, qkv_sums, slab):
    vmem = pl.BlockSpec(memory_space=pltpu.VMEM)
    return pl.pallas_call(
        functools.partial(small_kernel, slab),
        out_shape=jax.ShapeDtypeStruct((4, slab // 4, 128), BF),
        in_specs=[pl.BlockSpec(memory_space=pltpu.SMEM)] + [vmem] * 4,
        out_specs=vmem,
        compiler_params=pltpu.CompilerParams(vmem_limit_bytes=4 << 20),
    )(where, sums_one, sums_two, up_sums, qkv_sums)


def per_device_chip(
    tokens,
    cotangent,
    lengths,
    w_qkv,
    bias_q,
    bias_v,
    w_out,
    bias_out,
    gain_attn,
    shift_attn,
    w_up,
    bias_up,
    w_down,
    bias_down,
    gain_ffn,
    shift_ffn,
):
    quarter, width = tokens.shape[1:]
    half_rows = 2 * quarter
    units = w_up.shape[1] // 2
    slab = w_qkv.shape[0]
    wide = w_down.shape[0]
    half = width // 2
    slab_part, wide_part = slab // 4, wide // 8
    vec_rows = 16
    group = lax.axis_index("grp")
    line = lax.axis_index("shard")
    core = group % 2
    plane = group // 2
    col, row = plane % 2, plane // 2
    parity = line % 2
    where = jnp.stack([core, plane, line, parity]).astype(jnp.int32)

    vecs = [bias_q, bias_v, bias_out, gain_attn, shift_attn, bias_down, gain_ffn, shift_ffn, bias_up]
    moves = []
    slab_at = lambda c, p, z, e: p * slab_part
    for idx in range(3):
        at = lambda c, p, z, e, idx=idx: idx * width + c * half
        moves.append((0, slab_at, at, slab_part, half, 0, 0, idx * half))
    (qkv_piece,) = pack_blocks(
        where, [w_qkv], vecs, moves, [(slab_part + vec_rows, 3 * half)], (0, slab_part), slab
    )
    qkv_parts = along_line(qkv_piece)
    moves = []
    for idx in range(2):
        moves.append((idx, lambda c, p, z, e: e * quarter, 0, quarter, width, 2 * idx, 0, 0))
        moves.append((idx, lambda c, p, z, e: (1 - e) * quarter, 0, quarter, width, 2 * idx + 1, 0, 0))
    for idx in range(4):
        at = lambda c, p, z, e, idx=idx: idx * wide + c * (wide // 2)
        moves.append((2, slab_at, at, slab_part, wide // 2, 4, 0, idx * (wide // 2)))
    moves.append((3, slab_at, lambda c, p, z, e: c * half, slab_part, half, 4, 0, units))
    moves.append((4, lambda c, p, z, e: c * (wide // 2) + p * wide_part, 0, wide_part, width, 5, 0, 0))
    tok_first, tok_second, cot_first, cot_second, up_piece, down_piece = move_blocks(
        where,
        [after(tokens.reshape(half_rows, width), qkv_parts[0]), cotangent.reshape(half_rows, width), w_up, w_out, w_down],
        moves,
        [(quarter, width)] * 4 + [(slab_part, units + half), (wide_part, width)],
        grant=GRANT,
    )
    slab_start = lambda c, p, z, e: z * slab

    stack = lambda parts: join_blocks(where, parts)
    len_other = swap_core(lengths)
    len_all = jnp.where(core == 0, jnp.concatenate([lengths, len_other]), jnp.concatenate([len_other, lengths]))
    seq_len = len_all[line]
    place = lax.broadcasted_iota(jnp.int32, (4 * quarter, 128), 0)
    place = ((place // quarter) ^ (2 * core + parity)) * quarter + place % quarter
    bias = jnp.where(place < seq_len, 0.0, masked_score).astype(F32)
    tok_first, tok_second = send_rows(tok_first, tok_second)
    qkv_came = stack(after(qkv_parts, bias, down_piece))
    qkv_plane = across_plane(qkv_came)
    vec_block, qkv_bias, up_bias = join_vectors(where, qkv_piece, qkv_came, slab_part, slab, width)
    tok_own = stack(after([tok_first, tok_second], vec_block, *qkv_plane))
    up_parts = along_line(after(up_piece, tok_own))
    tok_all = stack([tok_own, swap_core(tok_own)])

    moves = []
    for idx in range(3):
        at = lambda c, p, z, e, idx=idx: idx * width + c * half
        moves.append((0, 0, at, slab, half, 0, slab_start, idx * half))
    moves += placed_moves(1, slab_part + vec_rows, slab_part, 0, 3 * half, 0)
    (qkv_weight,) = move_blocks(
        where, [w_qkv, after(qkv_came, vec_block)] + qkv_plane, moves, [(width, 3 * half)]
    )

    qkv = (dot32(tok_all, qkv_weight) + qkv_bias).astype(BF)
    pairs = half // PAIR
    contexts, lses = [], []
    for pair in range(pairs):
        qkv_in = after(qkv, contexts[-1]) if contexts else qkv
        if pair == 1:
            up_came = stack(after(up_parts, contexts[0]))
            up_plane = across_plane(up_came)
            down_far = swap_z(after(down_piece, up_came), 2)
            cot_first = send_first(after(cot_first, up_came))
            qkv_in = after(qkv, up_came)
        elif pair == 2:
            down_two = stack(after([down_piece, down_far], contexts[1]))
            down_near = swap_z(down_two, 1)
            cot_second = send_second(after(cot_second, down_two))
            qkv_in = after(qkv, down_two)
        got = attend_chip_forward(qkv_in, bias, pair)
        contexts.append(got[0])
        lses.append(got[1])
    context = jnp.concatenate(contexts, axis=1)
    down_near = after(down_near, context)
    down_came = stack([down_near[:wide_part], down_far, down_near[wide_part:]])
    cot_own = stack(after([cot_first, cot_second], down_came))

    moves = []
    for idx in range(4):
        at = lambda c, p, z, e, idx=idx: idx * wide + c * (wide // 2)
        moves.append((0, 0, at, slab, wide // 2, 0, slab_start, idx * (wide // 2)))
    moves.append((1, 0, lambda c, p, z, e: c * half, slab, half, 1, slab_start, 0))
    moves += placed_moves(2, slab_part, slab_part, 0, units, 0)
    moves += placed_moves(2, slab_part, slab_part, units, half, 1)
    up_weight, out_half = move_blocks(
        where,
        [w_up, w_out, after(up_came, down_came, cot_own)] + up_plane,
        moves,
        [(width, units), (width, half)],
    )
    out_got = swap_core(out_half)
    down_plane = across_plane(after(down_came, out_half))
    moves = [
        (0, lambda c, p, z, e: c * half, 0, half, half, 0, 0, lambda c, p, z, e: c * half),
        (1, lambda c, p, z, e: c * half, 0, half, half, 0, 0, lambda c, p, z, e: (1 - c) * half),
    ]
    (out_weight,) = move_blocks(where, [out_half, out_got], moves, [(half, width)])
    part = dot32(context, out_weight).astype(BF)
    got = swap_core(part)
    hidden_low, n_one, r_one, act, slope = ffn_up(part, got, tok_all, vec_block, up_bias, up_weight)

    cot_all = stack([cot_own, swap_core(cot_own)])
    moves = [
        (0, 0, 0, 4 * quarter, half, 0, 0, lambda c, p, z, e: c * half),
        (1, 0, 0, half_rows, half, 0, half_rows, lambda c, p, z, e: (1 - c) * half),
        (1, half_rows, 0, half_rows, half, 0, 0, lambda c, p, z, e: (1 - c) * half),
    ]
    (context_all,) = move_blocks(
        where, [context, swap_core(after(context, cot_own))], moves, [(4 * quarter, width)]
    )
    moves = [(0, lambda c, p, z, e: c * (wide // 2), 0, wide // 2, width, 0, lambda c, p, z, e: z * (wide // 2), 0)]
    moves += placed_moves(1, wide_part, wide_part, 0, width, 0)
    (down_weight,) = move_blocks(where, [w_down, after(down_came, act, cot_all, context_all)] + down_plane, moves, [(units, width)])
    part = dot32(act, down_weight).astype(BF)
    out_first, out_second, dr_two, dffn, sums_two = norm_turn(
        part, swap_core(part), n_one, cot_all, bias, vec_block
    )

    blocks = lambda grad: grad.reshape(4, 2, 2, grad.shape[0] // 16, grad.shape[1])
    g_down = contract_rows(act, dffn).astype(BF)
    down_state, sent = reduce_first([blocks(g_down)], wide_part // 2, col, row)
    dffn = after(dffn, sent)
    dup, part, up_sums = ffn_back(dffn, down_weight, slope, up_weight)
    got = swap_core(part)
    dup_late = after(dup, part)
    g_up = contract_rows(hidden_low, dup_late).astype(BF)
    up_state, sent_up = reduce_first([blocks(g_up)], slab_part // 2, col, row)
    dr_one, dattn, dattn_part, sums_one = norm_one_back(
        where, dr_two, part, after(got, sent_up), n_one, r_one, vec_block
    )
    grad_ctx = contract_cols(dattn, out_weight).astype(BF)
    g_out = contract_rows(context_all, after(dattn_part, grad_ctx)).astype(BF)
    down_state, sent = reduce_second(after(down_state, g_out), col, row)
    layer_first = return_block(after(out_first, g_down), 0)
    layer_second = return_block(after(out_second, layer_first, g_up), 1)

    dqkv = []
    side = lambda parts: jnp.concatenate(parts, axis=1)
    qkv_in = after(qkv, sent)
    dqkv.append(attend_chip_backward(qkv_in, bias, lses[0], grad_ctx, 0))
    layer_out = join_rows(*after((layer_first, layer_second), dqkv[-1]), parity)
    down_state, sent = reduce_near([after(down_state, layer_out)], line)
    up_state, sent_up = reduce_second(after(up_state, sent), col, row)
    qkv_in = after(qkv, sent_up)
    for pair in range(1, pairs - 1):
        dqkv.append(attend_chip_backward(qkv_in, bias, lses[pair], grad_ctx, pair))
    most = side([part[idx] for idx in range(3) for part in dqkv])
    g_most = contract_rows(tok_all, most).astype(BF)
    most_state, sent = reduce_first([blocks(g_most), blocks(g_out)], slab_part // 2, col, row)
    down_state, sent = reduce_far(after(down_state, sent), line)
    up_state, sent_up = reduce_near([after(up_state, sent)], line)
    qkv_in = after(qkv, sent_up)
    dqkv.append(attend_chip_backward(qkv_in, bias, lses[-1], grad_ctx, pairs - 1))
    most_state, sent = reduce_second(after(most_state, dqkv[-1]), col, row)
    last = side(dqkv[-1])
    g_last = contract_rows(tok_all, after(last, sent)).astype(BF)
    dqkv = side([part[idx] for idx in range(3) for part in dqkv])
    qkv_sums = jnp.sum(dqkv.astype(F32), axis=0, keepdims=True)
    small = small_grads(where, sums_one, sums_two, up_sums, qkv_sums, slab)
    small = jnp.pad(small[:, None, None], ((0, 0), (0, 1), (0, 1), (0, 0), (0, 0)))
    last_state, sent = reduce_first([blocks(g_last), small], slab_part // 2, col, row)
    down_state = spread_first(after(down_state, sent), True)
    up_state, sent_up = reduce_far(after(up_state, down_state[0]), line)
    dqkv = after(dqkv, sent_up)
    dtok_low = contract_cols(dqkv[half_rows:], qkv_weight).astype(BF)
    dtok_got = swap_core(dtok_low)
    grad_tok = contract_cols(after(dqkv[:half_rows], dtok_low), qkv_weight) + dr_one
    last_state, sent = reduce_second(after(last_state, grad_tok), col, row)
    down_state = spread_second(after(down_state, sent), True)
    grad_tok = (after(grad_tok, down_state[0]) + dtok_got.astype(F32)).astype(BF)
    back_first = return_block(grad_tok[:quarter], 0)
    up_state = spread_first(after(up_state, grad_tok), False)
    attn_state, sent = reduce_near([most_state, after(last_state, up_state[0])], line)
    down_state = spread_core(after(down_state, sent))
    up_state = spread_second(after(up_state, down_state[0]), False)
    attn_state, sent = reduce_far(after(attn_state, up_state[0], back_first), line)
    back_second = return_block(after(grad_tok[quarter:], sent), 1)
    up_state = spread_core(after(up_state, sent))
    down_layout = lambda half_at: [(0, width, 0, lambda part: half_at * (wide // 2) + part * wide_part, 0)]
    (grad_down,) = finish_grad(where, after(down_state, up_state[0]), True, down_layout, wide_part, [(wide, width)])
    slab_row = lambda part: part * slab_part
    up_layout = lambda half_at: [
        (idx * (wide // 2), wide // 2, 0, slab_row, idx * wide + half_at * (wide // 2)) for idx in range(4)
    ]
    (grad_up,) = finish_grad(
        where, after(up_state, grad_down), False, up_layout, slab_part, [(slab, 2 * units)]
    )
    attn_state, sent = direct_spread(after(attn_state, grad_up))
    grad_tokens = join_rows(*after((back_first, back_second), attn_state[1]), parity)
    attn_state = spread_core(after(attn_state, grad_tokens))
    span = half - PAIR
    attn_layout = lambda half_at: (
        [(idx * span, span, 0, slab_row, idx * width + half_at * half) for idx in range(3)]
        + [(3 * span, half, 1, slab_row, half_at * half)]
        + [
            (3 * span + half + idx * PAIR, PAIR, 0, slab_row, idx * width + half_at * half + span)
            for idx in range(3)
        ]
    )
    grad_qkv, grad_out, *vec_grads = finish_grad(
        where, after(attn_state, grad_up), True, attn_layout, slab_part, [(slab, 3 * width), (slab, width)], 4 * half
    )
    vec_of = lambda idx: vec_grads[idx]
    return (
        layer_out,
        grad_tokens,
        grad_qkv,
        vec_of(0),
        vec_of(1),
        grad_out,
        vec_of(2),
        vec_of(3),
        vec_of(4),
        grad_up,
        vec_of(8),
        grad_down,
        vec_of(5),
        vec_of(6),
        vec_of(7),
    )


def solution(mesh):
    placed = (
        P("grp", "shard", None),
        P("grp", "shard", None),
        P("grp"),
        P("shard", None),
        P("shard"),
        P("shard"),
        P("shard", None),
        P("shard"),
        P("shard"),
        P("shard"),
        P("shard", None),
        P("shard"),
        P("shard", None),
        P("shard"),
        P("shard"),
        P("shard"),
    )
    plan = per_device_chip if dict(mesh.shape) == {"grp": 8, "shard": 4} else per_device
    return jax.shard_map(
        plan,
        mesh=mesh,
        in_specs=placed,
        out_specs=(
            P("grp", "shard", None),
            P("grp", "shard", None),
            P("shard", None),
            P("shard"),
            P("shard"),
            P("shard", None),
            P("shard"),
            P("shard"),
            P("shard"),
            P("shard", None),
            P("shard"),
            P("shard", None),
            P("shard"),
            P("shard"),
            P("shard"),
        ),
        check_vma=False,
    )
```
